32 devices in a mesh: seq: 8 (over z, x), rows: 4 (over y, core).
Axes of the slice: x: 2, y: 2, z: 4, core: 2. Of those that a mesh axis runs over, the one named last changes fastest.
Arguments:
- tokens: bfloat16 [12, 1024, 512], P('rows', 'seq'), may hold values from -6 to 6
- segment_ids: int32 [12, 1024], P('rows', 'seq'), may hold values from 0 to 3, never falling along the last dimension, each value on 1 to 512 neighbouring positions
- padding: int32 [12, 1024], P('rows', 'seq'), may hold values 0 or 1
- gain_one: float32 [512], replicated, may hold values from 0.5 to 1.5
- w_query: bfloat16 [512, 512], replicated, may hold values from -0.25 to 0.25
- w_key: bfloat16 [512, 512], replicated, may hold values from -0.25 to 0.25
- w_value: bfloat16 [512, 512], replicated, may hold values from -0.25 to 0.25
- blend: float32 [2, 8], replicated, may hold values from 0.5 to 2
- w_out: bfloat16 [512, 512], replicated, may hold values from -0.75 to 0.75
- gain_two: float32 [512], replicated, may hold values from 0.5 to 1.5
- w_up: bfloat16 [512, 2048], replicated, may hold values from -0.25 to 0.25
- w_down: bfloat16 [2048, 512], replicated, may hold values from -0.125 to 0.125
- cotangent: bfloat16 [12, 1024, 512], P('rows', 'seq'), may hold values from -6 to 6
Outputs:
- output: bfloat16 [12, 1024, 512], P('rows', 'seq')
- grad_tokens: bfloat16 [12, 1024, 512], P('rows', 'seq')
- grad_gain_one: float32 [512], replicated
- grad_query: float32 [512, 512], replicated
- grad_key: float32 [512, 512], replicated
- grad_value: float32 [512, 512], replicated
- grad_blend: float32 [2, 8], replicated
- grad_out: float32 [512, 512], replicated
- grad_gain_two: float32 [512], replicated
- grad_up: float32 [512, 2048], replicated
- grad_down: float32 [2048, 512], replicated
The draws below stay inside these ranges and needn't reach their ends.
Inputs may be any that keep to these rules, and one draw needn't show every extreme that they name: `segment_ids`: within a row the ids never fall; each of the 4 documents of a row holds 1 to 512 tokens and one holds exactly 512.
All inputs are finite; a program needn't handle non-finite values. No bound on the sum of `padding` on one device may be relied on, other than what follows from the above.
Results may differ from the reference program's by a relative error of at most 0.014.
Values may be sent and summed in bfloat16 or wider, within the bound.
A program may use at most 256 MiB of HBM per device.

```python
import math
import jax
import jax.numpy as jnp
import numpy as np
from jax import lax

D = 512
H = 8
E = 64
FF = 2048
BAND = 30
SEGS = 4
ROWS = 12
LENGTH = 1024


def plant(entries, stream_key, least, largest):
    dims = entries.shape
    index_at = [jax.random.randint(jax.random.fold_in(stream_key, axis), (), 0, dims[axis]) for axis in range(len(dims))]
    entries = entries.at[tuple(index_at)].set(least)
    longest = dims.index(max(dims))
    index_at[longest] = (index_at[longest] + 1) % dims[longest]
    return entries.at[tuple(index_at)].set(largest)


def shard_levels(key, extent, shards, least, high):
    def one(dim, parts):
        draws = jax.random.uniform(jax.random.fold_in(jax.random.fold_in(key, 6), dim), (parts,), jnp.float32, least / len(shards), high / len(shards))
        return jnp.repeat(jnp.exp(draws), extent[dim] // parts).reshape((-1,) + (1,) * (len(extent) - dim - 1))

    loudness = one(*shards[0])
    for cut in shards[1:]:
        loudness = loudness * one(*cut)
    return loudness


def length_profile(amount, total, most, lean):
    portions = [(1 << 20) // math.isqrt(rank ** lean) + 1 for rank in range(2, amount + 1)]
    rest, given = total - most - (amount - 1), [1] * (amount - 1)
    while rest > 0:
        movable = [i for i in range(amount - 1) if given[i] < most]
        whole, budget = sum([portions[i] for i in movable]), rest
        for i in movable:
            addition = min(most - given[i], max(1, budget * portions[i] // whole), rest)
            given[i] = given[i] + addition
            rest = rest - addition
    return np.array([most] + given)


def ragged(key, amount, total, limit, skew):
    if amount == 2:
        one = jax.random.randint(key, (), max(1, total - limit), min(limit, total - 1) + 1)
        return jnp.stack([one, total - one])
    tallies = jnp.asarray(length_profile(amount, total, limit, skew), jnp.int32)
    twos = (amount - 1) // 2
    donor, receiver = tallies[1:1 + 2 * twos:2], tallies[2:2 + 2 * twos:2]
    slack = jnp.minimum(donor - 1, limit - receiver)
    moved = jax.random.randint(jax.random.fold_in(key, 1), (twos,), 0, 1 << 20) % (slack + 1)
    tallies = tallies.at[1:1 + 2 * twos:2].set(donor - moved).at[2:2 + 2 * twos:2].set(receiver + moved)
    return tallies[jax.random.permutation(jax.random.fold_in(key, 2), amount)]


def scatter_about(rng, extent, width, reach, cuts=(), kind=jnp.bfloat16):
    factor_of = shard_levels(rng, extent, cuts, -0.22, 0.18) if cuts else 1.0
    entries = jax.random.normal(rng, extent, jnp.float32) * width * factor_of
    return jnp.minimum(jnp.maximum(entries, -reach), reach).astype(kind)


def setup_inputs(seed: int = 0) -> dict:
    splits = jax.random.split(jax.random.key(seed), 14)
    return {
        "tokens": scatter_about(splits[0], (ROWS, LENGTH, D), 1.0, 6.0, ((0, 4), (1, 8))),
        "segment_ids": jax.vmap(lambda own: jnp.searchsorted(jnp.cumsum(ragged(own, SEGS, LENGTH, LENGTH // 2, 1)), jnp.arange(LENGTH), side="right"))(jax.random.split(splits[1], ROWS)).reshape((ROWS, LENGTH)).astype(jnp.int32),
        "padding": plant((jax.random.randint(splits[2], (ROWS, LENGTH), 0, 8) < 7).astype(jnp.int32), jax.random.fold_in(splits[2], 1), 0, 1),
        "gain_one": jnp.clip(1.0 + 0.1 * jax.random.normal(splits[3], (D,), jnp.float32), 0.5, 1.5),
        "w_query": scatter_about(splits[4], (D, D), D ** -0.5, 0.25),
        "w_key": scatter_about(splits[5], (D, D), D ** -0.5, 0.25),
        "w_value": scatter_about(splits[6], (D, D), D ** -0.5, 0.25),
        "blend": jnp.clip(jax.random.uniform(splits[7], (2, H), jnp.float32, 0.5, 2.0), 0.5, 2.0),
        "w_out": scatter_about(splits[8], (D, D), (D // 8) ** -0.5, 0.75),
        "gain_two": jnp.clip(1.0 + 0.1 * jax.random.normal(splits[9], (D,), jnp.float32), 0.5, 1.5),
        "w_up": scatter_about(splits[10], (D, FF), D ** -0.5, 0.25),
        "w_down": scatter_about(splits[11], (FF, D), FF ** -0.5, 0.125),
        "cotangent": scatter_about(splits[12], (ROWS, LENGTH, D), 1.0, 6.0, ((0, 4), (1, 8))),
    }


EPSILON = 1e-06
EXACT_PRECISION = lax.Precision.HIGHEST
NEGATIVE = -1e+30

@jax.custom_vjp
def low(v):
    return lax.optimization_barrier(v.astype(jnp.bfloat16)).astype(jnp.float32)

@jax.custom_vjp
def low_back(v):
    return v

def low_keep(v):
    return (low(v), None)

def low_pass(kept, grad):
    return (grad,)

def back_keep(v):
    return (v, None)

def back_low(kept, grad):
    return (low(grad),)
low.defvjp(low_keep, low_pass)
low_back.defvjp(back_keep, back_low)

def feature_one(values_in):
    return jnp.where(values_in > 0, values_in + 1.0, jnp.exp(jnp.where(values_in > 0, 0.0, values_in)))

def feature_two(values_in):
    return 1.0 + jnp.tanh(values_in)

def norm_value(inputs, gain_vec):
    inverse = lax.rsqrt(lax.optimization_barrier(jnp.mean(inputs * inputs, -1, keepdims=True)) + EPSILON)
    return inputs * inverse * gain_vec

def near_field(queries, key_rows, value_rows, seg_row, key_info):
    length = queries.shape[0]
    block = math.gcd(512, length)
    count_blocks = length // block
    score_scale = 1.0 / math.sqrt(E)
    key_pad = jnp.concatenate([jnp.zeros((BAND, H, E), queries.dtype), key_rows], 0)
    value_pad = jnp.concatenate([jnp.zeros((BAND, H, E), queries.dtype), value_rows], 0)
    info_pad = jnp.concatenate([jnp.zeros((BAND,), jnp.int32), key_info.astype(jnp.int32)], 0)

    def one_block(index):
        start = (index * block).astype(jnp.int32)
        q_block = lax.dynamic_slice_in_dim(queries, start, block, 0)
        key_block_tile = lax.dynamic_slice_in_dim(key_pad, start, block + BAND, 0)
        value_block_tile = lax.dynamic_slice_in_dim(value_pad, start, block + BAND, 0)
        seg_block = lax.dynamic_slice_in_dim(seg_row, start, block, 0)
        info_block = lax.dynamic_slice_in_dim(info_pad, start, block + BAND, 0)
        scores = low_back(score_scale * jnp.einsum('qhe,khe->hqk', q_block, key_block_tile, precision=EXACT_PRECISION))
        query_pos = jnp.arange(block)[:, None]
        wide_pos = jnp.arange(block + BAND)[None, :]
        inside = (wide_pos >= query_pos) & (wide_pos <= query_pos + BAND)
        allowed = inside & ((info_block[None, :] == seg_block[:, None] + 1) | (wide_pos == query_pos + BAND))
        weights = jax.nn.softmax(jnp.where(allowed[None], scores, NEGATIVE), axis=-1)
        weights = low(weights)
        return jnp.einsum('hqk,khe->qhe', weights, value_block_tile, precision=EXACT_PRECISION)
    pieces = lax.map(jax.checkpoint(one_block), jnp.arange(count_blocks, dtype=jnp.int32))
    return pieces.reshape(length, H, E)

def far_field(queries, key_rows, value_rows, seg_row, pad_row, feature):
    length = queries.shape[0]
    piece = math.gcd(256, length)
    count = length // piece
    feat_q = low(feature(queries))
    feat_k = low(feature(key_rows))
    shape_four = (count, piece, H, E)
    last_keys = seg_row[piece - 1::piece].astype(jnp.int32)
    prev_keys = jnp.concatenate([jnp.full((1,), -1, jnp.int32), last_keys[:-1]], 0)

    def step(carry, row_items):
        running_state, norm_state = carry
        fq_block, fk_block, value_block_tile, seg_block, pad_block, prev_key, last_key = row_items
        query_pos = jnp.arange(piece)[:, None]
        key_pos = jnp.arange(piece)[None, :]
        allowed = (seg_block[:, None] == seg_block[None, :]) & ((key_pos < query_pos) & (pad_block[None, :] == 1) | (key_pos == query_pos))
        kernel = jnp.einsum('qhe,khe->hqk', fq_block, fk_block, precision=EXACT_PRECISION) * allowed[None].astype(fq_block.dtype)
        kernel = low_back(low(kernel))
        numer = low_back(jnp.einsum('hqk,khe->qhe', kernel, value_block_tile, precision=EXACT_PRECISION))
        denom = jnp.einsum('hqk->qh', kernel)
        use_state = (seg_block == prev_key).astype(fq_block.dtype)
        numer = numer + use_state[:, None, None] * jnp.einsum('qhe,hef->qhf', fq_block, running_state, precision=EXACT_PRECISION)
        denom = denom + use_state[:, None] * jnp.einsum('qhe,he->qh', fq_block, norm_state, precision=EXACT_PRECISION)
        tail_weight = ((seg_block == last_key) & (pad_block == 1)).astype(fq_block.dtype)
        weighted_result = fk_block * tail_weight[:, None, None]
        retained_state = (last_key == prev_key).astype(fq_block.dtype)
        running_state = retained_state * running_state + jnp.einsum('pij,pic->ijc', weighted_result, value_block_tile, precision=EXACT_PRECISION)
        norm_state = retained_state * norm_state + lax.optimization_barrier(jnp.sum(weighted_result, 0))
        return ((running_state, norm_state), numer / denom[:, :, None])
    start_carry = (jnp.zeros((H, E, E), queries.dtype), jnp.zeros((H, E), queries.dtype))
    _, pieces = lax.scan(jax.checkpoint(step), start_carry, (feat_q.reshape(shape_four), feat_k.reshape(shape_four), value_rows.reshape(shape_four), seg_row.reshape(count, piece), pad_row.reshape(count, piece), prev_keys, last_keys))
    return pieces.reshape(length, H, E)

def row_forward(weights_all, row_x, seg_row, pad_row):
    gain_one, w_query, w_key, w_value, blend, w_out, gain_two, w_up, w_down = weights_all
    length = row_x.shape[0]
    normed = low(norm_value(row_x, gain_one))
    queries = low_back(low(jnp.dot(normed, w_query, precision=EXACT_PRECISION))).reshape(length, H, E)
    key_rows = low_back(low(jnp.dot(normed, w_key, precision=EXACT_PRECISION))).reshape(length, H, E)
    value_rows = low_back(low(jnp.dot(normed, w_value, precision=EXACT_PRECISION))).reshape(length, H, E)
    key_info = jnp.where(pad_row == 1, seg_row + 1, 0)
    near_out = near_field(queries, key_rows, value_rows, seg_row, key_info)
    far_one = far_field(queries, key_rows, value_rows, seg_row, pad_row, feature_one)
    far_two = far_field(queries, key_rows, value_rows, seg_row, pad_row, feature_two)
    blended = near_out + blend[0][None, :, None] * far_one + blend[1][None, :, None] * far_two
    mixed_low = low_back(low(blended.reshape(length, D)))
    branch = low_back(jnp.dot(mixed_low, w_out, precision=EXACT_PRECISION))
    middle = row_x + branch
    normed_two = low(norm_value(middle, gain_two))
    upward_value = low_back(jnp.dot(normed_two, w_up, precision=EXACT_PRECISION))
    active = low(jax.nn.gelu(upward_value, approximate=True))
    return middle + jnp.dot(active, w_down, precision=EXACT_PRECISION)

def reference(tokens, segment_ids, padding, gain_one, w_query, w_key, w_value, blend, w_out, gain_two, w_up, w_down, cotangent):
    weights_all = tuple((item.astype(jnp.float32) for item in (gain_one, w_query, w_key, w_value, blend, w_out, gain_two, w_up, w_down)))
    zero_grads = tuple((jnp.zeros(item.shape, jnp.float32) for item in weights_all))

    def row_step(totals, row_items):
        row_x, seg_row, pad_row, row_cot = row_items

        def forward(weights_in, x_in):
            return row_forward(weights_in, x_in, seg_row, pad_row)
        result, pullback = jax.vjp(forward, weights_all, row_x.astype(jnp.float32))
        row_grads, row_dx = pullback(row_cot.astype(jnp.float32))
        totals = tuple((left + right for left, right in zip(totals, row_grads)))
        return (totals, (result.astype(jnp.bfloat16), row_dx.astype(jnp.bfloat16)))
    totals, (outputs, grad_tokens) = lax.scan(row_step, zero_grads, (tokens, segment_ids, padding, cotangent))
    grad_gain_one, grad_query, grad_key, grad_value, grad_blend, grad_out, grad_gain_two, grad_up, grad_down = totals
    return (outputs, grad_tokens, grad_gain_one, grad_query, grad_key, grad_value, grad_blend, grad_out, grad_gain_two, grad_up, grad_down)
```

```python
import functools
import math

import jax
import jax.numpy as jnp
from jax import lax
from jax.experimental import pallas as pl
from jax.experimental.pallas import tpu as pltpu
from jax.sharding import PartitionSpec as P

MESH = pl.DeviceIdType.MESH
F32 = jnp.float32
BF = jnp.bfloat16
D = 512
H = 8
E = 64
FF = 2048
BAND = 30
T = 128
PAIRS = 4
PAY = 144
HALO = 32
EPSILON = 1e-06
NEGATIVE = -1e30
SCALE = 1.0 / math.sqrt(E)
GELU_A = math.sqrt(2.0 / math.pi)
GELU_B = 0.044715
ROW_UP = FF
ROW_OUT = 2 * FF
ROW_Q = ROW_OUT + D
ROW_SMALL = ROW_Q + 3 * D
SMALL = 16
ROWS_ALL = ROW_SMALL + SMALL


def nn(a, b):
    return lax.dot_general(a, b, (((1,), (0,)), ((), ())), preferred_element_type=F32)


def nt(a, b):
    return lax.dot_general(a, b, (((1,), (1,)), ((), ())), preferred_element_type=F32)


def tn(a, b):
    return lax.dot_general(a, b, (((0,), (0,)), ((), ())), preferred_element_type=F32)


def lane_low(rows):
    return lax.broadcasted_iota(jnp.int32, (rows, T), 1) < E


def low_high():
    low = lane_low(T).astype(F32)
    return low.astype(BF), (1.0 - low).astype(BF)


def two_blocks(x):
    low, high = low_high()
    rows = x.shape[0]
    return jnp.concatenate([x * low[:rows], x * high[:rows]], 0)


def pick(stacked):
    half = stacked.shape[0] // 2
    return jnp.where(lane_low(half), stacked[:half], stacked[half:])


def block_ones():
    i = lax.broadcasted_iota(jnp.int32, (T, T), 0) < E
    j = lax.broadcasted_iota(jnp.int32, (T, T), 1) < E
    return jnp.where(i == j, 1.0, 0.0).astype(BF)


def feature_one(t):
    return jnp.where(t > 0, t + 1.0, jnp.exp(jnp.minimum(t, 0.0)))


def slope_one(t):
    return jnp.where(t > 0, 1.0, jnp.exp(jnp.minimum(t, 0.0)))


def feature_two(t):
    return 1.0 + jnp.tanh(t)


def slope_two(t):
    tangent = jnp.tanh(t)
    return 1.0 - tangent * tangent


FEATURES = ((feature_one, slope_one), (feature_two, slope_two))


def layer_kernel(
    n,
    R,
    tok,
    seg,
    pad,
    gain_one,
    gain_two,
    blend,
    w_query,
    w_key,
    w_value,
    w_out_hbm,
    w_up_hbm,
    w_down_hbm,
    cot_hbm,
    out,
    grad_tok,
    grads,
    w_out,
    w_up,
    w_down,
    cot,
    normed,
    normed_two,
    mixed,
    middle,
    total,
    back_two,
    q_s,
    k_s,
    v_s,
    hk_s,
    hv_s,
    fq_s,
    fk_s,
    kk_s,
    p_s,
    ph_s,
    near_s,
    far_s,
    den_s,
    db_s,
    low_s,
    dden_s,
    dq_s,
    dk_s,
    dv_s,
    hdk_s,
    hdv_s,
    hdk_r,
    hdv_r,
    wide_s,
    far_mask,
    near_mask,
    use_mask,
    tail_mask,
    halo_mask,
    info_own,
    info_in,
    gb_s,
    pay_s,
    m1_r,
    sum_s,
    carry_r,
    pass_s,
    in_s,
    give_s,
    w_sem,
    info_send,
    info_recv,
    halo_send,
    halo_recv,
    chain_send,
    chain_recv,
):
    U = R * PAIRS
    HU = U // 2
    sq = lax.axis_index("seq")
    rw = lax.axis_index("rows")
    par = lax.rem(sq, 2)
    z = sq // 2
    nz = n // 2
    partner = sq + 1 - 2 * par

    def unit_row(u):
        return lax.rem(u, 2 * R) // 2

    def unit_pair(u):
        return (u // (2 * R)) * 2 + lax.rem(u, 2)

    def unit_of(r, hp):
        return (hp // 2) * 2 * R + r * 2 + hp % 2

    def send(src, dst, send_sem, recv_sem, to):
        return pltpu.make_async_remote_copy(
            src_ref=src,
            dst_ref=dst,
            send_sem=send_sem,
            recv_sem=recv_sem,
            device_id=(to, rw),
            device_id_type=MESH,
        )

    barrier = pltpu.get_barrier_semaphore()
    for step in (1, 2):

        @pl.when(sq >= step)
        def _():
            pl.semaphore_signal(barrier, inc=1, device_id=(sq - step, rw), device_id_type=MESH)

        @pl.when(sq + step < n)
        def _():
            pl.semaphore_signal(barrier, inc=1, device_id=(sq + step, rw), device_id_type=MESH)

    loads = [
        pltpu.make_async_copy(src, dst, w_sem.at[i])
        for i, (src, dst) in enumerate(
            ((w_out_hbm, w_out), (w_up_hbm, w_up), (w_down_hbm, w_down), (cot_hbm, cot))
        )
    ]
    for load in loads:
        load.start()

    for r in range(R):
        rows = pl.ds(r * T, T)
        x = tok[rows, :].astype(F32)
        inverse = lax.rsqrt(jnp.mean(x * x, -1, keepdims=True) + EPSILON)
        normed[rows, :] = (x * inverse * gain_one[...]).astype(BF)
    for weight, held in ((w_key, k_s), (w_value, v_s), (w_query, q_s)):
        whole = nn(normed[...], weight[...]).astype(BF)
        for r in range(R):
            for hp in range(PAIRS):
                held[unit_of(r, hp)] = whole[r * T : (r + 1) * T, hp * T : (hp + 1) * T]

    i_pos = lax.broadcasted_iota(jnp.int32, (T, T), 0)
    j_pos = lax.broadcasted_iota(jnp.int32, (T, T), 1)
    info_own[...] = jnp.zeros_like(info_own)
    for r in range(R):
        seg_row = seg[r : r + 1, :].astype(F32)
        pad_row = pad[r : r + 1, :].astype(F32)
        seg_j = jnp.broadcast_to(seg_row, (T, T))
        pad_j = jnp.broadcast_to(pad_row, (T, T))
        seg_i = seg_j.T
        pad_i = pad_j.T
        same = seg_i == seg_j
        open_key = same & (((j_pos < i_pos) & (pad_j == 1.0)) | (i_pos == j_pos))
        far_mask[r] = open_key.astype(F32)
        near_mask[r] = (open_key & (i_pos - j_pos <= BAND)).astype(F32)
        last = seg_i[T - 1 : T, :]
        tail_mask[r] = ((seg_i == last) & (pad_i == 1.0)).astype(F32)
        use_mask[r] = seg_i
        info_own[0, r : r + 1, :] = last
        info_own[1, r : r + 1, :] = jnp.where(pad_row == 1.0, seg_row + 1.0, 0.0)

    head = pl.ds(0, T - HALO)
    hk_s[:, head, :] = jnp.zeros((U, T - HALO, T), BF)
    hv_s[:, head, :] = jnp.zeros((U, T - HALO, T), BF)

    @pl.when(sq == 0)
    def _():
        tail = pl.ds(T - HALO, HALO)
        hk_s[:, tail, :] = jnp.zeros((U, HALO, T), BF)
        hv_s[:, tail, :] = jnp.zeros((U, HALO, T), BF)

    @pl.when(sq == n - 1)
    def _():
        hdk_r[...] = jnp.zeros((U, HALO, T), BF)
        hdv_r[...] = jnp.zeros((U, HALO, T), BF)

    pl.semaphore_wait(barrier, jnp.minimum(sq, 2) + jnp.minimum(n - 1 - sq, 2))

    def info_copy(slot, to):
        return send(info_own, info_in.at[slot], info_send.at[slot], info_recv.at[slot], to)

    def halo_copy(which, to):
        src, dst = ((k_s, hk_s), (v_s, hv_s))[which]
        tail = pl.ds(T - HALO, HALO)
        return send(
            src.at[:, tail, :], dst.at[:, tail, :], halo_send.at[which], halo_recv.at[which], to
        )

    for slot, step in enumerate((1, 2, -1)):
        inside = (sq + step >= 0) & (sq + step < n)
        came = (sq - step >= 0) & (sq - step < n)

        @pl.when(inside)
        def _():
            info_copy(slot, sq + step).start()

        @pl.when(jnp.logical_not(came))
        def _():
            info_in[slot, 0] = jnp.full((8, T), -1.0, F32)
            info_in[slot, 1] = jnp.zeros((8, T), F32)

    @pl.when(sq + 1 < n)
    def _():
        for which in range(2):
            halo_copy(which, sq + 1).start()

    ones_block = block_ones()

    def local_state(u, _):
        r = unit_row(u)
        tail = tail_mask[r].astype(BF)
        keys = k_s[u].astype(F32)
        values = v_s[u]
        norms = []
        for a, (feature, _slope) in enumerate(FEATURES):
            fk = feature(keys).astype(BF)
            fk_s[a, u] = fk
            weighted = fk * tail
            pay_s[0, u, a * E : (a + 1) * E, :] = pick(tn(weighted, values)).astype(BF)
            norm = jnp.sum(weighted.astype(F32), 0, keepdims=True)
            norms.append(jnp.broadcast_to(norm, (8, T)))
        pay_s[0, u, 2 * E : PAY, :] = jnp.concatenate(norms, 0).astype(BF)
        return 0

    lax.fori_loop(0, U, local_state, 0)

    def half(which, r):
        return pl.ds(which * HU + 2 * r, 2)

    def chain_copy(way, stage, r):
        step = 1 - 2 * way
        here = pl.ds(2 * r, 2)
        src, dst, to = (
            (pay_s.at[way, half(1 - par, r)], m1_r.at[way, here], partner),
            (pass_s.at[way, here], carry_r.at[way, here], sq + 2 * step),
            (give_s.at[way, here], in_s.at[way, half(par, r)], partner),
        )[stage]
        return send(src, dst, chain_send.at[way, stage, r], chain_recv.at[way, stage, r], to)

    def chain_arrival(way, stage, r):
        here = pl.ds(2 * r, 2)
        dst = (m1_r.at[way, here], carry_r.at[way, here], in_s.at[way, half(1 - par, r)])[stage]
        return send(dst, dst, chain_send.at[way, stage, r], chain_recv.at[way, stage, r], partner)

    def has_next(way):
        return (z + 1 < nz) if way == 0 else (z > 0)

    def has_before(way):
        return (z > 0) if way == 0 else (z + 1 < nz)

    def marks(r):
        own = info_own[0, r : r + 1, :]
        before, before_two, after = (info_in[s, 0, r : r + 1, :] for s in range(3))
        first = par == 0
        last_a = jnp.where(first, own, before)
        last_b = jnp.where(first, after, own)
        last_z = jnp.where(first, before, before_two)
        inner = (last_a == last_b).astype(F32)
        enter = (last_z == last_a).astype(F32)
        through = (last_z == last_b).astype(F32)
        return inner, enter, through

    def chain_begin(way):
        for r in range(R):
            chain_copy(way, 0, r).start()

        @pl.when(jnp.logical_not(has_before(way)))
        def _():
            carry_r[way] = jnp.zeros((HU, PAY, T), BF)

    def chain_pair(way):
        second = par == (1 - way)
        for r in range(R):
            chain_arrival(way, 0, r).wait_recv()
            inner, enter, _through = marks(r)
            weight = inner if way == 0 else enter
            one = jnp.ones_like(weight)
            mine = jnp.where(second, one, weight)
            other = jnp.where(second, weight, one)
            for j in range(2):
                own = pay_s[way, par * HU + 2 * r + j].astype(F32)
                got = m1_r[way, 2 * r + j].astype(F32)
                sum_s[2 * r + j] = mine * own + other * got

    def chain_pass(way):
        second = par == (1 - way)
        for r in range(R):

            @pl.when(has_before(way))
            def _():
                chain_arrival(way, 1, r).wait_recv()

            inner, enter, through = marks(r)
            weight = enter if way == 0 else inner
            for j in range(2):
                carry = carry_r[way, 2 * r + j].astype(F32)
                pass_s[way, 2 * r + j] = (sum_s[2 * r + j] + through * carry).astype(BF)

            @pl.when(has_next(way))
            def _():
                chain_copy(way, 1, r).start()

            for j in range(2):
                carry = carry_r[way, 2 * r + j].astype(F32)
                own = pay_s[way, par * HU + 2 * r + j].astype(F32)
                got = m1_r[way, 2 * r + j].astype(F32)
                later = jnp.where(second, got, own) + weight * carry
                in_s[way, par * HU + 2 * r + j] = jnp.where(second, later, carry).astype(BF)
                give_s[way, 2 * r + j] = jnp.where(second, carry, later).astype(BF)
            chain_copy(way, 2, r).start()

    def chain_finish(way):
        for r in range(R):
            chain_arrival(way, 2, r).wait_recv()

    def chain_drain(way):
        for r in range(R):
            chain_copy(way, 0, r).wait_send()

            @pl.when(has_next(way))
            def _():
                chain_copy(way, 1, r).wait_send()

            chain_copy(way, 2, r).wait_send()

    chain_begin(0)

    ones_pair = two_blocks(jnp.ones((T, T), BF))

    def far_local(u, _):
        r = unit_row(u)
        queries = q_s[u].astype(F32)
        values = two_blocks(v_s[u])
        mask = far_mask[r]
        mask = jnp.concatenate([mask, mask], 1)
        for a, (feature, _slope) in enumerate(FEATURES):
            fq = feature(queries).astype(BF)
            fq_s[a, u] = fq
            kernel = (nt(fq, two_blocks(fk_s[a, u])) * mask).astype(BF)
            kk_s[a, u] = kernel
            far_s[a, u] = nn(kernel, values)
            den_s[a, u] = nn(kernel, ones_pair)
        return 0

    lax.fori_loop(0, U, far_local, 0)

    for slot, step in enumerate((1, 2, -1)):
        came = (sq - step >= 0) & (sq - step < n)

        @pl.when(came)
        def _():
            info_copy(slot, sq).wait_recv()

    @pl.when(sq > 0)
    def _():
        for which in range(2):
            halo_copy(which, sq).wait_recv()

    i_low = lax.broadcasted_iota(jnp.int32, (HALO, T), 0)
    j_low = lax.broadcasted_iota(jnp.int32, (HALO, T), 1)
    for r in range(R):
        seg_i = use_mask[r]
        marks_before = info_in[0, 1, r : r + 1, :]
        reach = j_low >= T - BAND + i_low
        halo_mask[r] = (reach & (seg_i[:HALO] + 1.0 == marks_before)).astype(F32)
        use_mask[r] = (seg_i == info_in[0, 0, r : r + 1, :]).astype(F32)

    chain_pair(0)

    def near_local(u, _):
        r = unit_row(u)
        queries = q_s[u]
        scores = nt(queries, two_blocks(k_s[u])) * SCALE
        scores_halo = nt(queries[:HALO], two_blocks(hk_s[u])) * SCALE
        open_near = near_mask[r] > 0
        open_halo = halo_mask[r] > 0
        for side in range(2):
            lanes = slice(side * T, (side + 1) * T)
            s = jnp.where(open_near, scores[:, lanes], NEGATIVE)
            sh = jnp.where(open_halo, scores_halo[:, lanes], NEGATIVE)
            peak = jnp.max(s, -1, keepdims=True)
            peak_halo = jnp.maximum(peak[:HALO], jnp.max(sh, -1, keepdims=True))
            peak = jnp.concatenate([peak_halo, peak[HALO:]], 0)
            e = jnp.exp(s - peak)
            eh = jnp.exp(sh - peak_halo)
            norm = jnp.sum(e, -1, keepdims=True)
            norm_halo = norm[:HALO] + jnp.sum(eh, -1, keepdims=True)
            inverse = 1.0 / jnp.concatenate([norm_halo, norm[HALO:]], 0)
            p_s[u, :, lanes] = e * inverse
            ph_s[u, :, lanes] = eh * inverse[:HALO]
        near_s[u] = nn(p_s[u].astype(BF), two_blocks(v_s[u]))
        near_s[u, :HALO, :] += nn(ph_s[u].astype(BF), two_blocks(hv_s[u]))
        return 0

    cut = z * U // nz
    lax.fori_loop(0, cut, near_local, 0)
    chain_pass(0)
    lax.fori_loop(cut, U, near_local, 0)
    chain_finish(0)

    def blend_lanes(a, u):
        hp = unit_pair(u)
        low = lane_low(1)
        return jnp.where(low, blend[a, 2 * hp], blend[a, 2 * hp + 1])

    def far_finish(u, _):
        r = unit_row(u)
        hp = unit_pair(u)
        use = use_mask[r]
        blended = near_s[u]
        for a in range(2):
            fq = fq_s[a, u]
            state = two_blocks(in_s[0, u, a * E : (a + 1) * E, :])
            norm = in_s[0, u, 2 * E + 8 * a : 2 * E + 8 * a + 1, :].astype(F32)
            numer = far_s[a, u] + use * nn(fq, state)
            weighted = (fq.astype(F32) * norm).astype(BF)
            denom = den_s[a, u] + use * nn(weighted, ones_block)
            far = numer / denom
            far_s[a, u] = far
            den_s[a, u] = denom
            blended = blended + blend_lanes(a, u) * far
        rows = pl.ds(pl.multiple_of(r * T, T), T)
        lanes = pl.ds(pl.multiple_of(hp * T, T), T)
        mixed[rows, lanes] = blended.astype(BF)
        return 0

    lax.fori_loop(0, U, far_finish, 0)

    loads[0].wait()
    middle[...] = tok[...].astype(F32) + nn(mixed[...], w_out[...])
    for r in range(R):
        rows = pl.ds(r * T, T)
        mid = middle[rows, :]
        inverse = lax.rsqrt(jnp.mean(mid * mid, -1, keepdims=True) + EPSILON)
        normed_two[rows, :] = (mid * inverse * gain_two[...]).astype(BF)
    total[...] = jnp.zeros_like(total)
    back_two[...] = jnp.zeros_like(back_two)
    loads[1].wait()
    loads[2].wait()
    loads[3].wait()

    def feed(t, _):
        cols = pl.ds(pl.multiple_of(t * D, D), D)
        up = nn(normed_two[...], w_up[:, cols])
        square = up * up
        tangent = jnp.tanh(GELU_A * (up + GELU_B * square * up))
        act = (0.5 * up * (1.0 + tangent)).astype(BF)
        slope = 0.5 * (1.0 + tangent) + 0.5 * up * (1.0 - tangent * tangent) * GELU_A * (
            1.0 + 3.0 * GELU_B * square
        )
        total[...] += nn(act, w_down[cols, :])
        g = cot[...]
        grads[cols, :] = tn(act, g).astype(BF)
        d_up = (nt(g, w_down[cols, :]) * slope).astype(BF)
        grads[pl.ds(pl.multiple_of(ROW_UP + t * D, D), D), :] = tn(normed_two[...], d_up).astype(BF)
        back_two[...] += nt(d_up, w_up[:, cols])
        return 0

    lax.fori_loop(0, FF // D, feed, 0)
    out[...] = (middle[...] + total[...]).astype(BF)

    gain_grad_two = jnp.zeros((1, D), F32)
    for r in range(R):
        rows = pl.ds(r * T, T)
        mid = middle[rows, :]
        inverse = lax.rsqrt(jnp.mean(mid * mid, -1, keepdims=True) + EPSILON)
        d_n = back_two[rows, :]
        gain_grad_two += jnp.sum(d_n * mid * inverse, 0, keepdims=True)
        scaled = d_n * gain_two[...]
        d_mid = (
            cot[rows, :].astype(F32)
            + inverse * scaled
            - mid * (inverse * inverse * inverse) * jnp.mean(mid * scaled, -1, keepdims=True)
        )
        total[rows, :] = d_mid
        normed_two[rows, :] = d_mid.astype(BF)
    d_branch = normed_two[...]
    grads[ROW_OUT : ROW_OUT + D, :] = tn(mixed[...], d_branch).astype(BF)
    d_blended = nt(d_branch, w_out[...]).astype(BF)
    for r in range(R):
        for hp in range(PAIRS):
            db_s[unit_of(r, hp)] = d_blended[r * T : (r + 1) * T, hp * T : (hp + 1) * T]

    gb_s[...] = jnp.zeros_like(gb_s)

    def far_prepare(u, _):
        r = unit_row(u)
        hp = unit_pair(u)
        use = use_mask[r]
        use_low = use.astype(BF)
        d_out = db_s[u].astype(F32)
        norms = []
        for a in range(2):
            far = far_s[a, u]
            inverse = 1.0 / den_s[a, u]
            product = d_out * far
            row = a * PAIRS + hp
            gb_s[pl.ds(row, 1), :] += jnp.sum(product, 0, keepdims=True)
            weight = blend_lanes(a, u)
            product = product * weight
            high = product.astype(BF)
            rest = (product - high.astype(F32)).astype(BF)
            dden = -(nn(high, ones_block) + nn(rest, ones_block)) * inverse
            dden_s[a, u] = dden
            dnum = (weight * d_out * inverse).astype(BF)
            low_s[a, u] = dnum
            used = fq_s[a, u] * use_low
            pay_s[1, u, a * E : (a + 1) * E, :] = pick(tn(used, dnum)).astype(BF)
            norm = jnp.sum(used.astype(F32) * dden, 0, keepdims=True)
            norms.append(jnp.broadcast_to(norm, (8, T)))
        pay_s[1, u, 2 * E : PAY, :] = jnp.concatenate(norms, 0).astype(BF)
        return 0

    lax.fori_loop(0, U, far_prepare, 0)
    chain_begin(1)

    def near_back(u, _):
        keys = two_blocks(k_s[u])
        halo_keys = two_blocks(hk_s[u])
        queries = q_s[u]
        d_out = db_s[u]
        dp = nt(d_out, two_blocks(v_s[u]))
        dp_halo = nt(d_out[:HALO], two_blocks(hv_s[u]))
        p = p_s[u]
        p_halo = ph_s[u]
        ds = []
        ds_halo = []
        for side in range(2):
            lanes = slice(side * T, (side + 1) * T)
            ps, phs = p[:, lanes], p_halo[:, lanes]
            delta = jnp.sum(ps * dp[:, lanes], -1, keepdims=True)
            delta_halo = delta[:HALO] + jnp.sum(phs * dp_halo[:, lanes], -1, keepdims=True)
            delta = jnp.concatenate([delta_halo, delta[HALO:]], 0)
            ds.append(ps * (dp[:, lanes] - delta))
            ds_halo.append(phs * (dp_halo[:, lanes] - delta_halo))
        ds = jnp.concatenate(ds, 1).astype(BF)
        ds_halo = jnp.concatenate(ds_halo, 1).astype(BF)
        dq_s[u] = nn(ds, keys) * SCALE
        dq_s[u, :HALO, :] += nn(ds_halo, halo_keys) * SCALE
        dk_s[u] = pick(tn(ds, queries)) * SCALE
        dv_s[u] = pick(tn(p.astype(BF), d_out))
        hdk_s[u] = (pick(tn(ds_halo, queries[:HALO])) * SCALE)[T - HALO :].astype(BF)
        hdv_s[u] = pick(tn(p_halo.astype(BF), d_out[:HALO]))[T - HALO :].astype(BF)
        return 0

    lax.fori_loop(0, U, near_back, 0)

    def halo_back(which, to):
        src, dst = ((hdk_s, hdk_r), (hdv_s, hdv_r))[which]
        return send(src, dst, halo_send.at[2 + which], halo_recv.at[2 + which], to)

    @pl.when(sq > 0)
    def _():
        for which in range(2):
            halo_back(which, sq - 1).start()

    chain_pair(1)

    def far_back(u, _):
        r = unit_row(u)
        values = two_blocks(v_s[u])
        mask = far_mask[r]
        mask = jnp.concatenate([mask, mask], 1)
        use = use_mask[r]
        queries = q_s[u].astype(F32)
        keys = k_s[u].astype(F32)
        dq = dq_s[u]
        dk = dk_s[u]
        dv = dv_s[u]
        for a, (_feature, slope) in enumerate(FEATURES):
            dnum = low_s[a, u]
            dden = dden_s[a, u]
            fq = fq_s[a, u]
            fk = two_blocks(fk_s[a, u])
            added = jnp.concatenate(
                [
                    jnp.broadcast_to(dden[:, 0:1], (T, T)),
                    jnp.broadcast_to(dden[:, E : E + 1], (T, T)),
                ],
                1,
            )
            d_kernel = ((nt(dnum, values) + added) * mask).astype(BF)
            dv += pick(tn(kk_s[a, u], dnum))
            state = two_blocks(in_s[0, u, a * E : (a + 1) * E, :])
            norm = in_s[0, u, 2 * E + 8 * a : 2 * E + 8 * a + 1, :].astype(F32)
            dfq = nn(d_kernel, fk) + use * (nt(dnum, state) + dden * norm)
            dq += dfq * slope(queries)
            dk += pick(tn(d_kernel, fq)) * slope(keys)
        dq_s[u] = dq
        dk_s[u] = dk
        dv_s[u] = dv
        return 0

    cut_back = (nz - 1 - z) * U // nz
    lax.fori_loop(0, cut_back, far_back, 0)
    chain_pass(1)
    lax.fori_loop(cut_back, U, far_back, 0)

    @pl.when(sq + 1 < n)
    def _():
        for which in range(2):
            halo_back(which, sq).wait_recv()

    chain_finish(1)

    def far_close(u, _):
        r = unit_row(u)
        hp = unit_pair(u)
        tail = tail_mask[r]
        keys = k_s[u].astype(F32)
        values = v_s[u]
        dk = dk_s[u]
        dv = dv_s[u]
        for a, (_feature, slope) in enumerate(FEATURES):
            state = two_blocks(in_s[1, u, a * E : (a + 1) * E, :])
            norm = in_s[1, u, 2 * E + 8 * a : 2 * E + 8 * a + 1, :].astype(F32)
            dk += tail * (nt(values, state) + norm) * slope(keys)
            dv += tail * nn(fk_s[a, u], state)
        zero = jnp.zeros((T - HALO, T), F32)
        dk += jnp.concatenate([zero, hdk_r[u].astype(F32)], 0)
        dv += jnp.concatenate([zero, hdv_r[u].astype(F32)], 0)
        rows = pl.ds(pl.multiple_of(r * T, T), T)
        lanes = pl.ds(pl.multiple_of(hp * T, T), T)
        wide_s[0, rows, lanes] = dq_s[u].astype(BF)
        wide_s[1, rows, lanes] = dk.astype(BF)
        wide_s[2, rows, lanes] = dv.astype(BF)
        return 0

    lax.fori_loop(0, U, far_close, 0)

    for i, weight in enumerate((w_query, w_key, w_value)):
        grads[ROW_Q + i * D : ROW_Q + (i + 1) * D, :] = tn(normed[...], wide_s[i]).astype(BF)
        back = nt(wide_s[i], weight[...])
        if i == 0:
            back_two[...] = back
        else:
            back_two[...] += back
    gain_grad_one = jnp.zeros((1, D), F32)
    for r in range(R):
        rows = pl.ds(r * T, T)
        x = tok[rows, :].astype(F32)
        inverse = lax.rsqrt(jnp.mean(x * x, -1, keepdims=True) + EPSILON)
        d_n = back_two[rows, :]
        gain_grad_one += jnp.sum(d_n * x * inverse, 0, keepdims=True)
        scaled = d_n * gain_one[...]
        d_x = (
            total[rows, :]
            + inverse * scaled
            - x * (inverse * inverse * inverse) * jnp.mean(x * scaled, -1, keepdims=True)
        )
        grad_tok[rows, :] = d_x.astype(BF)
    blends = [
        jnp.concatenate([gb_s[a * PAIRS + hp : a * PAIRS + hp + 1, :] for hp in range(PAIRS)], 1)
        for a in range(2)
    ]
    small = jnp.concatenate(
        [gain_grad_one, gain_grad_two] + blends + [jnp.zeros((SMALL - 4, D), F32)], 0
    )
    grads[ROW_SMALL:ROWS_ALL, :] = small.astype(BF)

    for slot, step in enumerate((1, 2, -1)):

        @pl.when((sq + step >= 0) & (sq + step < n))
        def _():
            info_copy(slot, sq + step).wait_send()

    @pl.when(sq + 1 < n)
    def _():
        for which in range(2):
            halo_copy(which, sq + 1).wait_send()

    @pl.when(sq > 0)
    def _():
        for which in range(2):
            halo_back(which, sq - 1).wait_send()

    chain_drain(0)
    chain_drain(1)


def solution(mesh):
    n = mesh.shape["seq"]

    def shards(
        tokens,
        segment_ids,
        padding,
        gain_one,
        w_query,
        w_key,
        w_value,
        blend,
        w_out,
        gain_two,
        w_up,
        w_down,
        cotangent,
    ):
        R, tok_count, _ = tokens.shape
        M = R * tok_count
        U = R * PAIRS
        HU = U // 2
        vmem = pl.BlockSpec(memory_space=pltpu.VMEM)
        anyspace = pl.BlockSpec(memory_space=pl.ANY)
        smem = pl.BlockSpec(memory_space=pltpu.SMEM)
        V = pltpu.VMEM
        unit_f = V((U, T, T), F32)
        unit_b = V((U, T, T), BF)
        two_f = V((2, U, T, T), F32)
        two_b = V((2, U, T, T), BF)
        wide_f = V((M, D), F32)
        wide_b = V((M, D), BF)
        halo_b = V((U, HALO, T), BF)
        dma = pltpu.SemaphoreType.DMA
        scratch = [
            V((D, D), BF),
            V((D, FF), BF),
            V((FF, D), BF),
            wide_b,
            wide_b,
            wide_b,
            wide_b,
            wide_f,
            wide_f,
            wide_f,
            unit_b,
            unit_b,
            unit_b,
            unit_b,
            unit_b,
            two_b,
            two_b,
            V((2, U, T, 2 * T), BF),
            V((U, T, 2 * T), F32),
            V((U, HALO, 2 * T), F32),
            unit_f,
            two_f,
            two_f,
            unit_b,
            two_b,
            two_f,
            unit_f,
            unit_f,
            unit_f,
            halo_b,
            halo_b,
            halo_b,
            halo_b,
            V((3, M, D), BF),
            V((R, T, T), F32),
            V((R, T, T), F32),
            V((R, T, T), F32),
            V((R, T, T), F32),
            V((R, HALO, T), F32),
            V((2, 8, T), F32),
            V((3, 2, 8, T), F32),
            V((2 * PAIRS, T), F32),
            V((2, U, PAY, T), BF),
            V((2, HU, PAY, T), BF),
            V((HU, PAY, T), F32),
            V((2, HU, PAY, T), BF),
            V((2, HU, PAY, T), BF),
            V((2, U, PAY, T), BF),
            V((2, HU, PAY, T), BF),
            dma((4,)),
            dma((3,)),
            dma((3,)),
            dma((4,)),
            dma((4,)),
            dma((2, 3, R)),
            dma((2, 3, R)),
        ]
        out, grad_tok, grads = pl.pallas_call(
            functools.partial(layer_kernel, n, R),
            out_shape=(
                jax.ShapeDtypeStruct((M, D), BF),
                jax.ShapeDtypeStruct((M, D), BF),
                jax.ShapeDtypeStruct((ROWS_ALL, D), BF),
            ),
            in_specs=[vmem] * 5 + [smem] + [vmem] * 3 + [anyspace] * 4,
            out_specs=(vmem, vmem, vmem),
            scratch_shapes=scratch,
            compiler_params=pltpu.CompilerParams(
                collective_id=0, has_side_effects=True, vmem_limit_bytes=60 * 1024 * 1024
            ),
            name="layer",
        )(
            tokens.reshape(M, D),
            segment_ids,
            padding,
            gain_one.reshape(1, D),
            gain_two.reshape(1, D),
            blend,
            w_query,
            w_key,
            w_value,
            w_out,
            w_up,
            w_down,
            cotangent.reshape(M, D),
        )
        grads = lax.psum(grads, ("seq", "rows")).astype(F32)
        small = grads[ROW_SMALL:]
        grad_up = jnp.concatenate(
            [grads[ROW_UP + t * D : ROW_UP + (t + 1) * D] for t in range(FF // D)], 1
        )
        return (
            out.reshape(R, tok_count, D),
            grad_tok.reshape(R, tok_count, D),
            small[0],
            grads[ROW_Q : ROW_Q + D],
            grads[ROW_Q + D : ROW_Q + 2 * D],
            grads[ROW_Q + 2 * D : ROW_Q + 3 * D],
            small[2:4].reshape(2, H, E).sum(-1),
            grads[ROW_OUT : ROW_OUT + D],
            small[1],
            grad_up,
            grads[:FF],
        )

    row, whole = P("rows", "seq", None), P()
    return jax.shard_map(
        shards,
        mesh=mesh,
        in_specs=(row, P("rows", "seq"), P("rows", "seq")) + (whole,) * 9 + (row,),
        out_specs=(row, row) + (whole,) * 9,
        check_vma=False,
    )
```

```python
import functools
import math

import jax
import jax.numpy as jnp
from jax import lax
from jax.experimental import pallas as pl
from jax.experimental.pallas import tpu as pltpu
from jax.sharding import PartitionSpec as P

MESH = pl.DeviceIdType.MESH
F32 = jnp.float32
BF = jnp.bfloat16
D = 512
H = 8
E = 64
FF = 2048
BAND = 30
T = 128
PAIRS = 4
PAY = 144
HALO = 32
EPSILON = 1e-06
NEGATIVE = -1e30
SCALE = 1.0 / math.sqrt(E)
GELU_A = math.sqrt(2.0 / math.pi)
GELU_B = 0.044715
TILES = FF // D
ROW_OUT = 2 * FF
ROW_Q = ROW_OUT + D
ROWS_ALL = ROW_Q + 3 * D
SMALL = 8
LANES = D // 2
CHUNKS = ((0, FF), (FF, FF), (ROW_OUT, 2 * D), (ROW_Q + D, 2 * D))
PARTS = 4
LAYER_VMEM = 60 * 1024 * 1024
WIDEN_VMEM = 60 * 1024 * 1024


def both(*steps):
    return tuple((chunk, color, k) for chunk, k in steps for color in range(2))


ORDER = {
    "down": both((0, 0)),
    "up": both((0, 1), (1, 0)),
    "branch": both((1, 1)),
    "prepare": both(),
    "near_a": both(),
    "near_b": both((0, 2)),
    "pair": both((1, 2)),
    "far_0": both(),
    "far_1": both((0, 3)),
    "far_2": both((1, 3)),
    "far_3": both(),
    "query": both((2, 0)),
    "state": both((2, 1), (0, 4)),
    "close": both((1, 4)),
    "key": both((3, 0)),
    "back": both((0, 5), (2, 2), (3, 1)),
    "tail": both((1, 5), (3, 2), (0, 6), (2, 3), (3, 3), (1, 6), (2, 4), (3, 4), (0, 7), (2, 5), (3, 5), (1, 7), (0, 8), (2, 6), (3, 6), (1, 8), (2, 7), (3, 7), (2, 8), (3, 8)),
}


def row_down(t):
    return (t // 2) * FF + (t % 2) * D


def row_up(t):
    return row_down(t) + FF // 2


def nn(a, b):
    return lax.dot_general(a, b, (((1,), (0,)), ((), ())), preferred_element_type=F32)


def nt(a, b):
    return lax.dot_general(a, b, (((1,), (1,)), ((), ())), preferred_element_type=F32)


def tn(a, b):
    return lax.dot_general(a, b, (((0,), (0,)), ((), ())), preferred_element_type=F32)


def lane_low(rows):
    return lax.broadcasted_iota(jnp.int32, (rows, T), 1) < E


def low_high():
    low = lane_low(T).astype(F32)
    return low.astype(BF), (1.0 - low).astype(BF)


def two_blocks(x):
    low, high = low_high()
    rows = x.shape[0]
    return jnp.concatenate([x * low[:rows], x * high[:rows]], 0)


def pick(stacked):
    half = stacked.shape[0] // 2
    return jnp.where(lane_low(half), stacked[:half], stacked[half:])


def block_ones():
    i = lax.broadcasted_iota(jnp.int32, (T, T), 0) < E
    j = lax.broadcasted_iota(jnp.int32, (T, T), 1) < E
    return jnp.where(i == j, 1.0, 0.0).astype(BF)


def feature_one(t):
    return jnp.where(t > 0, t + 1.0, jnp.exp(jnp.minimum(t, 0.0)))


def slope_one(t):
    return jnp.where(t > 0, 1.0, jnp.exp(jnp.minimum(t, 0.0)))


def feature_two(t):
    return 1.0 + jnp.tanh(t)


def slope_two(t):
    tangent = jnp.tanh(t)
    return 1.0 - tangent * tangent


FEATURES = ((feature_one, slope_one), (feature_two, slope_two))


def bits(size):
    return size.bit_length() - 1


def sum_order(color, n_rows, n_seq):
    rows = [("rows", 2**b, 2) for b in range(bits(n_rows))]
    seq = [("seq", 2**b, 2) for b in range(bits(n_seq))]
    last = []
    if len(seq) > 2:
        last = [("seq", seq[-2][1], 4)]
        seq = seq[:-2]
    if color == 0:
        return rows + seq + last
    return rows[:1] + seq + rows[1:] + last


def sum_plan(color, n_rows, n_seq, rows, offset):
    plan = []
    for axis, low, group in sum_order(color, n_rows, n_seq):
        steps = [(low, group)]
        if group == 4 and rows % 64:
            steps = [(low, 2), (2 * low, 2)]
        for low, group in steps:
            split = rows % (16 * group) == 0
            part = rows // group if split else rows
            plan.append((axis, low, group, split, rows, part, offset))
            offset += (group - 1) * part
            rows = part
    return plan, offset


def sum_plans(n_rows, n_seq):
    plans = []
    offset = [0, 0]
    for _base, rows in CHUNKS:
        both = []
        for color in range(2):
            plan, offset[color] = sum_plan(color, n_rows, n_seq, rows, offset[color])
            both.append(plan)
        plans.append(both)
    return plans, max(offset)


def layer_kernel(
    n,
    n_rows,
    R,
    tok_hbm,
    seg_hbm,
    pad_hbm,
    gain_one_hbm,
    gain_two_hbm,
    blend_hbm,
    w_query_hbm,
    w_key_hbm,
    w_value_hbm,
    w_out_hbm,
    w_up_hbm,
    w_down_hbm,
    cot_hbm,
    out,
    grad_tok,
    small_out,
    full_hbm,
    grads,
    full,
    landed,
    small_s,
    small_r,
    tok,
    seg,
    pad,
    gain_one,
    gain_two,
    blend,
    w_query,
    w_key,
    w_value,
    w_out,
    w_up,
    w_down,
    cot,
    weight_s,
    normed,
    normed_two,
    mixed,
    middle,
    total,
    back_two,
    q_s,
    k_s,
    v_s,
    hk_s,
    hv_s,
    fq_s,
    fk_s,
    kk_s,
    p_s,
    ph_s,
    near_s,
    far_s,
    den_s,
    db_s,
    low_s,
    dden_s,
    dk_s,
    dv_s,
    hdk_s,
    hdv_s,
    hdk_r,
    hdv_r,
    wide_s,
    far_mask,
    near_mask,
    use_mask,
    tail_mask,
    halo_mask,
    info_own,
    info_in,
    gb_s,
    pay_s,
    m1_r,
    sum_s,
    carry_r,
    pass_s,
    in_s,
    give_s,
    w_sem,
    info_send,
    info_recv,
    halo_send,
    halo_recv,
    chain_send,
    chain_recv,
    sum_send,
    sum_recv,
    small_send,
    small_recv,
    full_sem,
):
    U = R * PAIRS
    HU = U // 2
    sq = lax.axis_index("seq")
    rw = lax.axis_index("rows")
    par = lax.rem(sq, 2)
    z = sq // 2
    nz = n // 2
    partner = sq + 1 - 2 * par

    def unit_row(u):
        return lax.rem(u, 2 * R) // 2

    def unit_pair(u):
        return (u // (2 * R)) * 2 + lax.rem(u, 2)

    def unit_of(r, hp):
        return (hp // 2) * 2 * R + r * 2 + hp % 2

    def send(src, dst, send_sem, recv_sem, to):
        return pltpu.make_async_remote_copy(
            src_ref=src,
            dst_ref=dst,
            send_sem=send_sem,
            recv_sem=recv_sem,
            device_id=(to, rw),
            device_id_type=MESH,
        )

    barrier = pltpu.get_barrier_semaphore()
    for step in (1, 2):

        @pl.when(sq >= step)
        def _():
            pl.semaphore_signal(barrier, inc=1, device_id=(sq - step, rw), device_id_type=MESH)

        @pl.when(sq + step < n)
        def _():
            pl.semaphore_signal(barrier, inc=1, device_id=(sq + step, rw), device_id_type=MESH)

    plans, _size = sum_plans(n_rows, n)
    partners = [("rows", 2**b) for b in range(bits(n_rows))]
    partners += [("seq", 2**b) for b in range(bits(n))]

    def peer_of(axis, low, group, step):
        own = rw if axis == "rows" else sq
        mine = lax.rem(own // low, group)
        other = own + (lax.rem(mine + step, group) - mine) * low
        return mine, ((sq, other) if axis == "rows" else (other, rw))

    groups = {(axis, low, 2) for axis, low in partners}
    for both in plans:
        for plan in both:
            groups |= {(axis, low, group) for axis, low, group, *_ in plan}
    greet = [(axis, low, group, d) for axis, low, group in sorted(groups) for d in range(1, group)]
    for axis, low, group, d in greet:
        pl.semaphore_signal(
            barrier, inc=1, device_id=peer_of(axis, low, group, d)[1], device_id_type=MESH
        )

    loads = [
        pltpu.make_async_copy(src, dst, w_sem.at[i])
        for i, (src, dst) in enumerate(
            (
                (tok_hbm, tok),
                (gain_one_hbm, gain_one),
                (w_key_hbm, w_key),
                (w_value_hbm, w_value),
                (seg_hbm, seg),
                (pad_hbm, pad),
                (w_query_hbm, w_query),
                (blend_hbm, blend),
                (gain_two_hbm, gain_two),
                (w_out_hbm, w_out),
                (w_up_hbm, w_up),
                (w_down_hbm, w_down),
                (cot_hbm, cot),
            )
        )
    ]
    for load in loads:
        load.start()
    loads[0].wait()
    loads[1].wait()

    for r in range(R):
        rows = pl.ds(r * T, T)
        x = tok[rows, :].astype(F32)
        inverse = lax.rsqrt(jnp.mean(x * x, -1, keepdims=True) + EPSILON)
        normed[rows, :] = (x * inverse * gain_one[...]).astype(BF)

    def project(load, weight, held):
        loads[load].wait()
        whole = nn(normed[...], weight[...]).astype(BF)
        for r in range(R):
            for hp in range(PAIRS):
                held[unit_of(r, hp)] = whole[r * T : (r + 1) * T, hp * T : (hp + 1) * T]

    project(2, w_key, k_s)
    project(3, w_value, v_s)
    loads[4].wait()
    loads[5].wait()

    i_pos = lax.broadcasted_iota(jnp.int32, (T, T), 0)
    j_pos = lax.broadcasted_iota(jnp.int32, (T, T), 1)
    info_own[...] = jnp.zeros_like(info_own)
    for r in range(R):
        seg_row = seg[r : r + 1, :].astype(F32)
        pad_row = pad[r : r + 1, :].astype(F32)
        seg_j = jnp.broadcast_to(seg_row, (T, T))
        pad_j = jnp.broadcast_to(pad_row, (T, T))
        seg_i = seg_j.T
        pad_i = pad_j.T
        same = seg_i == seg_j
        open_key = same & (((j_pos < i_pos) & (pad_j == 1.0)) | (i_pos == j_pos))
        far_mask[r] = open_key.astype(F32)
        near_mask[r] = (open_key & (i_pos - j_pos <= BAND)).astype(F32)
        last = seg_i[T - 1 : T, :]
        tail_mask[r] = ((seg_i == last) & (pad_i == 1.0)).astype(F32)
        use_mask[r] = seg_i
        info_own[0, r : r + 1, :] = last
        info_own[1, r : r + 1, :] = jnp.where(pad_row == 1.0, seg_row + 1.0, 0.0)

    head = pl.ds(0, T - HALO)
    hk_s[:, head, :] = jnp.zeros((U, T - HALO, T), BF)
    hv_s[:, head, :] = jnp.zeros((U, T - HALO, T), BF)

    @pl.when(sq == 0)
    def _():
        tail = pl.ds(T - HALO, HALO)
        hk_s[:, tail, :] = jnp.zeros((U, HALO, T), BF)
        hv_s[:, tail, :] = jnp.zeros((U, HALO, T), BF)

    @pl.when(sq == n - 1)
    def _():
        hdk_r[...] = jnp.zeros((U, HALO, T), BF)
        hdv_r[...] = jnp.zeros((U, HALO, T), BF)

    ones_block = block_ones()

    def local_state(u, _):
        r = unit_row(u)
        tail = tail_mask[r].astype(BF)
        keys = k_s[u].astype(F32)
        values = v_s[u]
        norms = []
        for a, (feature, _slope) in enumerate(FEATURES):
            fk = feature(keys).astype(BF)
            fk_s[a, u] = fk
            weighted = fk * tail
            pay_s[0, u, a * E : (a + 1) * E, :] = pick(tn(weighted, values)).astype(BF)
            norm = jnp.sum(weighted.astype(F32), 0, keepdims=True)
            norms.append(jnp.broadcast_to(norm, (8, T)))
        pay_s[0, u, 2 * E : PAY, :] = jnp.concatenate(norms, 0).astype(BF)
        return 0

    lax.fori_loop(0, U, local_state, 0)

    pl.semaphore_wait(barrier, jnp.minimum(sq, 2) + jnp.minimum(n - 1 - sq, 2) + len(greet))

    def starts_of(chunk, color):
        start = CHUNKS[chunk][0]
        found = [start]
        for axis, low, group, split, _rows, part, _offset in plans[chunk][color]:
            if split:
                start = start + peer_of(axis, low, group, 1)[0] * part
            found.append(start)
        return found

    starts = [[starts_of(c, color) for color in range(2)] for c in range(len(CHUNKS))]

    def aligned(start, size):
        return pl.ds(pl.multiple_of(start, 16), size)

    def sum_copy(src, dst, chunk, color, slot, d, to):
        return pltpu.make_async_remote_copy(
            src_ref=src,
            dst_ref=dst,
            send_sem=sum_send.at[chunk, color, slot, d - 1],
            recv_sem=sum_recv.at[chunk, color, slot, d - 1],
            device_id=to,
            device_id_type=MESH,
        )

    def scatter_copy(chunk, color, k, d):
        axis, low, group, split, _rows, part, offset = plans[chunk][color][k]
        mine, to = peer_of(axis, low, group, d)
        start = starts[chunk][color][k]
        if split:
            start = start + lax.rem(mine + d, group) * part
        src = grads.at[color, aligned(start, part)]
        dst = landed.at[color, pl.ds(offset + (d - 1) * part, part)]
        return sum_copy(src, dst, chunk, color, k, d, to)

    def scatter_add(chunk, color, k):
        axis, low, group, split, _rows, part, offset = plans[chunk][color][k]
        for d in range(1, group):
            scatter_copy(chunk, color, k, d).wait_recv()
        if not split:
            scatter_copy(chunk, color, k, 1).wait_send()
        start = starts[chunk][color][k + 1]
        block = math.gcd(part, 128)
        target = full if k + 1 == len(plans[chunk][color]) else grads

        def add(i, _):
            here = aligned(start + i * block, block)
            value = grads[color, here, :]
            for d in range(1, group):
                at = pl.multiple_of(offset + (d - 1) * part + i * block, 16)
                value += landed[color, pl.ds(at, block), :]
            target[color, here, :] = value
            return 0

        lax.fori_loop(0, part // block, add, 0)

    def gather_copy(chunk, color, k, d):
        axis, low, group, _split, _rows, part, _offset = plans[chunk][color][k]
        here = full.at[color, aligned(starts[chunk][color][k + 1], part)]
        slot = 2 * len(plans[chunk][color]) - 1 - k
        return sum_copy(here, here, chunk, color, slot, d, peer_of(axis, low, group, d)[1])

    def gather_arrival(chunk, color, k):
        axis, low, group, _split, _rows, part, _offset = plans[chunk][color][k]
        slot = 2 * len(plans[chunk][color]) - 1 - k
        for d in range(1, group):
            mine, to = peer_of(axis, low, group, d)
            source = lax.rem(mine - d + group, group)
            here = full.at[color, aligned(starts[chunk][color][k] + source * part, part)]
            sum_copy(here, here, chunk, color, slot, d, to).wait_recv()

    def sum_step(chunk, color, k):
        plan = plans[chunk][color]
        K = len(plan)
        if 1 <= k <= K:
            scatter_add(chunk, color, k - 1)
        elif K < k <= 2 * K and plan[2 * K - k][3]:
            gather_arrival(chunk, color, 2 * K - k)
        if k < K:
            for d in range(1, plan[k][2]):
                scatter_copy(chunk, color, k, d).start()
        elif k < 2 * K and plan[2 * K - 1 - k][3]:
            for d in range(1, plan[2 * K - 1 - k][2]):
                gather_copy(chunk, color, 2 * K - 1 - k, d).start()

    def full_copy(chunk, color):
        base, rows = CHUNKS[chunk]
        here = pl.ds(base, rows)
        return pltpu.make_async_copy(
            full.at[color, here], full_hbm.at[color, here], full_sem.at[chunk, color]
        )

    done = {}

    def sums(steps):
        for chunk, color, k in steps:
            last = 2 * len(plans[chunk][color])
            at = done.get((chunk, color), 0)
            while at <= min(k, last):
                sum_step(chunk, color, at)
                at += 1
                if at > last:
                    full_copy(chunk, color).start()
            done[chunk, color] = at

    def sums_rest():
        while True:
            left = [
                (chunk, color, done.get((chunk, color), 0))
                for chunk in range(len(CHUNKS))
                for color in range(2)
                if done.get((chunk, color), 0) <= 2 * len(plans[chunk][color])
            ]
            if not left:
                return
            sums(left)

    def sum_drain(chunk):
        for color in range(2):
            for k, stage in enumerate(plans[chunk][color]):
                for d in range(1, stage[2]):
                    if stage[3]:
                        scatter_copy(chunk, color, k, d).wait_send()
                        gather_copy(chunk, color, k, d).wait_send()

    def small_copy(b):
        axis, low = partners[b]
        return pltpu.make_async_remote_copy(
            src_ref=small_s,
            dst_ref=small_r.at[b],
            send_sem=small_send.at[b],
            recv_sem=small_recv.at[b],
            device_id=peer_of(axis, low, 2, 1)[1],
            device_id_type=MESH,
        )

    def small_step(b):
        if 1 <= b <= len(partners):
            small_copy(b - 1).wait()
            small_s[...] += small_r[b - 1]
        if b < len(partners):
            small_copy(b).start()

    def keep(base, value):
        low = value.astype(BF)
        rows = pl.ds(base, value.shape[0])
        grads[0, rows, :] = low[:, :LANES]
        grads[1, rows, :] = low[:, LANES:]

    def info_copy(slot, to):
        return send(info_own, info_in.at[slot], info_send.at[slot], info_recv.at[slot], to)

    def halo_copy(which, to):
        src, dst = ((k_s, hk_s), (v_s, hv_s))[which]
        tail = pl.ds(T - HALO, HALO)
        return send(
            src.at[:, tail, :], dst.at[:, tail, :], halo_send.at[which], halo_recv.at[which], to
        )

    for slot, step in enumerate((1, 2, -1)):
        inside = (sq + step >= 0) & (sq + step < n)
        came = (sq - step >= 0) & (sq - step < n)

        @pl.when(inside)
        def _():
            info_copy(slot, sq + step).start()

        @pl.when(jnp.logical_not(came))
        def _():
            info_in[slot, 0] = jnp.full((8, T), -1.0, F32)
            info_in[slot, 1] = jnp.zeros((8, T), F32)

    def half(which, r):
        return pl.ds(which * HU + 2 * r, 2)

    def chain_copy(way, stage, r):
        step = 1 - 2 * way
        here = pl.ds(2 * r, 2)
        src, dst, to = (
            (pay_s.at[way, half(1 - par, r)], m1_r.at[way, here], partner),
            (pass_s.at[way, here], carry_r.at[way, here], sq + 2 * step),
            (give_s.at[way, here], in_s.at[way, half(par, r)], partner),
        )[stage]
        return send(src, dst, chain_send.at[way, stage, r], chain_recv.at[way, stage, r], to)

    def chain_arrival(way, stage, r):
        here = pl.ds(2 * r, 2)
        dst = (m1_r.at[way, here], carry_r.at[way, here], in_s.at[way, half(1 - par, r)])[stage]
        return send(dst, dst, chain_send.at[way, stage, r], chain_recv.at[way, stage, r], partner)

    def has_next(way):
        return (z + 1 < nz) if way == 0 else (z > 0)

    def has_before(way):
        return (z > 0) if way == 0 else (z + 1 < nz)

    def marks(r):
        own = info_own[0, r : r + 1, :]
        before, before_two, after = (info_in[s, 0, r : r + 1, :] for s in range(3))
        first = par == 0
        last_a = jnp.where(first, own, before)
        last_b = jnp.where(first, after, own)
        last_z = jnp.where(first, before, before_two)
        inner = (last_a == last_b).astype(F32)
        enter = (last_z == last_a).astype(F32)
        through = (last_z == last_b).astype(F32)
        return inner, enter, through

    def chain_begin(way):
        for r in range(R):
            chain_copy(way, 0, r).start()

        @pl.when(jnp.logical_not(has_before(way)))
        def _():
            carry_r[way] = jnp.zeros((HU, PAY, T), BF)

    def chain_pair(way):
        second = par == (1 - way)
        for r in range(R):
            chain_arrival(way, 0, r).wait_recv()
            inner, enter, _through = marks(r)
            weight = inner if way == 0 else enter
            one = jnp.ones_like(weight)
            mine = jnp.where(second, one, weight)
            other = jnp.where(second, weight, one)
            for j in range(2):
                own = pay_s[way, par * HU + 2 * r + j].astype(F32)
                got = m1_r[way, 2 * r + j].astype(F32)
                sum_s[2 * r + j] = mine * own + other * got

    def chain_pass(way):
        second = par == (1 - way)
        for r in range(R):

            @pl.when(has_before(way))
            def _():
                chain_arrival(way, 1, r).wait_recv()

            inner, enter, through = marks(r)
            weight = enter if way == 0 else inner
            for j in range(2):
                carry = carry_r[way, 2 * r + j].astype(F32)
                pass_s[way, 2 * r + j] = (sum_s[2 * r + j] + through * carry).astype(BF)

            @pl.when(has_next(way))
            def _():
                chain_copy(way, 1, r).start()

            for j in range(2):
                carry = carry_r[way, 2 * r + j].astype(F32)
                own = pay_s[way, par * HU + 2 * r + j].astype(F32)
                got = m1_r[way, 2 * r + j].astype(F32)
                later = jnp.where(second, got, own) + weight * carry
                in_s[way, par * HU + 2 * r + j] = jnp.where(second, later, carry).astype(BF)
                give_s[way, 2 * r + j] = jnp.where(second, carry, later).astype(BF)
            chain_copy(way, 2, r).start()

    def chain_finish(way):
        for r in range(R):
            chain_arrival(way, 2, r).wait_recv()

    def chain_drain(way):
        for r in range(R):
            chain_copy(way, 0, r).wait_send()

            @pl.when(has_next(way))
            def _():
                chain_copy(way, 1, r).wait_send()

            chain_copy(way, 2, r).wait_send()

    chain_begin(0)

    @pl.when(sq + 1 < n)
    def _():
        for which in range(2):
            halo_copy(which, sq + 1).start()

    project(6, w_query, q_s)
    loads[7].wait()
    loads[8].wait()
    for a in range(2):
        for hp in range(PAIRS):
            sides = [
                jnp.broadcast_to(blend[a : a + 1, 2 * hp + side : 2 * hp + side + 1], (1, T))
                for side in range(2)
            ]
            weight_s[a * PAIRS + hp : a * PAIRS + hp + 1, :] = jnp.where(lane_low(1), *sides)
    ones_pair = two_blocks(jnp.ones((T, T), BF))

    def far_local(u, _):
        r = unit_row(u)
        queries = q_s[u].astype(F32)
        values = two_blocks(v_s[u])
        mask = far_mask[r]
        mask = jnp.concatenate([mask, mask], 1)
        for a, (feature, _slope) in enumerate(FEATURES):
            fq = feature(queries).astype(BF)
            fq_s[a, u] = fq
            kernel = (nt(fq, two_blocks(fk_s[a, u])) * mask).astype(BF)
            kk_s[a, u] = kernel
            far_s[a, u] = nn(kernel, values)
            den_s[a, u] = nn(kernel, ones_pair)
        return 0

    lax.fori_loop(0, U, far_local, 0)

    for slot, step in enumerate((1, 2, -1)):
        came = (sq - step >= 0) & (sq - step < n)

        @pl.when(came)
        def _():
            info_copy(slot, sq).wait_recv()

    @pl.when(sq > 0)
    def _():
        for which in range(2):
            halo_copy(which, sq).wait_recv()

    i_low = lax.broadcasted_iota(jnp.int32, (HALO, T), 0)
    j_low = lax.broadcasted_iota(jnp.int32, (HALO, T), 1)
    for r in range(R):
        seg_i = use_mask[r]
        marks_before = info_in[0, 1, r : r + 1, :]
        reach = j_low >= T - BAND + i_low
        halo_mask[r] = (reach & (seg_i[:HALO] + 1.0 == marks_before)).astype(F32)
        use_mask[r] = (seg_i == info_in[0, 0, r : r + 1, :]).astype(F32)

    chain_pair(0)

    def near_local(u, _):
        r = unit_row(u)
        queries = q_s[u]
        scores = nt(queries, two_blocks(k_s[u])) * SCALE
        scores_halo = nt(queries[:HALO], two_blocks(hk_s[u])) * SCALE
        open_near = near_mask[r] > 0
        open_halo = halo_mask[r] > 0
        for side in range(2):
            lanes = slice(side * T, (side + 1) * T)
            s = jnp.where(open_near, scores[:, lanes], NEGATIVE)
            sh = jnp.where(open_halo, scores_halo[:, lanes], NEGATIVE)
            peak = jnp.max(s, -1, keepdims=True)
            peak_halo = jnp.maximum(peak[:HALO], jnp.max(sh, -1, keepdims=True))
            peak = jnp.concatenate([peak_halo, peak[HALO:]], 0)
            e = jnp.exp(s - peak)
            eh = jnp.exp(sh - peak_halo)
            norm = jnp.sum(e, -1, keepdims=True)
            norm_halo = norm[:HALO] + jnp.sum(eh, -1, keepdims=True)
            inverse = 1.0 / jnp.concatenate([norm_halo, norm[HALO:]], 0)
            p_s[u, :, lanes] = e * inverse
            ph_s[u, :, lanes] = eh * inverse[:HALO]
        near_s[u] = nn(p_s[u].astype(BF), two_blocks(v_s[u]))
        near_s[u, :HALO, :] += nn(ph_s[u].astype(BF), two_blocks(hv_s[u]))
        return 0

    cut = z * U // nz
    lax.fori_loop(0, cut, near_local, 0)
    chain_pass(0)
    lax.fori_loop(cut, U, near_local, 0)
    chain_finish(0)

    def blend_lanes(a, u):
        return weight_s[pl.ds(a * PAIRS + unit_pair(u), 1), :]

    def far_finish(u, _):
        r = unit_row(u)
        hp = unit_pair(u)
        use = use_mask[r]
        blended = near_s[u]
        for a in range(2):
            fq = fq_s[a, u]
            state = two_blocks(in_s[0, u, a * E : (a + 1) * E, :])
            norm = in_s[0, u, 2 * E + 8 * a : 2 * E + 8 * a + 1, :].astype(F32)
            numer = far_s[a, u] + use * nn(fq, state)
            weighted = (fq.astype(F32) * norm).astype(BF)
            denom = den_s[a, u] + use * nn(weighted, ones_block)
            far = numer / denom
            far_s[a, u] = far
            den_s[a, u] = denom
            blended = blended + blend_lanes(a, u) * far
        rows = pl.ds(pl.multiple_of(r * T, T), T)
        lanes = pl.ds(pl.multiple_of(hp * T, T), T)
        mixed[rows, lanes] = blended.astype(BF)
        return 0

    lax.fori_loop(0, U, far_finish, 0)

    loads[9].wait()
    middle[...] = tok[...].astype(F32) + nn(mixed[...], w_out[...])
    for r in range(R):
        rows = pl.ds(r * T, T)
        mid = middle[rows, :]
        inverse = lax.rsqrt(jnp.mean(mid * mid, -1, keepdims=True) + EPSILON)
        normed_two[rows, :] = (mid * inverse * gain_two[...]).astype(BF)
    total[...] = jnp.zeros_like(total)
    back_two[...] = jnp.zeros_like(back_two)
    for i in (10, 11, 12):
        loads[i].wait()

    def feed(t, _):
        at = pl.multiple_of(t * D, D)
        cols = pl.ds(at, D)
        up = nn(normed_two[...], w_up[:, cols])
        square = up * up
        tangent = jnp.tanh(GELU_A * (up + GELU_B * square * up))
        act = (0.5 * up * (1.0 + tangent)).astype(BF)
        slope = 0.5 * (1.0 + tangent) + 0.5 * up * (1.0 - tangent * tangent) * GELU_A * (
            1.0 + 3.0 * GELU_B * square
        )
        total[...] += nn(act, w_down[cols, :])
        keep(pl.multiple_of(row_down(t), D), tn(act, cot[...]))
        d_up = (nt(cot[...], w_down[cols, :]) * slope).astype(BF)
        keep(pl.multiple_of(row_up(t), D), tn(normed_two[...], d_up))
        back_two[...] += nt(d_up, w_up[:, cols])
        return 0

    lax.fori_loop(0, TILES // 2, feed, 0)
    sums(ORDER["down"])
    lax.fori_loop(TILES // 2, TILES, feed, 0)
    sums(ORDER["up"])
    out[...] = (middle[...] + total[...]).astype(BF)

    gain_grad_two = jnp.zeros((1, D), F32)
    for r in range(R):
        rows = pl.ds(r * T, T)
        mid = middle[rows, :]
        inverse = lax.rsqrt(jnp.mean(mid * mid, -1, keepdims=True) + EPSILON)
        d_n = back_two[rows, :]
        gain_grad_two += jnp.sum(d_n * mid * inverse, 0, keepdims=True)
        scaled = d_n * gain_two[...]
        d_mid = (
            cot[rows, :].astype(F32)
            + inverse * scaled
            - mid * (inverse * inverse * inverse) * jnp.mean(mid * scaled, -1, keepdims=True)
        )
        total[rows, :] = d_mid
        normed_two[rows, :] = d_mid.astype(BF)
    d_branch = normed_two[...]
    keep(ROW_OUT, tn(mixed[...], d_branch))
    d_blended = nt(d_branch, w_out[...]).astype(BF)
    for r in range(R):
        for hp in range(PAIRS):
            db_s[unit_of(r, hp)] = d_blended[r * T : (r + 1) * T, hp * T : (hp + 1) * T]
    sums(ORDER["branch"])

    gb_s[...] = jnp.zeros_like(gb_s)

    def far_prepare(u, _):
        r = unit_row(u)
        hp = unit_pair(u)
        use = use_mask[r]
        use_low = use.astype(BF)
        d_out = db_s[u].astype(F32)
        norms = []
        for a in range(2):
            far = far_s[a, u]
            inverse = 1.0 / den_s[a, u]
            product = d_out * far
            row = a * PAIRS + hp
            gb_s[pl.ds(row, 1), :] += jnp.sum(product, 0, keepdims=True)
            weight = blend_lanes(a, u)
            product = product * weight
            high = product.astype(BF)
            rest = (product - high.astype(F32)).astype(BF)
            dden = -(nn(high, ones_block) + nn(rest, ones_block)) * inverse
            dden_s[a, u] = dden
            dnum = (weight * d_out * inverse).astype(BF)
            low_s[a, u] = dnum
            used = fq_s[a, u] * use_low
            pay_s[1, u, a * E : (a + 1) * E, :] = pick(tn(used, dnum)).astype(BF)
            norm = jnp.sum(used.astype(F32) * dden, 0, keepdims=True)
            norms.append(jnp.broadcast_to(norm, (8, T)))
        pay_s[1, u, 2 * E : PAY, :] = jnp.concatenate(norms, 0).astype(BF)
        return 0

    lax.fori_loop(0, U, far_prepare, 0)
    chain_begin(1)

    def near_back(u, _):
        keys = two_blocks(k_s[u])
        halo_keys = two_blocks(hk_s[u])
        queries = q_s[u]
        d_out = db_s[u]
        dp = nt(d_out, two_blocks(v_s[u]))
        dp_halo = nt(d_out[:HALO], two_blocks(hv_s[u]))
        p = p_s[u]
        p_halo = ph_s[u]
        ds = []
        ds_halo = []
        for side in range(2):
            lanes = slice(side * T, (side + 1) * T)
            ps, phs = p[:, lanes], p_halo[:, lanes]
            delta = jnp.sum(ps * dp[:, lanes], -1, keepdims=True)
            delta_halo = delta[:HALO] + jnp.sum(phs * dp_halo[:, lanes], -1, keepdims=True)
            delta = jnp.concatenate([delta_halo, delta[HALO:]], 0)
            ds.append(ps * (dp[:, lanes] - delta))
            ds_halo.append(phs * (dp_halo[:, lanes] - delta_halo))
        ds = jnp.concatenate(ds, 1).astype(BF)
        ds_halo = jnp.concatenate(ds_halo, 1).astype(BF)
        near_s[u] = nn(ds, keys) * SCALE
        near_s[u, :HALO, :] += nn(ds_halo, halo_keys) * SCALE
        dk_s[u] = pick(tn(ds, queries)) * SCALE
        dv_s[u] = pick(tn(p.astype(BF), d_out))
        hdk_s[u] = (pick(tn(ds_halo, queries[:HALO])) * SCALE)[T - HALO :].astype(BF)
        hdv_s[u] = pick(tn(p_halo.astype(BF), d_out[:HALO]))[T - HALO :].astype(BF)
        return 0

    sums(ORDER["prepare"])
    lax.fori_loop(0, HU, near_back, 0)
    sums(ORDER["near_a"])
    lax.fori_loop(HU, U, near_back, 0)
    sums(ORDER["near_b"])

    def halo_back(which, to):
        src, dst = ((hdk_s, hdk_r), (hdv_s, hdv_r))[which]
        return send(src, dst, halo_send.at[2 + which], halo_recv.at[2 + which], to)

    @pl.when(sq > 0)
    def _():
        for which in range(2):
            halo_back(which, sq - 1).start()

    chain_pair(1)
    sums(ORDER["pair"])

    def far_back(u, _):
        r = unit_row(u)
        values = two_blocks(v_s[u])
        mask = far_mask[r]
        mask = jnp.concatenate([mask, mask], 1)
        use = use_mask[r]
        queries = q_s[u].astype(F32)
        keys = k_s[u].astype(F32)
        dq = near_s[u]
        dk = dk_s[u]
        dv = dv_s[u]
        for a, (_feature, slope) in enumerate(FEATURES):
            dnum = low_s[a, u]
            dden = dden_s[a, u]
            fq = fq_s[a, u]
            fk = two_blocks(fk_s[a, u])
            added = jnp.concatenate(
                [
                    jnp.broadcast_to(dden[:, 0:1], (T, T)),
                    jnp.broadcast_to(dden[:, E : E + 1], (T, T)),
                ],
                1,
            )
            d_kernel = ((nt(dnum, values) + added) * mask).astype(BF)
            dv += pick(tn(kk_s[a, u], dnum))
            state = two_blocks(in_s[0, u, a * E : (a + 1) * E, :])
            norm = in_s[0, u, 2 * E + 8 * a : 2 * E + 8 * a + 1, :].astype(F32)
            dfq = nn(d_kernel, fk) + use * (nt(dnum, state) + dden * norm)
            dq += dfq * slope(queries)
            dk += pick(tn(d_kernel, fq)) * slope(keys)
        near_s[u] = dq
        dk_s[u] = dk
        dv_s[u] = dv
        return 0

    turn = (nz - 1 - z) * PARTS // nz
    for part in range(PARTS):

        @pl.when(turn == part)
        def _():
            chain_pass(1)

        lax.fori_loop(part * U // PARTS, (part + 1) * U // PARTS, far_back, 0)
        sums(ORDER["far_%d" % part])

    for u in range(U):
        r, hp = (u % (2 * R)) // 2, (u // (2 * R)) * 2 + u % 2
        wide_s[0, r * T : (r + 1) * T, hp * T : (hp + 1) * T] = near_s[u].astype(BF)
    keep(ROW_Q, tn(normed[...], wide_s[0]))
    sums(ORDER["query"])
    back_two[...] = nt(wide_s[0], w_query[...])

    @pl.when(sq + 1 < n)
    def _():
        for which in range(2):
            halo_back(which, sq).wait_recv()

    chain_finish(1)
    sums(ORDER["state"])

    def far_close(u, _):
        r = unit_row(u)
        hp = unit_pair(u)
        tail = tail_mask[r]
        keys = k_s[u].astype(F32)
        values = v_s[u]
        dk = dk_s[u]
        dv = dv_s[u]
        for a, (_feature, slope) in enumerate(FEATURES):
            state = two_blocks(in_s[1, u, a * E : (a + 1) * E, :])
            norm = in_s[1, u, 2 * E + 8 * a : 2 * E + 8 * a + 1, :].astype(F32)
            dk += tail * (nt(values, state) + norm) * slope(keys)
            dv += tail * nn(fk_s[a, u], state)
        zero = jnp.zeros((T - HALO, T), F32)
        dk += jnp.concatenate([zero, hdk_r[u].astype(F32)], 0)
        dv += jnp.concatenate([zero, hdv_r[u].astype(F32)], 0)
        rows = pl.ds(pl.multiple_of(r * T, T), T)
        lanes = pl.ds(pl.multiple_of(hp * T, T), T)
        wide_s[1, rows, lanes] = dk.astype(BF)
        wide_s[2, rows, lanes] = dv.astype(BF)
        return 0

    lax.fori_loop(0, U, far_close, 0)
    sums(ORDER["close"])
    for i in (1, 2):
        keep(ROW_Q + i * D, tn(normed[...], wide_s[i]))
    sums(ORDER["key"])
    for i, weight in ((1, w_key), (2, w_value)):
        back_two[...] += nt(wide_s[i], weight[...])
    gain_grad_one = jnp.zeros((1, D), F32)
    for r in range(R):
        rows = pl.ds(r * T, T)
        x = tok[rows, :].astype(F32)
        inverse = lax.rsqrt(jnp.mean(x * x, -1, keepdims=True) + EPSILON)
        d_n = back_two[rows, :]
        gain_grad_one += jnp.sum(d_n * x * inverse, 0, keepdims=True)
        scaled = d_n * gain_one[...]
        d_x = (
            total[rows, :]
            + inverse * scaled
            - x * (inverse * inverse * inverse) * jnp.mean(x * scaled, -1, keepdims=True)
        )
        grad_tok[rows, :] = d_x.astype(BF)
    blends = [
        jnp.concatenate([gb_s[a * PAIRS + hp : a * PAIRS + hp + 1, :] for hp in range(PAIRS)], 1)
        for a in range(2)
    ]
    small_s[...] = jnp.concatenate(
        [gain_grad_one, gain_grad_two] + blends + [jnp.zeros((SMALL - 4, D), F32)], 0
    )
    small_step(0)
    sums(ORDER["back"])
    for i, step in enumerate(ORDER["tail"]):
        sums((step,))
        if i % 2 and i // 2 < len(partners):
            small_step(i // 2 + 1)
    for b in range(len(ORDER["tail"]) // 2, len(partners)):
        small_step(b + 1)
    sums_rest()
    small_out[...] = small_s[...]

    for slot, step in enumerate((1, 2, -1)):

        @pl.when((sq + step >= 0) & (sq + step < n))
        def _():
            info_copy(slot, sq + step).wait_send()

    @pl.when(sq + 1 < n)
    def _():
        for which in range(2):
            halo_copy(which, sq + 1).wait_send()

    @pl.when(sq > 0)
    def _():
        for which in range(2):
            halo_back(which, sq - 1).wait_send()

    chain_drain(0)
    chain_drain(1)
    for c in range(len(CHUNKS)):
        sum_drain(c)
        for color in range(2):
            full_copy(c, color).wait()


def widen_kernel(
    grads,
    small,
    out_in,
    back_in,
    g_one,
    g_two,
    g_blend,
    g_query,
    g_key,
    g_value,
    g_out,
    g_up,
    g_down,
    out,
    back,
    held,
    wide,
    in_sem,
    out_sem,
    same_sem,
):
    blocks = ROWS_ALL // D
    targets = []
    for t in (0, 2):
        targets += [g_down.at[pl.ds((t + i) * D, D)] for i in range(2)]
        targets += [g_up.at[:, pl.ds((t + i) * D, D)] for i in range(2)]
    targets += [g_out, g_query, g_key, g_value]
    reads = [
        pltpu.make_async_copy(grads.at[:, pl.ds(i * D, D)], held.at[i], in_sem.at[i])
        for i in range(blocks)
    ]
    for read in reads:
        read.start()
    writes = [
        pltpu.make_async_copy(wide.at[i], targets[i], out_sem.at[i]) for i in range(blocks)
    ]
    same = [
        pltpu.make_async_copy(out_in, out, same_sem.at[0]),
        pltpu.make_async_copy(back_in, back, same_sem.at[1]),
    ]
    for copy in same:
        copy.start()
    g_one[...] = small[0]
    g_two[...] = small[1]
    for a in range(2):
        row = small[2 + a : 3 + a, :]
        lane = lax.broadcasted_iota(jnp.int32, (H, D), 1) // E
        head = lax.broadcasted_iota(jnp.int32, (H, D), 0)
        per_head = jnp.sum(jnp.where(lane == head, row, 0.0), -1, keepdims=True)
        g_blend[a : a + 1, :] = jnp.broadcast_to(per_head, (H, H)).T[:1]
    for i in range(blocks):
        reads[i].wait()
        wide[i, :, :LANES] = held[i, 0].astype(F32)
        wide[i, :, LANES:] = held[i, 1].astype(F32)
        writes[i].start()
    for copy in writes + same:
        copy.wait()


def solution(mesh):
    n = mesh.shape["seq"]
    n_rows = mesh.shape["rows"]

    def shards(
        tokens,
        segment_ids,
        padding,
        gain_one,
        w_query,
        w_key,
        w_value,
        blend,
        w_out,
        gain_two,
        w_up,
        w_down,
        cotangent,
    ):
        R, tok_count, _ = tokens.shape
        M = R * tok_count
        U = R * PAIRS
        HU = U // 2
        vmem = pl.BlockSpec(memory_space=pltpu.VMEM)
        anyspace = pl.BlockSpec(memory_space=pl.ANY)
        V = pltpu.VMEM
        unit_f = V((U, T, T), F32)
        unit_b = V((U, T, T), BF)
        two_f = V((2, U, T, T), F32)
        two_b = V((2, U, T, T), BF)
        wide_f = V((M, D), F32)
        wide_b = V((M, D), BF)
        halo_b = V((U, HALO, T), BF)
        dma = pltpu.SemaphoreType.DMA
        plans, landed_rows = sum_plans(n_rows, n)
        stages = 2 * max(len(plan) for both in plans for plan in both)
        count = bits(n) + bits(n_rows)
        scratch = [
            V((2, ROWS_ALL, LANES), BF),
            V((2, ROWS_ALL, LANES), BF),
            V((2, landed_rows, LANES), BF),
            V((SMALL, D), F32),
            V((count, SMALL, D), F32),
            wide_b,
            V((R, T), jnp.int32),
            V((R, T), jnp.int32),
            V((1, D), F32),
            V((1, D), F32),
            V((2, H), F32),
            V((D, D), BF),
            V((D, D), BF),
            V((D, D), BF),
            V((D, D), BF),
            V((D, FF), BF),
            V((FF, D), BF),
            wide_b,
            V((2 * PAIRS, T), F32),
            wide_b,
            wide_b,
            wide_b,
            wide_f,
            wide_f,
            wide_f,
            unit_b,
            unit_b,
            unit_b,
            unit_b,
            unit_b,
            two_b,
            two_b,
            V((2, U, T, 2 * T), BF),
            V((U, T, 2 * T), F32),
            V((U, HALO, 2 * T), F32),
            unit_f,
            two_f,
            two_f,
            unit_b,
            two_b,
            two_f,
            unit_f,
            unit_f,
            halo_b,
            halo_b,
            halo_b,
            halo_b,
            V((3, M, D), BF),
            V((R, T, T), F32),
            V((R, T, T), F32),
            V((R, T, T), F32),
            V((R, T, T), F32),
            V((R, HALO, T), F32),
            V((2, 8, T), F32),
            V((3, 2, 8, T), F32),
            V((2 * PAIRS, T), F32),
            V((2, U, PAY, T), BF),
            V((2, HU, PAY, T), BF),
            V((HU, PAY, T), F32),
            V((2, HU, PAY, T), BF),
            V((2, HU, PAY, T), BF),
            V((2, U, PAY, T), BF),
            V((2, HU, PAY, T), BF),
            dma((13,)),
            dma((3,)),
            dma((3,)),
            dma((4,)),
            dma((4,)),
            dma((2, 3, R)),
            dma((2, 3, R)),
            dma((len(CHUNKS), 2, stages, 3)),
            dma((len(CHUNKS), 2, stages, 3)),
            dma((count,)),
            dma((count,)),
            dma((len(CHUNKS), 2)),
        ]
        out, grad_tok, small, grads = pl.pallas_call(
            functools.partial(layer_kernel, n, n_rows, R),
            out_shape=(
                jax.ShapeDtypeStruct((M, D), BF),
                jax.ShapeDtypeStruct((M, D), BF),
                jax.ShapeDtypeStruct((SMALL, D), F32),
                jax.ShapeDtypeStruct((2, ROWS_ALL, LANES), BF),
            ),
            in_specs=[pl.BlockSpec(memory_space=pltpu.HBM)] * 13,
            out_specs=(vmem, vmem, vmem, anyspace),
            scratch_shapes=scratch,
            compiler_params=pltpu.CompilerParams(
                collective_id=0, has_side_effects=True, vmem_limit_bytes=LAYER_VMEM
            ),
            name="layer",
        )(
            tokens.reshape(M, D),
            segment_ids,
            padding,
            gain_one.reshape(1, D),
            gain_two.reshape(1, D),
            blend,
            w_query,
            w_key,
            w_value,
            w_out,
            w_up,
            w_down,
            cotangent.reshape(M, D),
        )
        square = jax.ShapeDtypeStruct((D, D), F32)
        token = jax.ShapeDtypeStruct((M, D), BF)
        blocks = ROWS_ALL // D
        g_one, g_two, g_blend, g_query, g_key, g_value, g_out, g_up, g_down, out, grad_tok = (
          pl.pallas_call(
            widen_kernel,
            out_shape=(
                jax.ShapeDtypeStruct((D,), F32),
                jax.ShapeDtypeStruct((D,), F32),
                jax.ShapeDtypeStruct((2, H), F32),
                square,
                square,
                square,
                square,
                jax.ShapeDtypeStruct((D, FF), F32),
                jax.ShapeDtypeStruct((FF, D), F32),
                token,
                token,
            ),
            in_specs=[anyspace, vmem, vmem, vmem],
            out_specs=(vmem,) * 3 + (anyspace,) * 8,
            scratch_shapes=[
                V((blocks, 2, D, LANES), BF),
                V((blocks, D, D), F32),
                dma((blocks,)),
                dma((blocks,)),
                dma((2,)),
            ],
            compiler_params=pltpu.CompilerParams(vmem_limit_bytes=WIDEN_VMEM),
            name="widen",
        )(grads, small, out, grad_tok))
        return (
            out.reshape(R, tok_count, D),
            grad_tok.reshape(R, tok_count, D),
            g_one,
            g_query,
            g_key,
            g_value,
            g_blend,
            g_out,
            g_two,
            g_up,
            g_down,
        )

    row, whole = P("rows", "seq", None), P()
    return jax.shard_map(
        shards,
        mesh=mesh,
        in_specs=(row, P("rows", "seq"), P("rows", "seq")) + (whole,) * 9 + (row,),
        out_specs=(row, row) + (whole,) * 9,
        check_vma=False,
    )
```

```python
import functools
import math

import jax
import jax.numpy as jnp
from jax import lax
from jax.experimental import pallas as pl
from jax.experimental.pallas import tpu as pltpu
from jax.sharding import PartitionSpec as P

MESH = pl.DeviceIdType.MESH
F32 = jnp.float32
BF = jnp.bfloat16
D = 512
H = 8
E = 64
FF = 2048
BAND = 30
T = 128
PAIRS = 4
PAY = 144
HALO = 32
EPSILON = 1e-06
NEGATIVE = -1e30
SCALE = 1.0 / math.sqrt(E)
GELU_A = math.sqrt(2.0 / math.pi)
GELU_B = 0.044715
TILES = FF // D
ROW_OUT = 2 * FF
ROW_Q = ROW_OUT + D
ROWS_ALL = ROW_Q + 3 * D
SMALL = 8
LANES = D // 2
CHUNKS = ((0, FF), (FF, FF), (ROW_OUT, 2 * D), (ROW_Q + D, 2 * D))
DIMS = (("cyxab", "caxyb"), ("cxyq", "cyxq"), ("cyxq", "cxyq"), ("cyxq", "cxyq"))
PARTS = 4
LAYER_VMEM = 60 * 1024 * 1024
WIDEN_VMEM = 60 * 1024 * 1024


ORDER = {
    "down": (
        (0, 0, 0), (0, 1, 0),
    ),
    "up": (),
    "branch": (),
    "prepare": (
        (1, 1, 0), (0, 1, 1), (1, 0, 0), (0, 0, 1),
    ),
    "near_a": (
        (1, 0, 1), (1, 1, 1),
    ),
    "near_b": (
        (0, 1, 2),
    ),
    "pair": (
        (0, 0, 2),
    ),
    "far_0": (),
    "far_1": (
        (0, 1, 3), (1, 0, 2), (0, 0, 3), (1, 1, 2), (0, 1, 4),
    ),
    "far_2": (),
    "far_3": (),
    "query": (
        (1, 0, 3),
    ),
    "state": (
        (0, 0, 4),
    ),
    "close": (
        (2, 1, 0), (2, 0, 0), (0, 1, 5),
    ),
    "key": (
        (2, 1, 1), (3, 0, 0), (1, 1, 3), (3, 1, 0), (2, 0, 1), (3, 1, 1),
        (1, 0, 4), (3, 0, 1), (2, 0, 2), (1, 1, 4), (2, 1, 2), (1, 0, 5),
        (3, 0, 2), (2, 0, 3), (2, 1, 3), (3, 1, 2), (0, 1, 6), (1, 1, 5),
        (0, 0, 5),
    ),
    "back": (
        (1, 0, 6), (2, 0, 4), (2, 1, 4), (0, 0, 6), (3, 0, 3), (1, 1, 6),
        (2, 0, 5), (0, 1, 7), (3, 1, 3), (2, 1, 5), (3, 0, 4), (0, 0, 7),
        (3, 1, 4), (1, 0, 7), (1, 1, 7), (2, 0, 6),
    ),
    "tail": (
        (0, 1, 8), (3, 0, 5), (3, 1, 5), (0, 0, 8), (2, 1, 6), (3, 0, 6),
        (3, 1, 6), (2, 1, 7), (0, 1, 9), (2, 0, 7), (0, 0, 9), (3, 1, 7),
        (1, 0, 8), (1, 1, 8), (3, 0, 7), (2, 0, 8), (2, 1, 8), (3, 1, 8),
        (3, 0, 8), (0, 0, 10), (0, 1, 10),
    ),
}


def row_down(t):
    return (t // 2) * FF + (t % 2) * D


def row_up(t):
    return row_down(t) + FF // 2


def nn(a, b):
    return lax.dot_general(a, b, (((1,), (0,)), ((), ())), preferred_element_type=F32)


def nt(a, b):
    return lax.dot_general(a, b, (((1,), (1,)), ((), ())), preferred_element_type=F32)


def tn(a, b):
    return lax.dot_general(a, b, (((0,), (0,)), ((), ())), preferred_element_type=F32)


def lane_low(rows):
    return lax.broadcasted_iota(jnp.int32, (rows, T), 1) < E


def low_high():
    low = lane_low(T).astype(F32)
    return low.astype(BF), (1.0 - low).astype(BF)


def two_blocks(x):
    low, high = low_high()
    rows = x.shape[0]
    return jnp.concatenate([x * low[:rows], x * high[:rows]], 0)


def pick(stacked):
    half = stacked.shape[0] // 2
    return jnp.where(lane_low(half), stacked[:half], stacked[half:])


def block_ones():
    i = lax.broadcasted_iota(jnp.int32, (T, T), 0) < E
    j = lax.broadcasted_iota(jnp.int32, (T, T), 1) < E
    return jnp.where(i == j, 1.0, 0.0).astype(BF)


def feature_one(t):
    return jnp.where(t > 0, t + 1.0, jnp.exp(jnp.minimum(t, 0.0)))


def slope_one(t):
    return jnp.where(t > 0, 1.0, jnp.exp(jnp.minimum(t, 0.0)))


def feature_two(t):
    return 1.0 + jnp.tanh(t)


def slope_two(t):
    tangent = jnp.tanh(t)
    return 1.0 - tangent * tangent


FEATURES = ((feature_one, slope_one), (feature_two, slope_two))


def bits(size):
    return size.bit_length() - 1


def sum_order(dims, n_rows, n_seq):
    rows = [("rows", 2**b, 2) for b in range(bits(n_rows))]
    seq = [("seq", 2**b, 2) for b in range(bits(n_seq))]
    near, far = seq[:-2], seq[-2:]
    found = {
        "c": rows[:1],
        "y": rows[1:],
        "x": near,
        "a": far[:1],
        "b": far[1:],
        "q": [("seq", far[0][1], 4)],
    }
    return [stage for dim in dims for stage in found[dim]]


def sum_plan(dims, n_rows, n_seq, rows, offset):
    plan = []
    for axis, low, group in sum_order(dims, n_rows, n_seq):
        steps = [(low, group)]
        if group == 4 and rows % 64:
            steps = [(low, 2), (2 * low, 2)]
        for low, group in steps:
            split = rows % (16 * group) == 0
            part = rows // group if split else rows
            plan.append((axis, low, group, split, rows, part, offset))
            offset += (group - 1) * part
            rows = part
    return plan, offset


def sum_plans(n_rows, n_seq):
    plans = []
    offset = [0, 0]
    for (_base, rows), dims in zip(CHUNKS, DIMS):
        both = []
        for color in range(2):
            plan, offset[color] = sum_plan(dims[color], n_rows, n_seq, rows, offset[color])
            both.append(plan)
        plans.append(both)
    return plans, max(offset)


def layer_kernel(
    n,
    n_rows,
    R,
    tok_hbm,
    seg_hbm,
    pad_hbm,
    gain_one_hbm,
    gain_two_hbm,
    blend_hbm,
    w_query_hbm,
    w_key_hbm,
    w_value_hbm,
    w_out_hbm,
    w_up_hbm,
    w_down_hbm,
    cot_hbm,
    out,
    grad_tok,
    small_out,
    full_hbm,
    grads,
    full,
    landed,
    small_s,
    small_r,
    tok,
    seg,
    pad,
    gain_one,
    gain_two,
    blend,
    w_query,
    w_key,
    w_value,
    w_out,
    w_up,
    w_down,
    cot,
    weight_s,
    normed,
    normed_two,
    mixed,
    middle,
    total,
    back_two,
    q_s,
    k_s,
    v_s,
    hk_s,
    hv_s,
    fq_s,
    fk_s,
    kk_s,
    p_s,
    ph_s,
    near_s,
    far_s,
    den_s,
    db_s,
    low_s,
    dden_s,
    dk_s,
    dv_s,
    hdk_s,
    hdv_s,
    hdk_r,
    hdv_r,
    wide_s,
    far_mask,
    near_mask,
    use_mask,
    tail_mask,
    halo_mask,
    info_own,
    info_in,
    gb_s,
    pay_s,
    m1_r,
    sum_s,
    carry_r,
    pass_s,
    in_s,
    give_s,
    w_sem,
    info_send,
    info_recv,
    halo_send,
    halo_recv,
    chain_send,
    chain_recv,
    sum_send,
    sum_recv,
    small_send,
    small_recv,
    full_sem,
):
    U = R * PAIRS
    HU = U // 2
    sq = lax.axis_index("seq")
    rw = lax.axis_index("rows")
    par = lax.rem(sq, 2)
    z = sq // 2
    nz = n // 2
    partner = sq + 1 - 2 * par

    def unit_row(u):
        return lax.rem(u, 2 * R) // 2

    def unit_pair(u):
        return (u // (2 * R)) * 2 + lax.rem(u, 2)

    def unit_of(r, hp):
        return (hp // 2) * 2 * R + r * 2 + hp % 2

    def send(src, dst, send_sem, recv_sem, to):
        return pltpu.make_async_remote_copy(
            src_ref=src,
            dst_ref=dst,
            send_sem=send_sem,
            recv_sem=recv_sem,
            device_id=(to, rw),
            device_id_type=MESH,
        )

    barrier = pltpu.get_barrier_semaphore()
    for step in (1, 2):

        @pl.when(sq >= step)
        def _():
            pl.semaphore_signal(barrier, inc=1, device_id=(sq - step, rw), device_id_type=MESH)

        @pl.when(sq + step < n)
        def _():
            pl.semaphore_signal(barrier, inc=1, device_id=(sq + step, rw), device_id_type=MESH)

    plans, _size = sum_plans(n_rows, n)
    partners = [("rows", 2**b) for b in range(bits(n_rows))]
    partners += [("seq", 2**b) for b in range(bits(n))]

    def peer_of(axis, low, group, step):
        own = rw if axis == "rows" else sq
        mine = lax.rem(own // low, group)
        other = own + (lax.rem(mine + step, group) - mine) * low
        return mine, ((sq, other) if axis == "rows" else (other, rw))

    groups = {(axis, low, 2) for axis, low in partners}
    for both in plans:
        for plan in both:
            groups |= {(axis, low, group) for axis, low, group, *_ in plan}
    greet = [(axis, low, group, d) for axis, low, group in sorted(groups) for d in range(1, group)]
    for axis, low, group, d in greet:
        pl.semaphore_signal(
            barrier, inc=1, device_id=peer_of(axis, low, group, d)[1], device_id_type=MESH
        )

    loads = [
        pltpu.make_async_copy(src, dst, w_sem.at[i])
        for i, (src, dst) in enumerate(
            (
                (tok_hbm, tok),
                (gain_one_hbm, gain_one),
                (w_key_hbm, w_key),
                (w_value_hbm, w_value),
                (seg_hbm, seg),
                (pad_hbm, pad),
                (w_query_hbm, w_query),
                (blend_hbm, blend),
                (gain_two_hbm, gain_two),
                (w_out_hbm, w_out),
                (w_up_hbm, w_up),
                (w_down_hbm, w_down),
                (cot_hbm, cot),
            )
        )
    ]
    for load in loads:
        load.start()
    loads[0].wait()
    loads[1].wait()

    for r in range(R):
        rows = pl.ds(r * T, T)
        x = tok[rows, :].astype(F32)
        inverse = lax.rsqrt(jnp.mean(x * x, -1, keepdims=True) + EPSILON)
        normed[rows, :] = (x * inverse * gain_one[...]).astype(BF)

    def project(load, weight, held):
        loads[load].wait()
        whole = nn(normed[...], weight[...]).astype(BF)
        for r in range(R):
            for hp in range(PAIRS):
                held[unit_of(r, hp)] = whole[r * T : (r + 1) * T, hp * T : (hp + 1) * T]

    project(2, w_key, k_s)
    project(3, w_value, v_s)
    loads[4].wait()
    loads[5].wait()

    i_pos = lax.broadcasted_iota(jnp.int32, (T, T), 0)
    j_pos = lax.broadcasted_iota(jnp.int32, (T, T), 1)
    info_own[...] = jnp.zeros_like(info_own)
    for r in range(R):
        seg_row = seg[r : r + 1, :].astype(F32)
        pad_row = pad[r : r + 1, :].astype(F32)
        seg_j = jnp.broadcast_to(seg_row, (T, T))
        pad_j = jnp.broadcast_to(pad_row, (T, T))
        seg_i = seg_j.T
        pad_i = pad_j.T
        same = seg_i == seg_j
        open_key = same & (((j_pos < i_pos) & (pad_j == 1.0)) | (i_pos == j_pos))
        far_mask[r] = open_key.astype(F32)
        near_mask[r] = (open_key & (i_pos - j_pos <= BAND)).astype(F32)
        last = seg_i[T - 1 : T, :]
        tail_mask[r] = ((seg_i == last) & (pad_i == 1.0)).astype(F32)
        use_mask[r] = seg_i
        info_own[0, r : r + 1, :] = last
        info_own[1, r : r + 1, :] = jnp.where(pad_row == 1.0, seg_row + 1.0, 0.0)

    head = pl.ds(0, T - HALO)
    hk_s[:, head, :] = jnp.zeros((U, T - HALO, T), BF)
    hv_s[:, head, :] = jnp.zeros((U, T - HALO, T), BF)

    @pl.when(sq == 0)
    def _():
        tail = pl.ds(T - HALO, HALO)
        hk_s[:, tail, :] = jnp.zeros((U, HALO, T), BF)
        hv_s[:, tail, :] = jnp.zeros((U, HALO, T), BF)

    @pl.when(sq == n - 1)
    def _():
        hdk_r[...] = jnp.zeros((U, HALO, T), BF)
        hdv_r[...] = jnp.zeros((U, HALO, T), BF)

    ones_block = block_ones()

    def local_state(u, _):
        r = unit_row(u)
        tail = tail_mask[r].astype(BF)
        keys = k_s[u].astype(F32)
        values = v_s[u]
        norms = []
        for a, (feature, _slope) in enumerate(FEATURES):
            fk = feature(keys).astype(BF)
            fk_s[a, u] = fk
            weighted = fk * tail
            pay_s[0, u, a * E : (a + 1) * E, :] = pick(tn(weighted, values)).astype(BF)
            norm = jnp.sum(weighted.astype(F32), 0, keepdims=True)
            norms.append(jnp.broadcast_to(norm, (8, T)))
        pay_s[0, u, 2 * E : PAY, :] = jnp.concatenate(norms, 0).astype(BF)
        return 0

    lax.fori_loop(0, U, local_state, 0, unroll=4)

    pl.semaphore_wait(barrier, jnp.minimum(sq, 2) + jnp.minimum(n - 1 - sq, 2) + len(greet))

    def starts_of(chunk, color):
        start = CHUNKS[chunk][0]
        found = [start]
        for axis, low, group, split, _rows, part, _offset in plans[chunk][color]:
            if split:
                start = start + peer_of(axis, low, group, 1)[0] * part
            found.append(start)
        return found

    starts = [[starts_of(c, color) for color in range(2)] for c in range(len(CHUNKS))]

    def aligned(start, size):
        return pl.ds(pl.multiple_of(start, 16), size)

    def sum_copy(src, dst, chunk, color, slot, d, to):
        return pltpu.make_async_remote_copy(
            src_ref=src,
            dst_ref=dst,
            send_sem=sum_send.at[chunk, color, slot, d - 1],
            recv_sem=sum_recv.at[chunk, color, slot, d - 1],
            device_id=to,
            device_id_type=MESH,
        )

    def scatter_copy(chunk, color, k, d):
        axis, low, group, split, _rows, part, offset = plans[chunk][color][k]
        mine, to = peer_of(axis, low, group, d)
        start = starts[chunk][color][k]
        if split:
            start = start + lax.rem(mine + d, group) * part
        src = grads.at[color, aligned(start, part)]
        dst = landed.at[color, pl.ds(offset + (d - 1) * part, part)]
        return sum_copy(src, dst, chunk, color, k, d, to)

    def scatter_add(chunk, color, k):
        axis, low, group, split, _rows, part, offset = plans[chunk][color][k]
        for d in range(1, group):
            scatter_copy(chunk, color, k, d).wait_recv()
        if not split:
            scatter_copy(chunk, color, k, 1).wait_send()
        start = starts[chunk][color][k + 1]
        block = math.gcd(part, 128)
        target = full if k + 1 == len(plans[chunk][color]) else grads

        def add(i, _):
            here = aligned(start + i * block, block)
            value = grads[color, here, :]
            for d in range(1, group):
                at = pl.multiple_of(offset + (d - 1) * part + i * block, 16)
                value += landed[color, pl.ds(at, block), :]
            target[color, here, :] = value
            return 0

        lax.fori_loop(0, part // block, add, 0)

    def gather_copy(chunk, color, k, d):
        axis, low, group, _split, _rows, part, _offset = plans[chunk][color][k]
        here = full.at[color, aligned(starts[chunk][color][k + 1], part)]
        slot = 2 * len(plans[chunk][color]) - 1 - k
        return sum_copy(here, here, chunk, color, slot, d, peer_of(axis, low, group, d)[1])

    def gather_arrival(chunk, color, k):
        axis, low, group, _split, _rows, part, _offset = plans[chunk][color][k]
        slot = 2 * len(plans[chunk][color]) - 1 - k
        for d in range(1, group):
            mine, to = peer_of(axis, low, group, d)
            source = lax.rem(mine - d + group, group)
            here = full.at[color, aligned(starts[chunk][color][k] + source * part, part)]
            sum_copy(here, here, chunk, color, slot, d, to).wait_recv()

    def sum_step(chunk, color, k):
        plan = plans[chunk][color]
        K = len(plan)
        if 1 <= k <= K:
            scatter_add(chunk, color, k - 1)
        elif K < k <= 2 * K and plan[2 * K - k][3]:
            gather_arrival(chunk, color, 2 * K - k)
        if k < K:
            for d in range(1, plan[k][2]):
                scatter_copy(chunk, color, k, d).start()
        elif k < 2 * K and plan[2 * K - 1 - k][3]:
            for d in range(1, plan[2 * K - 1 - k][2]):
                gather_copy(chunk, color, 2 * K - 1 - k, d).start()

    def full_copy(chunk, color):
        base, rows = CHUNKS[chunk]
        here = pl.ds(base, rows)
        return pltpu.make_async_copy(
            full.at[color, here], full_hbm.at[color, here], full_sem.at[chunk, color]
        )

    done = {}

    def sums(steps):
        for chunk, color, k in steps:
            last = 2 * len(plans[chunk][color])
            at = done.get((chunk, color), 0)
            while at <= min(k, last):
                sum_step(chunk, color, at)
                at += 1
                if at > last:
                    full_copy(chunk, color).start()
            done[chunk, color] = at

    def sums_rest():
        while True:
            left = [
                (chunk, color, done.get((chunk, color), 0))
                for chunk in range(len(CHUNKS))
                for color in range(2)
                if done.get((chunk, color), 0) <= 2 * len(plans[chunk][color])
            ]
            if not left:
                return
            sums(left)

    def sum_drain(chunk):
        for color in range(2):
            for k, stage in enumerate(plans[chunk][color]):
                for d in range(1, stage[2]):
                    if stage[3]:
                        scatter_copy(chunk, color, k, d).wait_send()
                        gather_copy(chunk, color, k, d).wait_send()

    def small_copy(b):
        axis, low = partners[b]
        return pltpu.make_async_remote_copy(
            src_ref=small_s,
            dst_ref=small_r.at[b],
            send_sem=small_send.at[b],
            recv_sem=small_recv.at[b],
            device_id=peer_of(axis, low, 2, 1)[1],
            device_id_type=MESH,
        )

    def small_step(b):
        if 1 <= b <= len(partners):
            small_copy(b - 1).wait()
            small_s[...] += small_r[b - 1]
        if b < len(partners):
            small_copy(b).start()

    def keep(base, value):
        low = value.astype(BF)
        rows = pl.ds(base, value.shape[0])
        grads[0, rows, :] = low[:, :LANES]
        grads[1, rows, :] = low[:, LANES:]

    def info_copy(slot, to):
        return send(info_own, info_in.at[slot], info_send.at[slot], info_recv.at[slot], to)

    def halo_copy(which, to):
        src, dst = ((k_s, hk_s), (v_s, hv_s))[which]
        tail = pl.ds(T - HALO, HALO)
        return send(
            src.at[:, tail, :], dst.at[:, tail, :], halo_send.at[which], halo_recv.at[which], to
        )

    for slot, step in enumerate((1, 2, -1)):
        inside = (sq + step >= 0) & (sq + step < n)
        came = (sq - step >= 0) & (sq - step < n)

        @pl.when(inside)
        def _():
            info_copy(slot, sq + step).start()

        @pl.when(jnp.logical_not(came))
        def _():
            info_in[slot, 0] = jnp.full((8, T), -1.0, F32)
            info_in[slot, 1] = jnp.zeros((8, T), F32)

    def half(which, c):
        return pl.ds(which * HU + c, 1)

    def chain_copy(way, stage, c):
        step = 1 - 2 * way
        here = pl.ds(c, 1)
        src, dst, to = (
            (pay_s.at[way, half(1 - par, c)], m1_r.at[way, here], partner),
            (pass_s.at[way, here], carry_r.at[way, here], sq + 2 * step),
            (give_s.at[way, here], in_s.at[way, half(par, c)], partner),
        )[stage]
        return send(src, dst, chain_send.at[way, stage, c], chain_recv.at[way, stage, c], to)

    def chain_arrival(way, stage, c):
        here = pl.ds(c, 1)
        dst = (m1_r.at[way, here], carry_r.at[way, here], in_s.at[way, half(1 - par, c)])[stage]
        return send(dst, dst, chain_send.at[way, stage, c], chain_recv.at[way, stage, c], partner)

    def has_next(way):
        return (z + 1 < nz) if way == 0 else (z > 0)

    def has_before(way):
        return (z > 0) if way == 0 else (z + 1 < nz)

    def marks(r):
        own = info_own[0, r : r + 1, :]
        before, before_two, after = (info_in[s, 0, r : r + 1, :] for s in range(3))
        first = par == 0
        last_a = jnp.where(first, own, before)
        last_b = jnp.where(first, after, own)
        last_z = jnp.where(first, before, before_two)
        inner = (last_a == last_b).astype(F32)
        enter = (last_z == last_a).astype(F32)
        through = (last_z == last_b).astype(F32)
        return inner, enter, through

    def chain_begin(way):
        for c in range(HU):
            chain_copy(way, 0, c).start()

        @pl.when(jnp.logical_not(has_before(way)))
        def _():
            carry_r[way] = jnp.zeros((HU, PAY, T), BF)

    def chain_pair(way):
        second = par == (1 - way)
        for c in range(HU):
            chain_arrival(way, 0, c).wait_recv()
            inner, enter, _through = marks(c // 2)
            weight = inner if way == 0 else enter
            one = jnp.ones_like(weight)
            mine = jnp.where(second, one, weight)
            other = jnp.where(second, weight, one)
            own = pay_s[way, par * HU + c].astype(F32)
            got = m1_r[way, c].astype(F32)
            sum_s[c] = mine * own + other * got

    def chain_pass(way):
        second = par == (1 - way)
        for c in range(HU):

            @pl.when(has_before(way))
            def _():
                chain_arrival(way, 1, c).wait_recv()

            inner, enter, through = marks(c // 2)
            weight = enter if way == 0 else inner
            carry = carry_r[way, c].astype(F32)
            pass_s[way, c] = (sum_s[c] + through * carry).astype(BF)

            @pl.when(has_next(way))
            def _():
                chain_copy(way, 1, c).start()

            own = pay_s[way, par * HU + c].astype(F32)
            got = m1_r[way, c].astype(F32)
            later = jnp.where(second, got, own) + weight * carry
            in_s[way, par * HU + c] = jnp.where(second, later, carry).astype(BF)
            give_s[way, c] = jnp.where(second, carry, later).astype(BF)
            chain_copy(way, 2, c).start()

    def chain_finish(way):
        for c in range(HU):
            chain_arrival(way, 2, c).wait_recv()

    def chain_drain(way):
        for c in range(HU):
            chain_copy(way, 0, c).wait_send()

            @pl.when(has_next(way))
            def _():
                chain_copy(way, 1, c).wait_send()

            chain_copy(way, 2, c).wait_send()

    chain_begin(0)

    @pl.when(sq + 1 < n)
    def _():
        for which in range(2):
            halo_copy(which, sq + 1).start()

    project(6, w_query, q_s)
    loads[7].wait()
    loads[8].wait()
    for a in range(2):
        for hp in range(PAIRS):
            sides = [
                jnp.broadcast_to(blend[a : a + 1, 2 * hp + side : 2 * hp + side + 1], (1, T))
                for side in range(2)
            ]
            weight_s[a * PAIRS + hp : a * PAIRS + hp + 1, :] = jnp.where(lane_low(1), *sides)
    ones_pair = two_blocks(jnp.ones((T, T), BF))

    def far_local(u, _):
        r = unit_row(u)
        queries = q_s[u].astype(F32)
        values = two_blocks(v_s[u])
        mask = far_mask[r]
        mask = jnp.concatenate([mask, mask], 1)
        for a, (feature, _slope) in enumerate(FEATURES):
            fq = feature(queries).astype(BF)
            fq_s[a, u] = fq
            kernel = (nt(fq, two_blocks(fk_s[a, u])) * mask).astype(BF)
            kk_s[a, u] = kernel
            far_s[a, u] = nn(kernel, values)
            den_s[a, u] = nn(kernel, ones_pair)
        return 0

    lax.fori_loop(0, U, far_local, 0, unroll=4)

    for slot, step in enumerate((1, 2, -1)):
        came = (sq - step >= 0) & (sq - step < n)

        @pl.when(came)
        def _():
            info_copy(slot, sq).wait_recv()

    @pl.when(sq > 0)
    def _():
        for which in range(2):
            halo_copy(which, sq).wait_recv()

    i_low = lax.broadcasted_iota(jnp.int32, (HALO, T), 0)
    j_low = lax.broadcasted_iota(jnp.int32, (HALO, T), 1)
    for r in range(R):
        seg_i = use_mask[r]
        marks_before = info_in[0, 1, r : r + 1, :]
        reach = j_low >= T - BAND + i_low
        halo_mask[r] = (reach & (seg_i[:HALO] + 1.0 == marks_before)).astype(F32)
        use_mask[r] = (seg_i == info_in[0, 0, r : r + 1, :]).astype(F32)

    chain_pair(0)

    def near_local(u, _):
        r = unit_row(u)
        queries = q_s[u]
        scores = nt(queries, two_blocks(k_s[u])) * SCALE
        scores_halo = nt(queries[:HALO], two_blocks(hk_s[u])) * SCALE
        open_near = near_mask[r] > 0
        open_halo = halo_mask[r] > 0
        for side in range(2):
            lanes = slice(side * T, (side + 1) * T)
            s = jnp.where(open_near, scores[:, lanes], NEGATIVE)
            sh = jnp.where(open_halo, scores_halo[:, lanes], NEGATIVE)
            peak = jnp.max(s, -1, keepdims=True)
            peak_halo = jnp.maximum(peak[:HALO], jnp.max(sh, -1, keepdims=True))
            peak = jnp.concatenate([peak_halo, peak[HALO:]], 0)
            e = jnp.exp(s - peak)
            eh = jnp.exp(sh - peak_halo)
            norm = jnp.sum(e, -1, keepdims=True)
            norm_halo = norm[:HALO] + jnp.sum(eh, -1, keepdims=True)
            inverse = 1.0 / jnp.concatenate([norm_halo, norm[HALO:]], 0)
            p_s[u, :, lanes] = e * inverse
            ph_s[u, :, lanes] = eh * inverse[:HALO]
        near_s[u] = nn(p_s[u].astype(BF), two_blocks(v_s[u]))
        near_s[u, :HALO, :] += nn(ph_s[u].astype(BF), two_blocks(hv_s[u]))
        return 0

    entry = z * PARTS // nz
    for part in range(PARTS):

        @pl.when(entry == part)
        def _():
            chain_pass(0)

        lax.fori_loop(part * U // PARTS, (part + 1) * U // PARTS, near_local, 0, unroll=3)
    chain_finish(0)

    def blend_lanes(a, u):
        return weight_s[pl.ds(a * PAIRS + unit_pair(u), 1), :]

    def far_finish(u, _):
        r = unit_row(u)
        hp = unit_pair(u)
        use = use_mask[r]
        blended = near_s[u]
        for a in range(2):
            fq = fq_s[a, u]
            state = two_blocks(in_s[0, u, a * E : (a + 1) * E, :])
            norm = in_s[0, u, 2 * E + 8 * a : 2 * E + 8 * a + 1, :].astype(F32)
            numer = far_s[a, u] + use * nn(fq, state)
            weighted = (fq.astype(F32) * norm).astype(BF)
            denom = den_s[a, u] + use * nn(weighted, ones_block)
            far = numer / denom
            far_s[a, u] = far
            den_s[a, u] = denom
            blended = blended + blend_lanes(a, u) * far
        rows = pl.ds(pl.multiple_of(r * T, T), T)
        lanes = pl.ds(pl.multiple_of(hp * T, T), T)
        mixed[rows, lanes] = blended.astype(BF)
        return 0

    lax.fori_loop(0, U, far_finish, 0, unroll=4)

    loads[9].wait()
    middle[...] = tok[...].astype(F32) + nn(mixed[...], w_out[...])
    for r in range(R):
        rows = pl.ds(r * T, T)
        mid = middle[rows, :]
        inverse = lax.rsqrt(jnp.mean(mid * mid, -1, keepdims=True) + EPSILON)
        normed_two[rows, :] = (mid * inverse * gain_two[...]).astype(BF)
    total[...] = jnp.zeros_like(total)
    back_two[...] = jnp.zeros_like(back_two)
    for i in (10, 11, 12):
        loads[i].wait()

    def feed(t, _):
        at = pl.multiple_of(t * D, D)
        cols = pl.ds(at, D)
        up = nn(normed_two[...], w_up[:, cols])
        square = up * up
        tangent = jnp.tanh(GELU_A * (up + GELU_B * square * up))
        act = (0.5 * up * (1.0 + tangent)).astype(BF)
        slope = 0.5 * (1.0 + tangent) + 0.5 * up * (1.0 - tangent * tangent) * GELU_A * (
            1.0 + 3.0 * GELU_B * square
        )
        total[...] += nn(act, w_down[cols, :])
        keep(pl.multiple_of(row_down(t), D), tn(act, cot[...]))
        d_up = (nt(cot[...], w_down[cols, :]) * slope).astype(BF)
        keep(pl.multiple_of(row_up(t), D), tn(normed_two[...], d_up))
        back_two[...] += nt(d_up, w_up[:, cols])
        return 0

    lax.fori_loop(0, TILES // 2, feed, 0, unroll=2)
    sums(ORDER["down"])
    lax.fori_loop(TILES // 2, TILES, feed, 0, unroll=2)
    sums(ORDER["up"])
    out[...] = (middle[...] + total[...]).astype(BF)

    gain_grad_two = jnp.zeros((1, D), F32)
    for r in range(R):
        rows = pl.ds(r * T, T)
        mid = middle[rows, :]
        inverse = lax.rsqrt(jnp.mean(mid * mid, -1, keepdims=True) + EPSILON)
        d_n = back_two[rows, :]
        gain_grad_two += jnp.sum(d_n * mid * inverse, 0, keepdims=True)
        scaled = d_n * gain_two[...]
        d_mid = (
            cot[rows, :].astype(F32)
            + inverse * scaled
            - mid * (inverse * inverse * inverse) * jnp.mean(mid * scaled, -1, keepdims=True)
        )
        total[rows, :] = d_mid
        normed_two[rows, :] = d_mid.astype(BF)
    d_branch = normed_two[...]
    keep(ROW_OUT, tn(mixed[...], d_branch))
    d_blended = nt(d_branch, w_out[...]).astype(BF)
    for r in range(R):
        for hp in range(PAIRS):
            db_s[unit_of(r, hp)] = d_blended[r * T : (r + 1) * T, hp * T : (hp + 1) * T]
    sums(ORDER["branch"])

    gb_s[...] = jnp.zeros_like(gb_s)

    def far_prepare(u, _):
        r = unit_row(u)
        hp = unit_pair(u)
        use = use_mask[r]
        use_low = use.astype(BF)
        d_out = db_s[u].astype(F32)
        norms = []
        for a in range(2):
            far = far_s[a, u]
            inverse = 1.0 / den_s[a, u]
            product = d_out * far
            row = a * PAIRS + hp
            gb_s[pl.ds(row, 1), :] += jnp.sum(product, 0, keepdims=True)
            weight = blend_lanes(a, u)
            product = product * weight
            high = product.astype(BF)
            rest = (product - high.astype(F32)).astype(BF)
            dden = -(nn(high, ones_block) + nn(rest, ones_block)) * inverse
            dden_s[a, u] = dden
            dnum = (weight * d_out * inverse).astype(BF)
            low_s[a, u] = dnum
            used = fq_s[a, u] * use_low
            pay_s[1, u, a * E : (a + 1) * E, :] = pick(tn(used, dnum)).astype(BF)
            norm = jnp.sum(used.astype(F32) * dden, 0, keepdims=True)
            norms.append(jnp.broadcast_to(norm, (8, T)))
        pay_s[1, u, 2 * E : PAY, :] = jnp.concatenate(norms, 0).astype(BF)
        return 0

    lax.fori_loop(0, U, far_prepare, 0, unroll=4)
    chain_begin(1)

    def near_back(u, _):
        keys = two_blocks(k_s[u])
        halo_keys = two_blocks(hk_s[u])
        queries = q_s[u]
        d_out = db_s[u]
        dp = nt(d_out, two_blocks(v_s[u]))
        dp_halo = nt(d_out[:HALO], two_blocks(hv_s[u]))
        p = p_s[u]
        p_halo = ph_s[u]
        ds = []
        ds_halo = []
        for side in range(2):
            lanes = slice(side * T, (side + 1) * T)
            ps, phs = p[:, lanes], p_halo[:, lanes]
            delta = jnp.sum(ps * dp[:, lanes], -1, keepdims=True)
            delta_halo = delta[:HALO] + jnp.sum(phs * dp_halo[:, lanes], -1, keepdims=True)
            delta = jnp.concatenate([delta_halo, delta[HALO:]], 0)
            ds.append(ps * (dp[:, lanes] - delta))
            ds_halo.append(phs * (dp_halo[:, lanes] - delta_halo))
        ds = jnp.concatenate(ds, 1).astype(BF)
        ds_halo = jnp.concatenate(ds_halo, 1).astype(BF)
        near_s[u] = nn(ds, keys) * SCALE
        near_s[u, :HALO, :] += nn(ds_halo, halo_keys) * SCALE
        dk_s[u] = pick(tn(ds, queries)) * SCALE
        dv_s[u] = pick(tn(p.astype(BF), d_out))
        hdk_s[u] = (pick(tn(ds_halo, queries[:HALO])) * SCALE)[T - HALO :].astype(BF)
        hdv_s[u] = pick(tn(p_halo.astype(BF), d_out[:HALO]))[T - HALO :].astype(BF)
        return 0

    sums(ORDER["prepare"])
    lax.fori_loop(0, HU, near_back, 0, unroll=3)
    sums(ORDER["near_a"])
    lax.fori_loop(HU, U, near_back, 0, unroll=3)
    sums(ORDER["near_b"])

    def halo_back(which, to):
        src, dst = ((hdk_s, hdk_r), (hdv_s, hdv_r))[which]
        return send(src, dst, halo_send.at[2 + which], halo_recv.at[2 + which], to)

    @pl.when(sq > 0)
    def _():
        for which in range(2):
            halo_back(which, sq - 1).start()

    chain_pair(1)
    sums(ORDER["pair"])

    def far_back(u, _):
        r = unit_row(u)
        values = two_blocks(v_s[u])
        mask = far_mask[r]
        mask = jnp.concatenate([mask, mask], 1)
        use = use_mask[r]
        queries = q_s[u].astype(F32)
        keys = k_s[u].astype(F32)
        dq = near_s[u]
        dk = dk_s[u]
        dv = dv_s[u]
        for a, (_feature, slope) in enumerate(FEATURES):
            dnum = low_s[a, u]
            dden = dden_s[a, u]
            fq = fq_s[a, u]
            fk = two_blocks(fk_s[a, u])
            added = jnp.concatenate(
                [
                    jnp.broadcast_to(dden[:, 0:1], (T, T)),
                    jnp.broadcast_to(dden[:, E : E + 1], (T, T)),
                ],
                1,
            )
            d_kernel = ((nt(dnum, values) + added) * mask).astype(BF)
            dv += pick(tn(kk_s[a, u], dnum))
            state = two_blocks(in_s[0, u, a * E : (a + 1) * E, :])
            norm = in_s[0, u, 2 * E + 8 * a : 2 * E + 8 * a + 1, :].astype(F32)
            dfq = nn(d_kernel, fk) + use * (nt(dnum, state) + dden * norm)
            dq += dfq * slope(queries)
            dk += pick(tn(d_kernel, fq)) * slope(keys)
        near_s[u] = dq
        dk_s[u] = dk
        dv_s[u] = dv
        return 0

    turn = (nz - 1 - z) * PARTS // nz
    for part in range(PARTS):

        @pl.when(turn == part)
        def _():
            chain_pass(1)

        lax.fori_loop(part * U // PARTS, (part + 1) * U // PARTS, far_back, 0, unroll=3)
        sums(ORDER["far_%d" % part])

    for u in range(U):
        r, hp = (u % (2 * R)) // 2, (u // (2 * R)) * 2 + u % 2
        wide_s[0, r * T : (r + 1) * T, hp * T : (hp + 1) * T] = near_s[u].astype(BF)
    keep(ROW_Q, tn(normed[...], wide_s[0]))
    sums(ORDER["query"])
    back_two[...] = nt(wide_s[0], w_query[...])

    @pl.when(sq + 1 < n)
    def _():
        for which in range(2):
            halo_back(which, sq).wait_recv()

    chain_finish(1)
    sums(ORDER["state"])

    def far_close(u, _):
        r = unit_row(u)
        hp = unit_pair(u)
        tail = tail_mask[r]
        keys = k_s[u].astype(F32)
        values = v_s[u]
        dk = dk_s[u]
        dv = dv_s[u]
        for a, (_feature, slope) in enumerate(FEATURES):
            state = two_blocks(in_s[1, u, a * E : (a + 1) * E, :])
            norm = in_s[1, u, 2 * E + 8 * a : 2 * E + 8 * a + 1, :].astype(F32)
            dk += tail * (nt(values, state) + norm) * slope(keys)
            dv += tail * nn(fk_s[a, u], state)
        zero = jnp.zeros((T - HALO, T), F32)
        dk += jnp.concatenate([zero, hdk_r[u].astype(F32)], 0)
        dv += jnp.concatenate([zero, hdv_r[u].astype(F32)], 0)
        rows = pl.ds(pl.multiple_of(r * T, T), T)
        lanes = pl.ds(pl.multiple_of(hp * T, T), T)
        wide_s[1, rows, lanes] = dk.astype(BF)
        wide_s[2, rows, lanes] = dv.astype(BF)
        return 0

    lax.fori_loop(0, U, far_close, 0, unroll=4)
    sums(ORDER["close"])
    for i in (1, 2):
        keep(ROW_Q + i * D, tn(normed[...], wide_s[i]))
    sums(ORDER["key"])
    for i, weight in ((1, w_key), (2, w_value)):
        back_two[...] += nt(wide_s[i], weight[...])
    gain_grad_one = jnp.zeros((1, D), F32)
    for r in range(R):
        rows = pl.ds(r * T, T)
        x = tok[rows, :].astype(F32)
        inverse = lax.rsqrt(jnp.mean(x * x, -1, keepdims=True) + EPSILON)
        d_n = back_two[rows, :]
        gain_grad_one += jnp.sum(d_n * x * inverse, 0, keepdims=True)
        scaled = d_n * gain_one[...]
        d_x = (
            total[rows, :]
            + inverse * scaled
            - x * (inverse * inverse * inverse) * jnp.mean(x * scaled, -1, keepdims=True)
        )
        grad_tok[rows, :] = d_x.astype(BF)
    blends = [
        jnp.concatenate([gb_s[a * PAIRS + hp : a * PAIRS + hp + 1, :] for hp in range(PAIRS)], 1)
        for a in range(2)
    ]
    small_s[...] = jnp.concatenate(
        [gain_grad_one, gain_grad_two] + blends + [jnp.zeros((SMALL - 4, D), F32)], 0
    )
    small_step(0)
    sums(ORDER["back"])
    for i, step in enumerate(ORDER["tail"]):
        sums((step,))
        if i % 2 and i // 2 < len(partners):
            small_step(i // 2 + 1)
    for b in range(len(ORDER["tail"]) // 2, len(partners)):
        small_step(b + 1)
    sums_rest()
    small_out[...] = small_s[...]

    for slot, step in enumerate((1, 2, -1)):

        @pl.when((sq + step >= 0) & (sq + step < n))
        def _():
            info_copy(slot, sq + step).wait_send()

    @pl.when(sq + 1 < n)
    def _():
        for which in range(2):
            halo_copy(which, sq + 1).wait_send()

    @pl.when(sq > 0)
    def _():
        for which in range(2):
            halo_back(which, sq - 1).wait_send()

    chain_drain(0)
    chain_drain(1)
    for c in range(len(CHUNKS)):
        sum_drain(c)
        for color in range(2):
            full_copy(c, color).wait()


def widen_kernel(
    grads,
    small,
    out_in,
    back_in,
    g_one,
    g_two,
    g_blend,
    g_query,
    g_key,
    g_value,
    g_out,
    g_up,
    g_down,
    out,
    back,
    held,
    wide,
    in_sem,
    out_sem,
    same_sem,
):
    blocks = ROWS_ALL // D
    targets = []
    for t in (0, 2):
        targets += [g_down.at[pl.ds((t + i) * D, D)] for i in range(2)]
        targets += [g_up.at[:, pl.ds((t + i) * D, D)] for i in range(2)]
    targets += [g_out, g_query, g_key, g_value]
    reads = [
        pltpu.make_async_copy(grads.at[:, pl.ds(i * D, D)], held.at[i], in_sem.at[i])
        for i in range(blocks)
    ]
    for read in reads:
        read.start()
    writes = [
        pltpu.make_async_copy(wide.at[i], targets[i], out_sem.at[i]) for i in range(blocks)
    ]
    same = [
        pltpu.make_async_copy(out_in, out, same_sem.at[0]),
        pltpu.make_async_copy(back_in, back, same_sem.at[1]),
    ]
    for copy in same:
        copy.start()
    g_one[...] = small[0]
    g_two[...] = small[1]
    for a in range(2):
        row = small[2 + a : 3 + a, :]
        lane = lax.broadcasted_iota(jnp.int32, (H, D), 1) // E
        head = lax.broadcasted_iota(jnp.int32, (H, D), 0)
        per_head = jnp.sum(jnp.where(lane == head, row, 0.0), -1, keepdims=True)
        g_blend[a : a + 1, :] = jnp.broadcast_to(per_head, (H, H)).T[:1]
    for i in range(blocks):
        reads[i].wait()
        wide[i, :, :LANES] = held[i, 0].astype(F32)
        wide[i, :, LANES:] = held[i, 1].astype(F32)
        writes[i].start()
    for copy in writes + same:
        copy.wait()


def solution(mesh):
    n = mesh.shape["seq"]
    n_rows = mesh.shape["rows"]

    def shards(
        tokens,
        segment_ids,
        padding,
        gain_one,
        w_query,
        w_key,
        w_value,
        blend,
        w_out,
        gain_two,
        w_up,
        w_down,
        cotangent,
    ):
        R, tok_count, _ = tokens.shape
        M = R * tok_count
        U = R * PAIRS
        HU = U // 2
        vmem = pl.BlockSpec(memory_space=pltpu.VMEM)
        anyspace = pl.BlockSpec(memory_space=pl.ANY)
        V = pltpu.VMEM
        unit_f = V((U, T, T), F32)
        unit_b = V((U, T, T), BF)
        two_f = V((2, U, T, T), F32)
        two_b = V((2, U, T, T), BF)
        wide_f = V((M, D), F32)
        wide_b = V((M, D), BF)
        halo_b = V((U, HALO, T), BF)
        dma = pltpu.SemaphoreType.DMA
        plans, landed_rows = sum_plans(n_rows, n)
        stages = 2 * max(len(plan) for both in plans for plan in both)
        count = bits(n) + bits(n_rows)
        scratch = [
            V((2, ROWS_ALL, LANES), BF),
            V((2, ROWS_ALL, LANES), BF),
            V((2, landed_rows, LANES), BF),
            V((SMALL, D), F32),
            V((count, SMALL, D), F32),
            wide_b,
            V((R, T), jnp.int32),
            V((R, T), jnp.int32),
            V((1, D), F32),
            V((1, D), F32),
            V((2, H), F32),
            V((D, D), BF),
            V((D, D), BF),
            V((D, D), BF),
            V((D, D), BF),
            V((D, FF), BF),
            V((FF, D), BF),
            wide_b,
            V((2 * PAIRS, T), F32),
            wide_b,
            wide_b,
            wide_b,
            wide_f,
            wide_f,
            wide_f,
            unit_b,
            unit_b,
            unit_b,
            unit_b,
            unit_b,
            two_b,
            two_b,
            V((2, U, T, 2 * T), BF),
            V((U, T, 2 * T), F32),
            V((U, HALO, 2 * T), F32),
            unit_f,
            two_f,
            two_f,
            unit_b,
            two_b,
            two_f,
            unit_f,
            unit_f,
            halo_b,
            halo_b,
            halo_b,
            halo_b,
            V((3, M, D), BF),
            V((R, T, T), F32),
            V((R, T, T), F32),
            V((R, T, T), F32),
            V((R, T, T), F32),
            V((R, HALO, T), F32),
            V((2, 8, T), F32),
            V((3, 2, 8, T), F32),
            V((2 * PAIRS, T), F32),
            V((2, U, PAY, T), BF),
            V((2, HU, PAY, T), BF),
            V((HU, PAY, T), F32),
            V((2, HU, PAY, T), BF),
            V((2, HU, PAY, T), BF),
            V((2, U, PAY, T), BF),
            V((2, HU, PAY, T), BF),
            dma((13,)),
            dma((3,)),
            dma((3,)),
            dma((4,)),
            dma((4,)),
            dma((2, 3, HU)),
            dma((2, 3, HU)),
            dma((len(CHUNKS), 2, stages, 3)),
            dma((len(CHUNKS), 2, stages, 3)),
            dma((count,)),
            dma((count,)),
            dma((len(CHUNKS), 2)),
        ]
        out, grad_tok, small, grads = pl.pallas_call(
            functools.partial(layer_kernel, n, n_rows, R),
            out_shape=(
                jax.ShapeDtypeStruct((M, D), BF),
                jax.ShapeDtypeStruct((M, D), BF),
                jax.ShapeDtypeStruct((SMALL, D), F32),
                jax.ShapeDtypeStruct((2, ROWS_ALL, LANES), BF),
            ),
            in_specs=[pl.BlockSpec(memory_space=pltpu.HBM)] * 13,
            out_specs=(vmem, vmem, vmem, anyspace),
            scratch_shapes=scratch,
            compiler_params=pltpu.CompilerParams(
                collective_id=0, has_side_effects=True, vmem_limit_bytes=LAYER_VMEM
            ),
            name="layer",
        )(
            tokens.reshape(M, D),
            segment_ids,
            padding,
            gain_one.reshape(1, D),
            gain_two.reshape(1, D),
            blend,
            w_query,
            w_key,
            w_value,
            w_out,
            w_up,
            w_down,
            cotangent.reshape(M, D),
        )
        square = jax.ShapeDtypeStruct((D, D), F32)
        token = jax.ShapeDtypeStruct((M, D), BF)
        blocks = ROWS_ALL // D
        g_one, g_two, g_blend, g_query, g_key, g_value, g_out, g_up, g_down, out, grad_tok = (
          pl.pallas_call(
            widen_kernel,
            out_shape=(
                jax.ShapeDtypeStruct((D,), F32),
                jax.ShapeDtypeStruct((D,), F32),
                jax.ShapeDtypeStruct((2, H), F32),
                square,
                square,
                square,
                square,
                jax.ShapeDtypeStruct((D, FF), F32),
                jax.ShapeDtypeStruct((FF, D), F32),
                token,
                token,
            ),
            in_specs=[anyspace, vmem, vmem, vmem],
            out_specs=(vmem,) * 3 + (anyspace,) * 8,
            scratch_shapes=[
                V((blocks, 2, D, LANES), BF),
                V((blocks, D, D), F32),
                dma((blocks,)),
                dma((blocks,)),
                dma((2,)),
            ],
            compiler_params=pltpu.CompilerParams(vmem_limit_bytes=WIDEN_VMEM),
            name="widen",
        )(grads, small, out, grad_tok))
        return (
            out.reshape(R, tok_count, D),
            grad_tok.reshape(R, tok_count, D),
            g_one,
            g_query,
            g_key,
            g_value,
            g_blend,
            g_out,
            g_two,
            g_up,
            g_down,
        )

    row, whole = P("rows", "seq", None), P()
    return jax.shard_map(
        shards,
        mesh=mesh,
        in_specs=(row, P("rows", "seq"), P("rows", "seq")) + (whole,) * 9 + (row,),
        out_specs=(row, row) + (whole,) * 9,
        check_vma=False,
    )
```

```python
import functools
import math

import jax
import jax.numpy as jnp
from jax import lax
from jax.experimental import pallas as pl
from jax.experimental.pallas import tpu as pltpu
from jax.sharding import PartitionSpec as P

MESH = pl.DeviceIdType.MESH
F32 = jnp.float32
BF = jnp.bfloat16
D = 512
H = 8
E = 64
FF = 2048
BAND = 30
T = 128
PAIRS = 4
PAY = 144
HALO = 32
EPSILON = 1e-06
NEGATIVE = -1e30
SCALE = 1.0 / math.sqrt(E)
GELU_A = math.sqrt(2.0 / math.pi)
GELU_B = 0.044715
TILES = FF // D
ROW_OUT = 2 * FF
ROW_Q = ROW_OUT + D
ROWS_ALL = ROW_Q + 3 * D
SMALL = 8
LANES = D // 2
CHUNKS = ((0, FF), (FF, FF), (ROW_OUT, 2 * D), (ROW_Q + D, 2 * D))
DIMS = (("cyxab", "caxyb"), ("cxyq", "cyxq"), ("cyxq", "cxyq"), ("cyxq", "cxyq"))
PARTS = 4
LAYER_VMEM = 60 * 1024 * 1024
WIDEN_VMEM = 60 * 1024 * 1024


ORDER = {
    "down": (
        (0, 0, 0), (0, 1, 0),
    ),
    "up": (),
    "branch": (),
    "prepare": (
        (1, 1, 0), (0, 1, 1), (1, 0, 0), (0, 0, 1),
    ),
    "near_a": (
        (1, 0, 1), (1, 1, 1),
    ),
    "near_b": (
        (0, 1, 2),
    ),
    "pair": (
        (0, 0, 2),
    ),
    "far_0": (),
    "far_1": (
        (0, 1, 3), (1, 0, 2), (0, 0, 3), (1, 1, 2), (0, 1, 4),
    ),
    "far_2": (),
    "far_3": (),
    "query": (
        (1, 0, 3),
    ),
    "state": (
        (0, 0, 4),
    ),
    "close": (
        (2, 1, 0), (2, 0, 0), (0, 1, 5),
    ),
    "key": (
        (2, 1, 1), (3, 0, 0), (1, 1, 3), (3, 1, 0), (2, 0, 1), (3, 1, 1),
        (1, 0, 4), (3, 0, 1), (2, 0, 2), (1, 1, 4), (2, 1, 2), (1, 0, 5),
        (3, 0, 2), (2, 0, 3), (2, 1, 3), (3, 1, 2), (0, 1, 6), (1, 1, 5),
        (0, 0, 5),
    ),
    "back": (
        (1, 0, 6), (2, 0, 4), (2, 1, 4), (0, 0, 6), (3, 0, 3), (1, 1, 6),
        (2, 0, 5), (0, 1, 7), (3, 1, 3), (2, 1, 5), (3, 0, 4), (0, 0, 7),
        (3, 1, 4), (1, 0, 7), (1, 1, 7), (2, 0, 6),
    ),
    "tail": (
        (0, 1, 8), (3, 0, 5), (3, 1, 5), (0, 0, 8), (2, 1, 6), (3, 0, 6),
        (3, 1, 6), (2, 1, 7), (0, 1, 9), (2, 0, 7), (0, 0, 9), (3, 1, 7),
        (1, 0, 8), (1, 1, 8), (3, 0, 7), (2, 0, 8), (2, 1, 8), (3, 1, 8),
        (3, 0, 8), (0, 0, 10), (0, 1, 10),
    ),
}


def row_down(t):
    return (t // 2) * FF + (t % 2) * D


def row_up(t):
    return row_down(t) + FF // 2


def nn(a, b):
    return lax.dot_general(a, b, (((1,), (0,)), ((), ())), preferred_element_type=F32)


def nt(a, b):
    return lax.dot_general(a, b, (((1,), (1,)), ((), ())), preferred_element_type=F32)


def tn(a, b):
    return lax.dot_general(a, b, (((0,), (0,)), ((), ())), preferred_element_type=F32)


def lane_low(rows):
    return lax.broadcasted_iota(jnp.int32, (rows, T), 1) < E


def low_high():
    low = lane_low(T).astype(F32)
    return low.astype(BF), (1.0 - low).astype(BF)


def two_blocks(x):
    low, high = low_high()
    rows = x.shape[0]
    return jnp.concatenate([x * low[:rows], x * high[:rows]], 0)


def pick(stacked):
    half = stacked.shape[0] // 2
    return jnp.where(lane_low(half), stacked[:half], stacked[half:])


def block_ones():
    i = lax.broadcasted_iota(jnp.int32, (T, T), 0) < E
    j = lax.broadcasted_iota(jnp.int32, (T, T), 1) < E
    return jnp.where(i == j, 1.0, 0.0).astype(BF)


def feature_one(t):
    return jnp.where(t > 0, t + 1.0, jnp.exp(jnp.minimum(t, 0.0)))


def slope_one(t):
    return jnp.where(t > 0, 1.0, jnp.exp(jnp.minimum(t, 0.0)))


def feature_two(t):
    return 1.0 + jnp.tanh(t)


def slope_two(t):
    tangent = jnp.tanh(t)
    return 1.0 - tangent * tangent


FEATURES = ((feature_one, slope_one), (feature_two, slope_two))


def bits(size):
    return size.bit_length() - 1


def sum_order(dims, n_rows, n_seq):
    rows = [("rows", 2**b, 2) for b in range(bits(n_rows))]
    seq = [("seq", 2**b, 2) for b in range(bits(n_seq))]
    near, far = seq[:-2], seq[-2:]
    found = {
        "c": rows[:1],
        "y": rows[1:],
        "x": near,
        "a": far[:1],
        "b": far[1:],
        "q": [("seq", far[0][1], 4)],
    }
    return [stage for dim in dims for stage in found[dim]]


def sum_plan(dims, n_rows, n_seq, rows, offset):
    plan = []
    for axis, low, group in sum_order(dims, n_rows, n_seq):
        steps = [(low, group)]
        if group == 4 and rows % 64:
            steps = [(low, 2), (2 * low, 2)]
        for low, group in steps:
            split = rows % (16 * group) == 0
            part = rows // group if split else rows
            plan.append((axis, low, group, split, rows, part, offset))
            offset += (group - 1) * part
            rows = part
    return plan, offset


def sum_plans(n_rows, n_seq):
    plans = []
    offset = [0, 0]
    for (_base, rows), dims in zip(CHUNKS, DIMS):
        both = []
        for color in range(2):
            plan, offset[color] = sum_plan(dims[color], n_rows, n_seq, rows, offset[color])
            both.append(plan)
        plans.append(both)
    return plans, max(offset)


def layer_kernel(
    n,
    n_rows,
    R,
    tok_hbm,
    seg_hbm,
    pad_hbm,
    gain_one_hbm,
    gain_two_hbm,
    blend_hbm,
    w_query_hbm,
    w_key_hbm,
    w_value_hbm,
    w_out_hbm,
    w_up_hbm,
    w_down_hbm,
    cot_hbm,
    out,
    grad_tok,
    small_out,
    full_hbm,
    grads,
    full,
    landed,
    small_s,
    small_r,
    tok,
    seg,
    pad,
    gain_one,
    gain_two,
    blend,
    w_query,
    w_key,
    w_value,
    w_out,
    w_up,
    w_down,
    cot,
    weight_s,
    normed,
    normed_two,
    mixed,
    middle,
    total,
    back_two,
    q_s,
    k_s,
    v_s,
    hk_s,
    hv_s,
    fq_s,
    fk_s,
    kk_s,
    p_s,
    ph_s,
    near_s,
    far_s,
    den_s,
    db_s,
    low_s,
    dden_s,
    dk_s,
    dv_s,
    hdk_s,
    hdv_s,
    hdk_r,
    hdv_r,
    wide_s,
    far_mask,
    near_mask,
    use_mask,
    tail_mask,
    halo_mask,
    info_own,
    info_in,
    gb_s,
    pay_s,
    m1_r,
    sum_s,
    carry_r,
    pass_s,
    in_s,
    give_s,
    w_sem,
    info_send,
    info_recv,
    halo_send,
    halo_recv,
    chain_send,
    chain_recv,
    sum_send,
    sum_recv,
    small_send,
    small_recv,
    full_sem,
):
    U = R * PAIRS
    HU = U // 2
    sq = lax.axis_index("seq")
    rw = lax.axis_index("rows")
    par = lax.rem(sq, 2)
    z = sq // 2
    nz = n // 2
    partner = sq + 1 - 2 * par

    def unit_row(u):
        return lax.rem(u, 2 * R) // 2

    def unit_pair(u):
        return (u // (2 * R)) * 2 + lax.rem(u, 2)

    def unit_of(r, hp):
        return (hp // 2) * 2 * R + r * 2 + hp % 2

    def send(src, dst, send_sem, recv_sem, to):
        return pltpu.make_async_remote_copy(
            src_ref=src,
            dst_ref=dst,
            send_sem=send_sem,
            recv_sem=recv_sem,
            device_id=(to, rw),
            device_id_type=MESH,
        )

    barrier = pltpu.get_barrier_semaphore()
    for step in (1, 2):

        @pl.when(sq >= step)
        def _():
            pl.semaphore_signal(barrier, inc=1, device_id=(sq - step, rw), device_id_type=MESH)

        @pl.when(sq + step < n)
        def _():
            pl.semaphore_signal(barrier, inc=1, device_id=(sq + step, rw), device_id_type=MESH)

    plans, _size = sum_plans(n_rows, n)
    partners = [("rows", 2**b) for b in range(bits(n_rows))]
    partners += [("seq", 2**b) for b in range(bits(n))]

    def peer_of(axis, low, group, step):
        own = rw if axis == "rows" else sq
        mine = lax.rem(own // low, group)
        other = own + (lax.rem(mine + step, group) - mine) * low
        return mine, ((sq, other) if axis == "rows" else (other, rw))

    groups = {(axis, low, 2) for axis, low in partners}
    for both in plans:
        for plan in both:
            groups |= {(axis, low, group) for axis, low, group, *_ in plan}
    greet = [(axis, low, group, d) for axis, low, group in sorted(groups) for d in range(1, group)]
    for axis, low, group, d in greet:
        pl.semaphore_signal(
            barrier, inc=1, device_id=peer_of(axis, low, group, d)[1], device_id_type=MESH
        )

    loads = [
        pltpu.make_async_copy(src, dst, w_sem.at[i])
        for i, (src, dst) in enumerate(
            (
                (tok_hbm, tok),
                (gain_one_hbm, gain_one),
                (w_key_hbm, w_key),
                (w_value_hbm, w_value),
                (seg_hbm, seg),
                (pad_hbm, pad),
                (w_query_hbm, w_query),
                (blend_hbm, blend),
                (gain_two_hbm, gain_two),
                (w_out_hbm, w_out),
                (w_up_hbm, w_up),
                (w_down_hbm, w_down),
                (cot_hbm, cot),
            )
        )
    ]
    for load in loads:
        load.start()
    loads[0].wait()
    loads[1].wait()

    for r in range(R):
        rows = pl.ds(r * T, T)
        x = tok[rows, :].astype(F32)
        inverse = lax.rsqrt(jnp.mean(x * x, -1, keepdims=True) + EPSILON)
        normed[rows, :] = (x * inverse * gain_one[...]).astype(BF)

    def project(load, weight, held):
        loads[load].wait()
        whole = nn(normed[...], weight[...]).astype(BF)
        for r in range(R):
            for hp in range(PAIRS):
                held[unit_of(r, hp)] = whole[r * T : (r + 1) * T, hp * T : (hp + 1) * T]

    project(2, w_key, k_s)
    project(3, w_value, v_s)
    loads[4].wait()
    loads[5].wait()

    i_pos = lax.broadcasted_iota(jnp.int32, (T, T), 0)
    j_pos = lax.broadcasted_iota(jnp.int32, (T, T), 1)
    info_own[...] = jnp.zeros_like(info_own)
    for r in range(R):
        seg_row = seg[r : r + 1, :].astype(F32)
        pad_row = pad[r : r + 1, :].astype(F32)
        seg_j = jnp.broadcast_to(seg_row, (T, T))
        seg_i = seg_j.T
        pad_i = jnp.broadcast_to(pad_row, (T, T)).T
        last = seg_i[T - 1 : T, :]
        tail_mask[r] = ((seg_i == last) & (pad_i == 1.0)).astype(F32)
        use_mask[r] = seg_i
        info_own[0, r : r + 1, :] = last
        info_own[1, r : r + 1, :] = jnp.where(pad_row == 1.0, seg_row + 1.0, 0.0)

    head = pl.ds(0, T - HALO)
    hk_s[:, head, :] = jnp.zeros((U, T - HALO, T), BF)
    hv_s[:, head, :] = jnp.zeros((U, T - HALO, T), BF)

    @pl.when(sq == 0)
    def _():
        tail = pl.ds(T - HALO, HALO)
        hk_s[:, tail, :] = jnp.zeros((U, HALO, T), BF)
        hv_s[:, tail, :] = jnp.zeros((U, HALO, T), BF)

    @pl.when(sq == n - 1)
    def _():
        hdk_r[...] = jnp.zeros((U, HALO, T), BF)
        hdv_r[...] = jnp.zeros((U, HALO, T), BF)

    ones_block = block_ones()

    def local_state(u, _):
        r = unit_row(u)
        tail = tail_mask[r].astype(BF)
        keys = k_s[u].astype(F32)
        values = v_s[u]
        norms = []
        for a, (feature, _slope) in enumerate(FEATURES):
            fk = feature(keys).astype(BF)
            fk_s[a, u] = fk
            weighted = fk * tail
            pay_s[0, u, a * E : (a + 1) * E, :] = pick(tn(weighted, values)).astype(BF)
            norm = jnp.sum(weighted.astype(F32), 0, keepdims=True)
            norms.append(jnp.broadcast_to(norm, (8, T)))
        pay_s[0, u, 2 * E : PAY, :] = jnp.concatenate(norms, 0).astype(BF)
        return 0

    def local_part(which):
        return lambda i, _: local_state(which * HU + i, 0)

    lax.fori_loop(0, HU, local_part(1 - par), 0, unroll=3)

    pl.semaphore_wait(barrier, jnp.minimum(sq, 2) + jnp.minimum(n - 1 - sq, 2) + len(greet))

    def starts_of(chunk, color):
        start = CHUNKS[chunk][0]
        found = [start]
        for axis, low, group, split, _rows, part, _offset in plans[chunk][color]:
            if split:
                start = start + peer_of(axis, low, group, 1)[0] * part
            found.append(start)
        return found

    starts = [[starts_of(c, color) for color in range(2)] for c in range(len(CHUNKS))]

    def aligned(start, size):
        return pl.ds(pl.multiple_of(start, 16), size)

    def sum_copy(src, dst, chunk, color, slot, d, to):
        return pltpu.make_async_remote_copy(
            src_ref=src,
            dst_ref=dst,
            send_sem=sum_send.at[chunk, color, slot, d - 1],
            recv_sem=sum_recv.at[chunk, color, slot, d - 1],
            device_id=to,
            device_id_type=MESH,
        )

    def scatter_copy(chunk, color, k, d):
        axis, low, group, split, _rows, part, offset = plans[chunk][color][k]
        mine, to = peer_of(axis, low, group, d)
        start = starts[chunk][color][k]
        if split:
            start = start + lax.rem(mine + d, group) * part
        src = grads.at[color, aligned(start, part)]
        dst = landed.at[color, pl.ds(offset + (d - 1) * part, part)]
        return sum_copy(src, dst, chunk, color, k, d, to)

    def scatter_add(chunk, color, k):
        axis, low, group, split, _rows, part, offset = plans[chunk][color][k]
        for d in range(1, group):
            scatter_copy(chunk, color, k, d).wait_recv()
        if not split:
            scatter_copy(chunk, color, k, 1).wait_send()
        start = starts[chunk][color][k + 1]
        block = math.gcd(part, 128)
        target = full if k + 1 == len(plans[chunk][color]) else grads

        def add(i, _):
            here = aligned(start + i * block, block)
            value = grads[color, here, :]
            for d in range(1, group):
                at = pl.multiple_of(offset + (d - 1) * part + i * block, 16)
                value += landed[color, pl.ds(at, block), :]
            target[color, here, :] = value
            return 0

        lax.fori_loop(0, part // block, add, 0)

    def gather_copy(chunk, color, k, d):
        axis, low, group, _split, _rows, part, _offset = plans[chunk][color][k]
        here = full.at[color, aligned(starts[chunk][color][k + 1], part)]
        slot = 2 * len(plans[chunk][color]) - 1 - k
        return sum_copy(here, here, chunk, color, slot, d, peer_of(axis, low, group, d)[1])

    def gather_arrival(chunk, color, k):
        axis, low, group, _split, _rows, part, _offset = plans[chunk][color][k]
        slot = 2 * len(plans[chunk][color]) - 1 - k
        for d in range(1, group):
            mine, to = peer_of(axis, low, group, d)
            source = lax.rem(mine - d + group, group)
            here = full.at[color, aligned(starts[chunk][color][k] + source * part, part)]
            sum_copy(here, here, chunk, color, slot, d, to).wait_recv()

    def sum_step(chunk, color, k):
        plan = plans[chunk][color]
        K = len(plan)
        if 1 <= k <= K:
            scatter_add(chunk, color, k - 1)
        elif K < k <= 2 * K and plan[2 * K - k][3]:
            gather_arrival(chunk, color, 2 * K - k)
        if k < K:
            for d in range(1, plan[k][2]):
                scatter_copy(chunk, color, k, d).start()
        elif k < 2 * K and plan[2 * K - 1 - k][3]:
            for d in range(1, plan[2 * K - 1 - k][2]):
                gather_copy(chunk, color, 2 * K - 1 - k, d).start()

    def full_copy(chunk, color):
        base, rows = CHUNKS[chunk]
        here = pl.ds(base, rows)
        return pltpu.make_async_copy(
            full.at[color, here], full_hbm.at[color, here], full_sem.at[chunk, color]
        )

    done = {}

    def sums(steps):
        for chunk, color, k in steps:
            last = 2 * len(plans[chunk][color])
            at = done.get((chunk, color), 0)
            while at <= min(k, last):
                sum_step(chunk, color, at)
                at += 1
                if at > last:
                    full_copy(chunk, color).start()
            done[chunk, color] = at

    def sums_rest():
        while True:
            left = [
                (chunk, color, done.get((chunk, color), 0))
                for chunk in range(len(CHUNKS))
                for color in range(2)
                if done.get((chunk, color), 0) <= 2 * len(plans[chunk][color])
            ]
            if not left:
                return
            sums(left)

    def sum_drain(chunk):
        for color in range(2):
            for k, stage in enumerate(plans[chunk][color]):
                for d in range(1, stage[2]):
                    if stage[3]:
                        scatter_copy(chunk, color, k, d).wait_send()
                        gather_copy(chunk, color, k, d).wait_send()

    def small_copy(b):
        axis, low = partners[b]
        return pltpu.make_async_remote_copy(
            src_ref=small_s,
            dst_ref=small_r.at[b],
            send_sem=small_send.at[b],
            recv_sem=small_recv.at[b],
            device_id=peer_of(axis, low, 2, 1)[1],
            device_id_type=MESH,
        )

    def small_step(b):
        if 1 <= b <= len(partners):
            small_copy(b - 1).wait()
            small_s[...] += small_r[b - 1]
        if b < len(partners):
            small_copy(b).start()

    def keep(base, value):
        low = value.astype(BF)
        rows = pl.ds(base, value.shape[0])
        grads[0, rows, :] = low[:, :LANES]
        grads[1, rows, :] = low[:, LANES:]

    def info_copy(slot, to):
        return send(info_own, info_in.at[slot], info_send.at[slot], info_recv.at[slot], to)

    def halo_copy(which, to):
        src, dst = ((k_s, hk_s), (v_s, hv_s))[which]
        tail = pl.ds(T - HALO, HALO)
        return send(
            src.at[:, tail, :], dst.at[:, tail, :], halo_send.at[which], halo_recv.at[which], to
        )

    for slot, step in enumerate((1, 2, -1)):
        inside = (sq + step >= 0) & (sq + step < n)
        came = (sq - step >= 0) & (sq - step < n)

        @pl.when(inside)
        def _():
            info_copy(slot, sq + step).start()

        @pl.when(jnp.logical_not(came))
        def _():
            info_in[slot, 0] = jnp.full((8, T), -1.0, F32)
            info_in[slot, 1] = jnp.zeros((8, T), F32)

    def half(which, c):
        return pl.ds(which * HU + c, 1)

    def chain_copy(way, stage, c):
        step = 1 - 2 * way
        here = pl.ds(c, 1)
        src, dst, to = (
            (pay_s.at[way, half(1 - par, c)], m1_r.at[way, here], partner),
            (pass_s.at[way, here], carry_r.at[way, here], sq + 2 * step),
            (give_s.at[way, here], in_s.at[way, half(par, c)], partner),
        )[stage]
        return send(src, dst, chain_send.at[way, stage, c], chain_recv.at[way, stage, c], to)

    def chain_arrival(way, stage, c):
        here = pl.ds(c, 1)
        dst = (m1_r.at[way, here], carry_r.at[way, here], in_s.at[way, half(1 - par, c)])[stage]
        return send(dst, dst, chain_send.at[way, stage, c], chain_recv.at[way, stage, c], partner)

    def has_next(way):
        return (z + 1 < nz) if way == 0 else (z > 0)

    def has_before(way):
        return (z > 0) if way == 0 else (z + 1 < nz)

    def marks(r):
        own = info_own[0, r : r + 1, :]
        before, before_two, after = (info_in[s, 0, r : r + 1, :] for s in range(3))
        first = par == 0
        last_a = jnp.where(first, own, before)
        last_b = jnp.where(first, after, own)
        last_z = jnp.where(first, before, before_two)
        inner = (last_a == last_b).astype(F32)
        enter = (last_z == last_a).astype(F32)
        through = (last_z == last_b).astype(F32)
        return inner, enter, through

    def chain_begin(way):
        for c in range(HU):
            chain_copy(way, 0, c).start()

        @pl.when(jnp.logical_not(has_before(way)))
        def _():
            carry_r[way] = jnp.zeros((HU, PAY, T), BF)

    def chain_pair(way):
        second = par == (1 - way)
        for c in range(HU):
            chain_arrival(way, 0, c).wait_recv()
            inner, enter, _through = marks(c // 2)
            weight = inner if way == 0 else enter
            one = jnp.ones_like(weight)
            mine = jnp.where(second, one, weight)
            other = jnp.where(second, weight, one)
            own = pay_s[way, par * HU + c].astype(F32)
            got = m1_r[way, c].astype(F32)
            sum_s[c] = mine * own + other * got

    def chain_pass(way):
        second = par == (1 - way)
        for c in range(HU):

            @pl.when(has_before(way))
            def _():
                chain_arrival(way, 1, c).wait_recv()

            inner, enter, through = marks(c // 2)
            weight = enter if way == 0 else inner
            carry = carry_r[way, c].astype(F32)
            pass_s[way, c] = (sum_s[c] + through * carry).astype(BF)

            @pl.when(has_next(way))
            def _():
                chain_copy(way, 1, c).start()

            own = pay_s[way, par * HU + c].astype(F32)
            got = m1_r[way, c].astype(F32)
            later = jnp.where(second, got, own) + weight * carry
            in_s[way, par * HU + c] = jnp.where(second, later, carry).astype(BF)
            give_s[way, c] = jnp.where(second, carry, later).astype(BF)
            chain_copy(way, 2, c).start()

    def chain_finish(way):
        for c in range(HU):
            chain_arrival(way, 2, c).wait_recv()

    def chain_drain(way):
        for c in range(HU):
            chain_copy(way, 0, c).wait_send()

            @pl.when(has_next(way))
            def _():
                chain_copy(way, 1, c).wait_send()

            chain_copy(way, 2, c).wait_send()

    chain_begin(0)
    lax.fori_loop(0, HU, local_part(par), 0, unroll=3)

    @pl.when(sq + 1 < n)
    def _():
        for which in range(2):
            halo_copy(which, sq + 1).start()

    for r in range(R):
        same = use_mask[r] == seg[r : r + 1, :].astype(F32)
        pad_j = pad[r : r + 1, :]
        open_key = same & (((j_pos < i_pos) & (pad_j == 1)) | (i_pos == j_pos))
        far_mask[r] = open_key.astype(F32)
        near_mask[r] = (open_key & (i_pos - j_pos <= BAND)).astype(F32)
    project(6, w_query, q_s)
    loads[7].wait()
    loads[8].wait()
    for a in range(2):
        for hp in range(PAIRS):
            sides = [
                jnp.broadcast_to(blend[a : a + 1, 2 * hp + side : 2 * hp + side + 1], (1, T))
                for side in range(2)
            ]
            weight_s[a * PAIRS + hp : a * PAIRS + hp + 1, :] = jnp.where(lane_low(1), *sides)
    ones_pair = two_blocks(jnp.ones((T, T), BF))

    def far_local(u, _):
        r = unit_row(u)
        queries = q_s[u].astype(F32)
        values = two_blocks(v_s[u])
        mask = far_mask[r]
        mask = jnp.concatenate([mask, mask], 1)
        for a, (feature, _slope) in enumerate(FEATURES):
            fq = feature(queries).astype(BF)
            fq_s[a, u] = fq
            kernel = (nt(fq, two_blocks(fk_s[a, u])) * mask).astype(BF)
            kk_s[a, u] = kernel
            far_s[a, u] = nn(kernel, values)
            den_s[a, u] = nn(kernel, ones_pair)
        return 0

    lax.fori_loop(0, U, far_local, 0, unroll=4)

    for slot, step in enumerate((1, 2, -1)):
        came = (sq - step >= 0) & (sq - step < n)

        @pl.when(came)
        def _():
            info_copy(slot, sq).wait_recv()

    @pl.when(sq > 0)
    def _():
        for which in range(2):
            halo_copy(which, sq).wait_recv()

    i_low = lax.broadcasted_iota(jnp.int32, (HALO, T), 0)
    j_low = lax.broadcasted_iota(jnp.int32, (HALO, T), 1)
    for r in range(R):
        seg_i = use_mask[r]
        marks_before = info_in[0, 1, r : r + 1, :]
        reach = j_low >= T - BAND + i_low
        halo_mask[r] = (reach & (seg_i[:HALO] + 1.0 == marks_before)).astype(F32)
        use_mask[r] = (seg_i == info_in[0, 0, r : r + 1, :]).astype(F32)

    chain_pair(0)

    def near_local(u, _):
        r = unit_row(u)
        queries = q_s[u]
        scores = nt(queries, two_blocks(k_s[u])) * SCALE
        scores_halo = nt(queries[:HALO], two_blocks(hk_s[u])) * SCALE
        open_near = near_mask[r] > 0
        open_halo = halo_mask[r] > 0
        for side in range(2):
            lanes = slice(side * T, (side + 1) * T)
            s = jnp.where(open_near, scores[:, lanes], NEGATIVE)
            sh = jnp.where(open_halo, scores_halo[:, lanes], NEGATIVE)
            peak = jnp.max(s, -1, keepdims=True)
            peak_halo = jnp.maximum(peak[:HALO], jnp.max(sh, -1, keepdims=True))
            peak = jnp.concatenate([peak_halo, peak[HALO:]], 0)
            e = jnp.exp(s - peak)
            eh = jnp.exp(sh - peak_halo)
            norm = jnp.sum(e, -1, keepdims=True)
            norm_halo = norm[:HALO] + jnp.sum(eh, -1, keepdims=True)
            inverse = 1.0 / jnp.concatenate([norm_halo, norm[HALO:]], 0)
            p_s[u, :, lanes] = e * inverse
            ph_s[u, :, lanes] = eh * inverse[:HALO]
        near_s[u] = nn(p_s[u].astype(BF), two_blocks(v_s[u]))
        near_s[u, :HALO, :] += nn(ph_s[u].astype(BF), two_blocks(hv_s[u]))
        return 0

    entry = z * PARTS // nz
    for part in range(PARTS):

        @pl.when(entry == part)
        def _():
            chain_pass(0)

        lax.fori_loop(part * U // PARTS, (part + 1) * U // PARTS, near_local, 0, unroll=3)
    chain_finish(0)

    def blend_lanes(a, u):
        return weight_s[pl.ds(a * PAIRS + unit_pair(u), 1), :]

    def far_finish(u, _):
        r = unit_row(u)
        hp = unit_pair(u)
        use = use_mask[r]
        blended = near_s[u]
        for a in range(2):
            fq = fq_s[a, u]
            state = two_blocks(in_s[0, u, a * E : (a + 1) * E, :])
            norm = in_s[0, u, 2 * E + 8 * a : 2 * E + 8 * a + 1, :].astype(F32)
            numer = far_s[a, u] + use * nn(fq, state)
            weighted = (fq.astype(F32) * norm).astype(BF)
            denom = den_s[a, u] + use * nn(weighted, ones_block)
            far = numer / denom
            far_s[a, u] = far
            den_s[a, u] = denom
            blended = blended + blend_lanes(a, u) * far
        rows = pl.ds(pl.multiple_of(r * T, T), T)
        lanes = pl.ds(pl.multiple_of(hp * T, T), T)
        mixed[rows, lanes] = blended.astype(BF)
        return 0

    lax.fori_loop(0, U, far_finish, 0, unroll=4)

    loads[9].wait()
    middle[...] = tok[...].astype(F32) + nn(mixed[...], w_out[...])
    for r in range(R):
        rows = pl.ds(r * T, T)
        mid = middle[rows, :]
        inverse = lax.rsqrt(jnp.mean(mid * mid, -1, keepdims=True) + EPSILON)
        normed_two[rows, :] = (mid * inverse * gain_two[...]).astype(BF)
    total[...] = jnp.zeros_like(total)
    back_two[...] = jnp.zeros_like(back_two)
    for i in (10, 11, 12):
        loads[i].wait()

    def feed(t, _):
        at = pl.multiple_of(t * D, D)
        cols = pl.ds(at, D)
        up = nn(normed_two[...], w_up[:, cols])
        square = up * up
        tangent = jnp.tanh(GELU_A * (up + GELU_B * square * up))
        act = (0.5 * up * (1.0 + tangent)).astype(BF)
        slope = 0.5 * (1.0 + tangent) + 0.5 * up * (1.0 - tangent * tangent) * GELU_A * (
            1.0 + 3.0 * GELU_B * square
        )
        total[...] += nn(act, w_down[cols, :])
        keep(pl.multiple_of(row_down(t), D), tn(act, cot[...]))
        d_up = (nt(cot[...], w_down[cols, :]) * slope).astype(BF)
        keep(pl.multiple_of(row_up(t), D), tn(normed_two[...], d_up))
        back_two[...] += nt(d_up, w_up[:, cols])
        return 0

    lax.fori_loop(0, TILES // 2, feed, 0, unroll=2)
    sums(ORDER["down"])
    lax.fori_loop(TILES // 2, TILES, feed, 0, unroll=2)
    sums(ORDER["up"])
    out[...] = (middle[...] + total[...]).astype(BF)

    gain_grad_two = jnp.zeros((1, D), F32)
    for r in range(R):
        rows = pl.ds(r * T, T)
        mid = middle[rows, :]
        inverse = lax.rsqrt(jnp.mean(mid * mid, -1, keepdims=True) + EPSILON)
        d_n = back_two[rows, :]
        gain_grad_two += jnp.sum(d_n * mid * inverse, 0, keepdims=True)
        scaled = d_n * gain_two[...]
        d_mid = (
            cot[rows, :].astype(F32)
            + inverse * scaled
            - mid * (inverse * inverse * inverse) * jnp.mean(mid * scaled, -1, keepdims=True)
        )
        total[rows, :] = d_mid
        normed_two[rows, :] = d_mid.astype(BF)
    d_branch = normed_two[...]
    keep(ROW_OUT, tn(mixed[...], d_branch))
    d_blended = nt(d_branch, w_out[...]).astype(BF)
    for r in range(R):
        for hp in range(PAIRS):
            db_s[unit_of(r, hp)] = d_blended[r * T : (r + 1) * T, hp * T : (hp + 1) * T]
    sums(ORDER["branch"])

    gb_s[...] = jnp.zeros_like(gb_s)

    def far_prepare(u, _):
        r = unit_row(u)
        hp = unit_pair(u)
        use = use_mask[r]
        use_low = use.astype(BF)
        d_out = db_s[u].astype(F32)
        norms = []
        for a in range(2):
            far = far_s[a, u]
            inverse = 1.0 / den_s[a, u]
            product = d_out * far
            row = a * PAIRS + hp
            gb_s[pl.ds(row, 1), :] += jnp.sum(product, 0, keepdims=True)
            weight = blend_lanes(a, u)
            product = product * weight
            high = product.astype(BF)
            rest = (product - high.astype(F32)).astype(BF)
            dden = -(nn(high, ones_block) + nn(rest, ones_block)) * inverse
            dden_s[a, u] = dden
            dnum = (weight * d_out * inverse).astype(BF)
            low_s[a, u] = dnum
            used = fq_s[a, u] * use_low
            pay_s[1, u, a * E : (a + 1) * E, :] = pick(tn(used, dnum)).astype(BF)
            norm = jnp.sum(used.astype(F32) * dden, 0, keepdims=True)
            norms.append(jnp.broadcast_to(norm, (8, T)))
        pay_s[1, u, 2 * E : PAY, :] = jnp.concatenate(norms, 0).astype(BF)
        return 0

    def prepare_part(which):
        return lambda i, _: far_prepare(which * HU + i, 0)

    lax.fori_loop(0, HU, prepare_part(1 - par), 0, unroll=3)
    chain_begin(1)
    lax.fori_loop(0, HU, prepare_part(par), 0, unroll=3)

    def near_back(u, _):
        keys = two_blocks(k_s[u])
        halo_keys = two_blocks(hk_s[u])
        queries = q_s[u]
        d_out = db_s[u]
        dp = nt(d_out, two_blocks(v_s[u]))
        dp_halo = nt(d_out[:HALO], two_blocks(hv_s[u]))
        p = p_s[u]
        p_halo = ph_s[u]
        ds = []
        ds_halo = []
        for side in range(2):
            lanes = slice(side * T, (side + 1) * T)
            ps, phs = p[:, lanes], p_halo[:, lanes]
            delta = jnp.sum(ps * dp[:, lanes], -1, keepdims=True)
            delta_halo = delta[:HALO] + jnp.sum(phs * dp_halo[:, lanes], -1, keepdims=True)
            delta = jnp.concatenate([delta_halo, delta[HALO:]], 0)
            ds.append(ps * (dp[:, lanes] - delta))
            ds_halo.append(phs * (dp_halo[:, lanes] - delta_halo))
        ds = jnp.concatenate(ds, 1).astype(BF)
        ds_halo = jnp.concatenate(ds_halo, 1).astype(BF)
        near_s[u] = nn(ds, keys) * SCALE
        near_s[u, :HALO, :] += nn(ds_halo, halo_keys) * SCALE
        dk_s[u] = pick(tn(ds, queries)) * SCALE
        dv_s[u] = pick(tn(p.astype(BF), d_out))
        hdk_s[u] = (pick(tn(ds_halo, queries[:HALO])) * SCALE)[T - HALO :].astype(BF)
        hdv_s[u] = pick(tn(p_halo.astype(BF), d_out[:HALO]))[T - HALO :].astype(BF)
        return 0

    sums(ORDER["prepare"])
    lax.fori_loop(0, HU, near_back, 0, unroll=3)
    sums(ORDER["near_a"])
    lax.fori_loop(HU, U, near_back, 0, unroll=3)
    sums(ORDER["near_b"])

    def halo_back(which, to):
        src, dst = ((hdk_s, hdk_r), (hdv_s, hdv_r))[which]
        return send(src, dst, halo_send.at[2 + which], halo_recv.at[2 + which], to)

    @pl.when(sq > 0)
    def _():
        for which in range(2):
            halo_back(which, sq - 1).start()

    chain_pair(1)
    sums(ORDER["pair"])

    def far_back(u, _):
        r = unit_row(u)
        values = two_blocks(v_s[u])
        mask = far_mask[r]
        mask = jnp.concatenate([mask, mask], 1)
        use = use_mask[r]
        queries = q_s[u].astype(F32)
        keys = k_s[u].astype(F32)
        dq = near_s[u]
        dk = dk_s[u]
        dv = dv_s[u]
        for a, (_feature, slope) in enumerate(FEATURES):
            dnum = low_s[a, u]
            dden = dden_s[a, u]
            fq = fq_s[a, u]
            fk = two_blocks(fk_s[a, u])
            added = jnp.concatenate(
                [
                    jnp.broadcast_to(dden[:, 0:1], (T, T)),
                    jnp.broadcast_to(dden[:, E : E + 1], (T, T)),
                ],
                1,
            )
            d_kernel = ((nt(dnum, values) + added) * mask).astype(BF)
            dv += pick(tn(kk_s[a, u], dnum))
            state = two_blocks(in_s[0, u, a * E : (a + 1) * E, :])
            norm = in_s[0, u, 2 * E + 8 * a : 2 * E + 8 * a + 1, :].astype(F32)
            dfq = nn(d_kernel, fk) + use * (nt(dnum, state) + dden * norm)
            dq += dfq * slope(queries)
            dk += pick(tn(d_kernel, fq)) * slope(keys)
        near_s[u] = dq
        dk_s[u] = dk
        dv_s[u] = dv
        return 0

    turn = (nz - 1 - z) * PARTS // nz
    for part in range(PARTS):

        @pl.when(turn == part)
        def _():
            chain_pass(1)

        lax.fori_loop(part * U // PARTS, (part + 1) * U // PARTS, far_back, 0, unroll=3)
        sums(ORDER["far_%d" % part])

    for u in range(U):
        r, hp = (u % (2 * R)) // 2, (u // (2 * R)) * 2 + u % 2
        wide_s[0, r * T : (r + 1) * T, hp * T : (hp + 1) * T] = near_s[u].astype(BF)
    keep(ROW_Q, tn(normed[...], wide_s[0]))
    sums(ORDER["query"])
    back_two[...] = nt(wide_s[0], w_query[...])

    @pl.when(sq + 1 < n)
    def _():
        for which in range(2):
            halo_back(which, sq).wait_recv()

    chain_finish(1)
    sums(ORDER["state"])

    def far_close(u, _):
        r = unit_row(u)
        hp = unit_pair(u)
        tail = tail_mask[r]
        keys = k_s[u].astype(F32)
        values = v_s[u]
        dk = dk_s[u]
        dv = dv_s[u]
        for a, (_feature, slope) in enumerate(FEATURES):
            state = two_blocks(in_s[1, u, a * E : (a + 1) * E, :])
            norm = in_s[1, u, 2 * E + 8 * a : 2 * E + 8 * a + 1, :].astype(F32)
            dk += tail * (nt(values, state) + norm) * slope(keys)
            dv += tail * nn(fk_s[a, u], state)
        zero = jnp.zeros((T - HALO, T), F32)
        dk += jnp.concatenate([zero, hdk_r[u].astype(F32)], 0)
        dv += jnp.concatenate([zero, hdv_r[u].astype(F32)], 0)
        rows = pl.ds(pl.multiple_of(r * T, T), T)
        lanes = pl.ds(pl.multiple_of(hp * T, T), T)
        wide_s[1, rows, lanes] = dk.astype(BF)
        wide_s[2, rows, lanes] = dv.astype(BF)
        return 0

    lax.fori_loop(0, U, far_close, 0, unroll=4)
    sums(ORDER["close"])
    first = 2 - lax.rem(rw, 2)
    keep(pl.multiple_of(ROW_Q + first * D, D), tn(normed[...], wide_s[first]))
    sums(((3, 0, 0), (3, 1, 0)))
    rest = 3 - first
    keep(pl.multiple_of(ROW_Q + rest * D, D), tn(normed[...], wide_s[rest]))
    sums(ORDER["key"])
    for i, weight in ((1, w_key), (2, w_value)):
        back_two[...] += nt(wide_s[i], weight[...])
    gain_grad_one = jnp.zeros((1, D), F32)
    for r in range(R):
        rows = pl.ds(r * T, T)
        x = tok[rows, :].astype(F32)
        inverse = lax.rsqrt(jnp.mean(x * x, -1, keepdims=True) + EPSILON)
        d_n = back_two[rows, :]
        gain_grad_one += jnp.sum(d_n * x * inverse, 0, keepdims=True)
        scaled = d_n * gain_one[...]
        d_x = (
            total[rows, :]
            + inverse * scaled
            - x * (inverse * inverse * inverse) * jnp.mean(x * scaled, -1, keepdims=True)
        )
        grad_tok[rows, :] = d_x.astype(BF)
    blends = [
        jnp.concatenate([gb_s[a * PAIRS + hp : a * PAIRS + hp + 1, :] for hp in range(PAIRS)], 1)
        for a in range(2)
    ]
    small_s[...] = jnp.concatenate(
        [gain_grad_one, gain_grad_two] + blends + [jnp.zeros((SMALL - 4, D), F32)], 0
    )
    small_step(0)
    sums(ORDER["back"])
    for i, step in enumerate(ORDER["tail"]):
        sums((step,))
        if i % 2 and i // 2 < len(partners):
            small_step(i // 2 + 1)
    for b in range(len(ORDER["tail"]) // 2, len(partners)):
        small_step(b + 1)
    sums_rest()
    small_out[...] = small_s[...]

    for slot, step in enumerate((1, 2, -1)):

        @pl.when((sq + step >= 0) & (sq + step < n))
        def _():
            info_copy(slot, sq + step).wait_send()

    @pl.when(sq + 1 < n)
    def _():
        for which in range(2):
            halo_copy(which, sq + 1).wait_send()

    @pl.when(sq > 0)
    def _():
        for which in range(2):
            halo_back(which, sq - 1).wait_send()

    chain_drain(0)
    chain_drain(1)
    for c in range(len(CHUNKS)):
        sum_drain(c)
        for color in range(2):
            full_copy(c, color).wait()


def widen_kernel(
    grads,
    small_in,
    out_in,
    back_in,
    g_one,
    g_two,
    g_blend,
    g_query,
    g_key,
    g_value,
    g_out,
    g_up,
    g_down,
    out,
    back,
    small,
    gains,
    blends,
    token,
    held,
    wide,
    small_sem,
    token_sem,
    in_sem,
    out_sem,
):
    blocks = ROWS_ALL // D
    targets = []
    for t in (0, 2):
        targets += [g_down.at[pl.ds((t + i) * D, D)] for i in range(2)]
        targets += [g_up.at[:, pl.ds((t + i) * D, D)] for i in range(2)]
    targets += [g_out, g_query, g_key, g_value]
    small_read = pltpu.make_async_copy(small_in, small, small_sem.at[0])
    reads = [
        pltpu.make_async_copy(grads.at[:, pl.ds(i * D, D)], held.at[i], in_sem.at[i])
        for i in range(blocks)
    ]
    token_reads = [
        pltpu.make_async_copy(src, token.at[i], token_sem.at[i])
        for i, src in enumerate((out_in, back_in))
    ]
    for read in [small_read] + reads + token_reads:
        read.start()
    writes = [
        pltpu.make_async_copy(wide.at[i], targets[i], out_sem.at[i]) for i in range(blocks)
    ]
    small_writes = [
        pltpu.make_async_copy(src, dst, small_sem.at[i + 1])
        for i, (src, dst) in enumerate(
            ((gains.at[0], g_one), (gains.at[1], g_two), (blends, g_blend))
        )
    ]
    token_writes = [
        pltpu.make_async_copy(token.at[i], dst, token_sem.at[i + 2])
        for i, dst in enumerate((out, back))
    ]
    for i in range(blocks):
        reads[i].wait()
        wide[i, :, :LANES] = held[i, 0].astype(F32)
        wide[i, :, LANES:] = held[i, 1].astype(F32)
        writes[i].start()
    for read, write in zip(token_reads, token_writes):
        read.wait()
        write.start()
    small_read.wait()
    gains[...] = small[:2, :]
    lane = lax.broadcasted_iota(jnp.int32, (H, D), 1) // E
    head = lax.broadcasted_iota(jnp.int32, (H, D), 0)
    for a in range(2):
        row = small[2 + a : 3 + a, :]
        per_head = jnp.sum(jnp.where(lane == head, row, 0.0), -1, keepdims=True)
        blends[a : a + 1, :] = jnp.broadcast_to(per_head, (H, H)).T[:1]
    for write in small_writes:
        write.start()
    for write in small_writes + writes + token_writes:
        write.wait()


def solution(mesh):
    n = mesh.shape["seq"]
    n_rows = mesh.shape["rows"]

    def shards(
        tokens,
        segment_ids,
        padding,
        gain_one,
        w_query,
        w_key,
        w_value,
        blend,
        w_out,
        gain_two,
        w_up,
        w_down,
        cotangent,
    ):
        R, tok_count, _ = tokens.shape
        M = R * tok_count
        U = R * PAIRS
        HU = U // 2
        vmem = pl.BlockSpec(memory_space=pltpu.VMEM)
        anyspace = pl.BlockSpec(memory_space=pl.ANY)
        V = pltpu.VMEM
        unit_f = V((U, T, T), F32)
        unit_b = V((U, T, T), BF)
        two_f = V((2, U, T, T), F32)
        two_b = V((2, U, T, T), BF)
        wide_f = V((M, D), F32)
        wide_b = V((M, D), BF)
        halo_b = V((U, HALO, T), BF)
        dma = pltpu.SemaphoreType.DMA
        plans, landed_rows = sum_plans(n_rows, n)
        stages = 2 * max(len(plan) for both in plans for plan in both)
        count = bits(n) + bits(n_rows)
        scratch = [
            V((2, ROWS_ALL, LANES), BF),
            V((2, ROWS_ALL, LANES), BF),
            V((2, landed_rows, LANES), BF),
            V((SMALL, D), F32),
            V((count, SMALL, D), F32),
            wide_b,
            V((R, T), jnp.int32),
            V((R, T), jnp.int32),
            V((1, D), F32),
            V((1, D), F32),
            V((2, H), F32),
            V((D, D), BF),
            V((D, D), BF),
            V((D, D), BF),
            V((D, D), BF),
            V((D, FF), BF),
            V((FF, D), BF),
            wide_b,
            V((2 * PAIRS, T), F32),
            wide_b,
            wide_b,
            wide_b,
            wide_f,
            wide_f,
            wide_f,
            unit_b,
            unit_b,
            unit_b,
            unit_b,
            unit_b,
            two_b,
            two_b,
            V((2, U, T, 2 * T), BF),
            V((U, T, 2 * T), F32),
            V((U, HALO, 2 * T), F32),
            unit_f,
            two_f,
            two_f,
            unit_b,
            two_b,
            two_f,
            unit_f,
            unit_f,
            halo_b,
            halo_b,
            halo_b,
            halo_b,
            V((3, M, D), BF),
            V((R, T, T), F32),
            V((R, T, T), F32),
            V((R, T, T), F32),
            V((R, T, T), F32),
            V((R, HALO, T), F32),
            V((2, 8, T), F32),
            V((3, 2, 8, T), F32),
            V((2 * PAIRS, T), F32),
            V((2, U, PAY, T), BF),
            V((2, HU, PAY, T), BF),
            V((HU, PAY, T), F32),
            V((2, HU, PAY, T), BF),
            V((2, HU, PAY, T), BF),
            V((2, U, PAY, T), BF),
            V((2, HU, PAY, T), BF),
            dma((13,)),
            dma((3,)),
            dma((3,)),
            dma((4,)),
            dma((4,)),
            dma((2, 3, HU)),
            dma((2, 3, HU)),
            dma((len(CHUNKS), 2, stages, 3)),
            dma((len(CHUNKS), 2, stages, 3)),
            dma((count,)),
            dma((count,)),
            dma((len(CHUNKS), 2)),
        ]
        out, grad_tok, small, grads = pl.pallas_call(
            functools.partial(layer_kernel, n, n_rows, R),
            out_shape=(
                jax.ShapeDtypeStruct((M, D), BF),
                jax.ShapeDtypeStruct((M, D), BF),
                jax.ShapeDtypeStruct((SMALL, D), F32),
                jax.ShapeDtypeStruct((2, ROWS_ALL, LANES), BF),
            ),
            in_specs=[pl.BlockSpec(memory_space=pltpu.HBM)] * 13,
            out_specs=(vmem, vmem, vmem, anyspace),
            scratch_shapes=scratch,
            compiler_params=pltpu.CompilerParams(
                collective_id=0, has_side_effects=True, vmem_limit_bytes=LAYER_VMEM
            ),
            name="layer",
        )(
            tokens.reshape(M, D),
            segment_ids,
            padding,
            gain_one.reshape(1, D),
            gain_two.reshape(1, D),
            blend,
            w_query,
            w_key,
            w_value,
            w_out,
            w_up,
            w_down,
            cotangent.reshape(M, D),
        )
        square = jax.ShapeDtypeStruct((D, D), F32)
        token = jax.ShapeDtypeStruct((M, D), BF)
        blocks = ROWS_ALL // D
        g_one, g_two, g_blend, g_query, g_key, g_value, g_out, g_up, g_down, out, grad_tok = (
          pl.pallas_call(
            widen_kernel,
            out_shape=(
                jax.ShapeDtypeStruct((D,), F32),
                jax.ShapeDtypeStruct((D,), F32),
                jax.ShapeDtypeStruct((2, H), F32),
                square,
                square,
                square,
                square,
                jax.ShapeDtypeStruct((D, FF), F32),
                jax.ShapeDtypeStruct((FF, D), F32),
                token,
                token,
            ),
            in_specs=[anyspace] * 4,
            out_specs=(anyspace,) * 11,
            scratch_shapes=[
                V((SMALL, D), F32),
                V((2, D), F32),
                V((2, H), F32),
                V((2, M, D), BF),
                V((blocks, 2, D, LANES), BF),
                V((blocks, D, D), F32),
                dma((4,)),
                dma((4,)),
                dma((blocks,)),
                dma((blocks,)),
            ],
            compiler_params=pltpu.CompilerParams(vmem_limit_bytes=WIDEN_VMEM),
            name="widen",
        )(grads, small, out, grad_tok))
        return (
            out.reshape(R, tok_count, D),
            grad_tok.reshape(R, tok_count, D),
            g_one,
            g_query,
            g_key,
            g_value,
            g_blend,
            g_out,
            g_two,
            g_up,
            g_down,
        )

    row, whole = P("rows", "seq", None), P()
    return jax.shard_map(
        shards,
        mesh=mesh,
        in_specs=(row, P("rows", "seq"), P("rows", "seq")) + (whole,) * 9 + (row,),
        out_specs=(row, row) + (whole,) * 9,
        check_vma=False,
    )
```

```python
import functools
import math

import jax
import jax.numpy as jnp
from jax import lax
from jax.experimental import pallas as pl
from jax.experimental.pallas import tpu as pltpu
from jax.sharding import PartitionSpec as P

MESH = pl.DeviceIdType.MESH
F32 = jnp.float32
BF = jnp.bfloat16
D = 512
H = 8
E = 64
FF = 2048
BAND = 30
T = 128
PAIRS = 4
PAY = 144
HALO = 32
EPSILON = 1e-06
NEGATIVE = -1e30
SCALE = 1.0 / math.sqrt(E)
GELU_A = math.sqrt(2.0 / math.pi)
GELU_B = 0.044715
TILES = FF // D
ROW_OUT = 2 * FF
ROW_Q = ROW_OUT + D
ROWS_ALL = ROW_Q + 3 * D
SMALL = 8
LANES = D // 2
CHUNKS = ((0, FF), (FF, FF), (ROW_OUT, 2 * D), (ROW_Q + D, 2 * D))
DIMS = (("cyxab", "caxyb"), ("cxyq", "cyxq"), ("cyxq", "cxyq"), ("cyxq", "cxyq"))
PARTS = 4
LAYER_VMEM = 60 * 1024 * 1024
WIDEN_VMEM = 60 * 1024 * 1024


ORDER = {
    "down": (
        (0, 0, 0), (0, 1, 0),
    ),
    "up": (),
    "branch": (),
    "prepare": (
        (1, 1, 0), (0, 1, 1), (1, 0, 0), (0, 0, 1),
    ),
    "near_a": (
        (1, 0, 1), (1, 1, 1),
    ),
    "near_b": (
        (0, 1, 2),
    ),
    "pair": (
        (0, 0, 2),
    ),
    "far_0": (),
    "far_1": (
        (0, 1, 3), (1, 0, 2), (0, 0, 3), (1, 1, 2), (0, 1, 4),
    ),
    "far_2": (),
    "far_3": (),
    "query": (
        (1, 0, 3),
    ),
    "state": (
        (0, 0, 4),
    ),
    "close": (
        (2, 1, 0), (2, 0, 0), (0, 1, 5),
    ),
    "key": (
        (2, 1, 1), (3, 0, 0), (1, 1, 3), (3, 1, 0), (2, 0, 1), (3, 1, 1),
        (1, 0, 4), (3, 0, 1), (2, 0, 2), (1, 1, 4), (2, 1, 2), (1, 0, 5),
        (3, 0, 2), (2, 0, 3), (2, 1, 3), (3, 1, 2), (0, 1, 6), (1, 1, 5),
        (0, 0, 5),
    ),
    "back": (
        (1, 0, 6), (2, 0, 4), (2, 1, 4), (0, 0, 6), (3, 0, 3), (1, 1, 6),
        (2, 0, 5), (0, 1, 7), (3, 1, 3), (2, 1, 5), (3, 0, 4), (0, 0, 7),
        (3, 1, 4), (1, 0, 7), (1, 1, 7), (2, 0, 6),
    ),
    "tail": (
        (0, 1, 8), (3, 0, 5), (3, 1, 5), (0, 0, 8), (2, 1, 6), (3, 0, 6),
        (3, 1, 6), (2, 1, 7), (0, 1, 9), (2, 0, 7), (0, 0, 9), (3, 1, 7),
        (1, 0, 8), (1, 1, 8), (3, 0, 7), (2, 0, 8), (2, 1, 8), (3, 1, 8),
        (3, 0, 8), (0, 0, 10), (0, 1, 10),
    ),
}


def row_down(t):
    return (t // 2) * FF + (t % 2) * D


def row_up(t):
    return row_down(t) + FF // 2


def nn(a, b):
    return lax.dot_general(a, b, (((1,), (0,)), ((), ())), preferred_element_type=F32)


def nt(a, b):
    return lax.dot_general(a, b, (((1,), (1,)), ((), ())), preferred_element_type=F32)


def tn(a, b):
    return lax.dot_general(a, b, (((0,), (0,)), ((), ())), preferred_element_type=F32)


def lane_low(rows):
    return lax.broadcasted_iota(jnp.int32, (rows, T), 1) < E


def low_high():
    low = lane_low(T).astype(F32)
    return low.astype(BF), (1.0 - low).astype(BF)


def two_blocks(x):
    low, high = low_high()
    rows = x.shape[0]
    return jnp.concatenate([x * low[:rows], x * high[:rows]], 0)


def pick(stacked):
    half = stacked.shape[0] // 2
    return jnp.where(lane_low(half), stacked[:half], stacked[half:])


def block_ones():
    i = lax.broadcasted_iota(jnp.int32, (T, T), 0) < E
    j = lax.broadcasted_iota(jnp.int32, (T, T), 1) < E
    return jnp.where(i == j, 1.0, 0.0).astype(BF)


def feature_one(t):
    return jnp.where(t > 0, t + 1.0, jnp.exp(jnp.minimum(t, 0.0)))


def slope_one(t):
    return jnp.where(t > 0, 1.0, jnp.exp(jnp.minimum(t, 0.0)))


def feature_two(t):
    return 1.0 + jnp.tanh(t)


def slope_two(t):
    tangent = jnp.tanh(t)
    return 1.0 - tangent * tangent


FEATURES = ((feature_one, slope_one), (feature_two, slope_two))


def bits(size):
    return size.bit_length() - 1


def sum_order(dims, n_rows, n_seq):
    rows = [("rows", 2**b, 2) for b in range(bits(n_rows))]
    seq = [("seq", 2**b, 2) for b in range(bits(n_seq))]
    near, far = seq[:-2], seq[-2:]
    found = {
        "c": rows[:1],
        "y": rows[1:],
        "x": near,
        "a": far[:1],
        "b": far[1:],
        "q": [("seq", far[0][1], 4)],
    }
    return [stage for dim in dims for stage in found[dim]]


def sum_plan(dims, n_rows, n_seq, rows, offset):
    plan = []
    for axis, low, group in sum_order(dims, n_rows, n_seq):
        steps = [(low, group)]
        if group == 4 and rows % 64:
            steps = [(low, 2), (2 * low, 2)]
        for low, group in steps:
            split = rows % (16 * group) == 0
            part = rows // group if split else rows
            plan.append((axis, low, group, split, rows, part, offset))
            offset += (group - 1) * part
            rows = part
    return plan, offset


def sum_plans(n_rows, n_seq):
    plans = []
    offset = [0, 0]
    for (_base, rows), dims in zip(CHUNKS, DIMS):
        both = []
        for color in range(2):
            plan, offset[color] = sum_plan(dims[color], n_rows, n_seq, rows, offset[color])
            both.append(plan)
        plans.append(both)
    return plans, max(offset)


def layer_kernel(
    n,
    n_rows,
    R,
    tok_hbm,
    seg_hbm,
    pad_hbm,
    gain_one_hbm,
    gain_two_hbm,
    blend_hbm,
    w_query_hbm,
    w_key_hbm,
    w_value_hbm,
    w_out_hbm,
    w_up_hbm,
    w_down_hbm,
    cot_hbm,
    out,
    grad_tok,
    small_out,
    full_hbm,
    grads,
    full,
    landed,
    small_s,
    small_r,
    tok,
    seg,
    pad,
    gain_one,
    gain_two,
    blend,
    w_query,
    w_key,
    w_value,
    w_out,
    w_up,
    w_down,
    cot,
    weight_s,
    normed,
    normed_two,
    mixed,
    middle,
    total,
    back_two,
    q_s,
    k_s,
    v_s,
    hk_s,
    hv_s,
    fq_s,
    fk_s,
    kk_s,
    p_s,
    ph_s,
    near_s,
    far_s,
    den_s,
    db_s,
    low_s,
    dden_s,
    dk_s,
    dv_s,
    hdk_s,
    hdv_s,
    hdk_r,
    hdv_r,
    wide_s,
    far_mask,
    near_mask,
    use_mask,
    tail_mask,
    halo_mask,
    info_own,
    info_in,
    gb_s,
    pay_s,
    m1_r,
    sum_s,
    carry_r,
    pass_s,
    in_s,
    give_s,
    w_sem,
    info_send,
    info_recv,
    halo_send,
    halo_recv,
    chain_send,
    chain_recv,
    sum_send,
    sum_recv,
    small_send,
    small_recv,
    full_sem,
):
    U = R * PAIRS
    HU = U // 2
    sq = lax.axis_index("seq")
    rw = lax.axis_index("rows")
    par = lax.rem(sq, 2)
    z = sq // 2
    nz = n // 2
    partner = sq + 1 - 2 * par

    def unit_row(u):
        return lax.rem(u, 2 * R) // 2

    def unit_pair(u):
        return (u // (2 * R)) * 2 + lax.rem(u, 2)

    def unit_of(r, hp):
        return (hp // 2) * 2 * R + r * 2 + hp % 2

    def send(src, dst, send_sem, recv_sem, to):
        return pltpu.make_async_remote_copy(
            src_ref=src,
            dst_ref=dst,
            send_sem=send_sem,
            recv_sem=recv_sem,
            device_id=(to, rw),
            device_id_type=MESH,
        )

    barrier = pltpu.get_barrier_semaphore()
    for step in (1, 2):

        @pl.when(sq >= step)
        def _():
            pl.semaphore_signal(barrier, inc=1, device_id=(sq - step, rw), device_id_type=MESH)

        @pl.when(sq + step < n)
        def _():
            pl.semaphore_signal(barrier, inc=1, device_id=(sq + step, rw), device_id_type=MESH)

    plans, _size = sum_plans(n_rows, n)
    partners = [("rows", 2**b) for b in range(bits(n_rows))]
    partners += [("seq", 2**b) for b in range(bits(n))]

    def peer_of(axis, low, group, step):
        own = rw if axis == "rows" else sq
        mine = lax.rem(own // low, group)
        other = own + (lax.rem(mine + step, group) - mine) * low
        return mine, ((sq, other) if axis == "rows" else (other, rw))

    groups = {(axis, low, 2) for axis, low in partners}
    for both in plans:
        for plan in both:
            groups |= {(axis, low, group) for axis, low, group, *_ in plan}
    greet = [
        (axis, low, group, d)
        for axis, low, group in sorted(groups)
        for d in range(1, group)
        if (axis, low) != ("seq", 1) and not (group == 2 and (axis, low, 4) in groups)
    ]
    for axis, low, group, d in greet:
        pl.semaphore_signal(
            barrier, inc=1, device_id=peer_of(axis, low, group, d)[1], device_id_type=MESH
        )

    loads = [
        pltpu.make_async_copy(src, dst, w_sem.at[i])
        for i, (src, dst) in enumerate(
            (
                (tok_hbm, tok),
                (gain_one_hbm, gain_one),
                (w_key_hbm, w_key),
                (w_value_hbm, w_value),
                (seg_hbm, seg),
                (pad_hbm, pad),
                (w_query_hbm, w_query),
                (blend_hbm, blend),
                (gain_two_hbm, gain_two),
                (w_out_hbm, w_out),
                (w_up_hbm, w_up),
                (w_down_hbm, w_down),
                (cot_hbm, cot),
            )
        )
    ]
    for load in loads:
        load.start()
    loads[0].wait()
    loads[1].wait()

    for r in range(R):
        rows = pl.ds(r * T, T)
        x = tok[rows, :].astype(F32)
        inverse = lax.rsqrt(jnp.mean(x * x, -1, keepdims=True) + EPSILON)
        normed[rows, :] = (x * inverse * gain_one[...]).astype(BF)

    def project(load, weight, held):
        loads[load].wait()
        whole = nn(normed[...], weight[...]).astype(BF)
        for r in range(R):
            for hp in range(PAIRS):
                held[unit_of(r, hp)] = whole[r * T : (r + 1) * T, hp * T : (hp + 1) * T]

    project(2, w_key, k_s)
    project(3, w_value, v_s)
    loads[4].wait()
    loads[5].wait()

    i_pos = lax.broadcasted_iota(jnp.int32, (T, T), 0)
    j_pos = lax.broadcasted_iota(jnp.int32, (T, T), 1)
    info_own[...] = jnp.zeros_like(info_own)
    for r in range(R):
        seg_row = seg[r : r + 1, :].astype(F32)
        pad_row = pad[r : r + 1, :].astype(F32)
        seg_j = jnp.broadcast_to(seg_row, (T, T))
        seg_i = seg_j.T
        pad_i = jnp.broadcast_to(pad_row, (T, T)).T
        last = seg_i[T - 1 : T, :]
        tail_mask[r] = ((seg_i == last) & (pad_i == 1.0)).astype(F32)
        use_mask[r] = seg_i
        info_own[0, r : r + 1, :] = last
        info_own[1, r : r + 1, :] = jnp.where(pad_row == 1.0, seg_row + 1.0, 0.0)

    head = pl.ds(0, T - HALO)
    hk_s[:, head, :] = jnp.zeros((U, T - HALO, T), BF)
    hv_s[:, head, :] = jnp.zeros((U, T - HALO, T), BF)

    @pl.when(sq == 0)
    def _():
        tail = pl.ds(T - HALO, HALO)
        hk_s[:, tail, :] = jnp.zeros((U, HALO, T), BF)
        hv_s[:, tail, :] = jnp.zeros((U, HALO, T), BF)

    @pl.when(sq == n - 1)
    def _():
        hdk_r[...] = jnp.zeros((U, HALO, T), BF)
        hdv_r[...] = jnp.zeros((U, HALO, T), BF)

    ones_block = block_ones()

    def local_state(u, _):
        r = unit_row(u)
        tail = tail_mask[r].astype(BF)
        keys = k_s[u].astype(F32)
        values = v_s[u]
        norms = []
        for a, (feature, _slope) in enumerate(FEATURES):
            fk = feature(keys).astype(BF)
            fk_s[a, u] = fk
            weighted = fk * tail
            pay_s[0, u, a * E : (a + 1) * E, :] = pick(tn(weighted, values)).astype(BF)
            norm = jnp.sum(weighted.astype(F32), 0, keepdims=True)
            norms.append(jnp.broadcast_to(norm, (8, T)))
        pay_s[0, u, 2 * E : PAY, :] = jnp.concatenate(norms, 0).astype(BF)
        return 0

    def local_part(which):
        return lambda i, _: local_state(which * HU + i, 0)

    lax.fori_loop(0, HU, local_part(1 - par), 0, unroll=3)

    pl.semaphore_wait(barrier, jnp.minimum(sq, 2) + jnp.minimum(n - 1 - sq, 2) + len(greet))

    def starts_of(chunk, color):
        start = CHUNKS[chunk][0]
        found = [start]
        for axis, low, group, split, _rows, part, _offset in plans[chunk][color]:
            if split:
                start = start + peer_of(axis, low, group, 1)[0] * part
            found.append(start)
        return found

    starts = [[starts_of(c, color) for color in range(2)] for c in range(len(CHUNKS))]

    def aligned(start, size):
        return pl.ds(pl.multiple_of(start, 16), size)

    def sum_copy(src, dst, chunk, color, slot, d, to):
        return pltpu.make_async_remote_copy(
            src_ref=src,
            dst_ref=dst,
            send_sem=sum_send.at[chunk, color, slot, d - 1],
            recv_sem=sum_recv.at[chunk, color, slot, d - 1],
            device_id=to,
            device_id_type=MESH,
        )

    def scatter_copy(chunk, color, k, d):
        axis, low, group, split, _rows, part, offset = plans[chunk][color][k]
        mine, to = peer_of(axis, low, group, d)
        start = starts[chunk][color][k]
        if split:
            start = start + lax.rem(mine + d, group) * part
        src = grads.at[color, aligned(start, part)]
        dst = landed.at[color, pl.ds(offset + (d - 1) * part, part)]
        return sum_copy(src, dst, chunk, color, k, d, to)

    def scatter_add(chunk, color, k):
        axis, low, group, split, _rows, part, offset = plans[chunk][color][k]
        for d in range(1, group):
            scatter_copy(chunk, color, k, d).wait_recv()
        if not split:
            scatter_copy(chunk, color, k, 1).wait_send()
        start = starts[chunk][color][k + 1]
        block = math.gcd(part, 128)
        target = full if k + 1 == len(plans[chunk][color]) else grads

        def add(i, _):
            here = aligned(start + i * block, block)
            value = grads[color, here, :]
            for d in range(1, group):
                at = pl.multiple_of(offset + (d - 1) * part + i * block, 16)
                value += landed[color, pl.ds(at, block), :]
            target[color, here, :] = value
            return 0

        lax.fori_loop(0, part // block, add, 0)

    def gather_copy(chunk, color, k, d):
        axis, low, group, _split, _rows, part, _offset = plans[chunk][color][k]
        here = full.at[color, aligned(starts[chunk][color][k + 1], part)]
        slot = 2 * len(plans[chunk][color]) - 1 - k
        return sum_copy(here, here, chunk, color, slot, d, peer_of(axis, low, group, d)[1])

    def gather_arrival(chunk, color, k):
        axis, low, group, _split, _rows, part, _offset = plans[chunk][color][k]
        slot = 2 * len(plans[chunk][color]) - 1 - k
        for d in range(1, group):
            mine, to = peer_of(axis, low, group, d)
            source = lax.rem(mine - d + group, group)
            here = full.at[color, aligned(starts[chunk][color][k] + source * part, part)]
            sum_copy(here, here, chunk, color, slot, d, to).wait_recv()

    def sum_step(chunk, color, k):
        plan = plans[chunk][color]
        K = len(plan)
        if 1 <= k <= K:
            scatter_add(chunk, color, k - 1)
        elif K < k <= 2 * K and plan[2 * K - k][3]:
            gather_arrival(chunk, color, 2 * K - k)
        if k < K:
            for d in range(1, plan[k][2]):
                scatter_copy(chunk, color, k, d).start()
        elif k < 2 * K and plan[2 * K - 1 - k][3]:
            for d in range(1, plan[2 * K - 1 - k][2]):
                gather_copy(chunk, color, 2 * K - 1 - k, d).start()

    def full_copy(chunk, color):
        base, rows = CHUNKS[chunk]
        here = pl.ds(base, rows)
        return pltpu.make_async_copy(
            full.at[color, here], full_hbm.at[color, here], full_sem.at[chunk, color]
        )

    done = {}

    def sums(steps):
        for chunk, color, k in steps:
            last = 2 * len(plans[chunk][color])
            at = done.get((chunk, color), 0)
            while at <= min(k, last):
                sum_step(chunk, color, at)
                at += 1
                if at > last:
                    full_copy(chunk, color).start()
            done[chunk, color] = at

    def sums_rest():
        while True:
            left = [
                (chunk, color, done.get((chunk, color), 0))
                for chunk in range(len(CHUNKS))
                for color in range(2)
                if done.get((chunk, color), 0) <= 2 * len(plans[chunk][color])
            ]
            if not left:
                return
            sums(left)

    def sum_drain(chunk):
        for color in range(2):
            for k, stage in enumerate(plans[chunk][color]):
                for d in range(1, stage[2]):
                    if stage[3]:
                        scatter_copy(chunk, color, k, d).wait_send()
                        gather_copy(chunk, color, k, d).wait_send()

    def small_copy(b):
        axis, low = partners[b]
        return pltpu.make_async_remote_copy(
            src_ref=small_s,
            dst_ref=small_r.at[b],
            send_sem=small_send.at[b],
            recv_sem=small_recv.at[b],
            device_id=peer_of(axis, low, 2, 1)[1],
            device_id_type=MESH,
        )

    def small_step(b):
        if 1 <= b <= len(partners):
            small_copy(b - 1).wait()
            small_s[...] += small_r[b - 1]
        if b < len(partners):
            small_copy(b).start()

    def keep(base, value):
        low = value.astype(BF)
        rows = pl.ds(base, value.shape[0])
        grads[0, rows, :] = low[:, :LANES]
        grads[1, rows, :] = low[:, LANES:]

    def info_copy(slot, to):
        return send(info_own, info_in.at[slot], info_send.at[slot], info_recv.at[slot], to)

    def halo_copy(which, to):
        src, dst = ((k_s, hk_s), (v_s, hv_s))[which]
        tail = pl.ds(T - HALO, HALO)
        return send(
            src.at[:, tail, :], dst.at[:, tail, :], halo_send.at[which], halo_recv.at[which], to
        )

    for slot, step in enumerate((1, 2, -1)):
        inside = (sq + step >= 0) & (sq + step < n)
        came = (sq - step >= 0) & (sq - step < n)

        @pl.when(inside)
        def _():
            info_copy(slot, sq + step).start()

        @pl.when(jnp.logical_not(came))
        def _():
            info_in[slot, 0] = jnp.full((8, T), -1.0, F32)
            info_in[slot, 1] = jnp.zeros((8, T), F32)

    def half(which, c):
        return pl.ds(which * HU + c, 1)

    def chain_copy(way, stage, c):
        step = 1 - 2 * way
        here = pl.ds(c, 1)
        src, dst, to = (
            (pay_s.at[way, half(1 - par, c)], m1_r.at[way, here], partner),
            (pass_s.at[way, here], carry_r.at[way, here], sq + 2 * step),
            (give_s.at[way, here], in_s.at[way, half(par, c)], partner),
        )[stage]
        return send(src, dst, chain_send.at[way, stage, c], chain_recv.at[way, stage, c], to)

    def chain_arrival(way, stage, c):
        here = pl.ds(c, 1)
        dst = (m1_r.at[way, here], carry_r.at[way, here], in_s.at[way, half(1 - par, c)])[stage]
        return send(dst, dst, chain_send.at[way, stage, c], chain_recv.at[way, stage, c], partner)

    def has_next(way):
        return (z + 1 < nz) if way == 0 else (z > 0)

    def has_before(way):
        return (z > 0) if way == 0 else (z + 1 < nz)

    def marks(r):
        own = info_own[0, r : r + 1, :]
        before, before_two, after = (info_in[s, 0, r : r + 1, :] for s in range(3))
        first = par == 0
        last_a = jnp.where(first, own, before)
        last_b = jnp.where(first, after, own)
        last_z = jnp.where(first, before, before_two)
        inner = (last_a == last_b).astype(F32)
        enter = (last_z == last_a).astype(F32)
        through = (last_z == last_b).astype(F32)
        return inner, enter, through

    def chain_begin(way):
        for c in range(HU):
            chain_copy(way, 0, c).start()

        @pl.when(jnp.logical_not(has_before(way)))
        def _():
            carry_r[way] = jnp.zeros((HU, PAY, T), BF)

    def chain_pair(way):
        second = par == (1 - way)
        for c in range(HU):
            chain_arrival(way, 0, c).wait_recv()
            inner, enter, _through = marks(c // 2)
            weight = inner if way == 0 else enter
            one = jnp.ones_like(weight)
            mine = jnp.where(second, one, weight)
            other = jnp.where(second, weight, one)
            own = pay_s[way, par * HU + c].astype(F32)
            got = m1_r[way, c].astype(F32)
            sum_s[c] = mine * own + other * got

    def chain_pass(way):
        second = par == (1 - way)
        for c in range(HU):

            @pl.when(has_before(way))
            def _():
                chain_arrival(way, 1, c).wait_recv()

            inner, enter, through = marks(c // 2)
            weight = enter if way == 0 else inner
            carry = carry_r[way, c].astype(F32)
            pass_s[way, c] = (sum_s[c] + through * carry).astype(BF)

            @pl.when(has_next(way))
            def _():
                chain_copy(way, 1, c).start()

            own = pay_s[way, par * HU + c].astype(F32)
            got = m1_r[way, c].astype(F32)
            later = jnp.where(second, got, own) + weight * carry
            in_s[way, par * HU + c] = jnp.where(second, later, carry).astype(BF)
            give_s[way, c] = jnp.where(second, carry, later).astype(BF)
            chain_copy(way, 2, c).start()

    def chain_finish(way):
        for c in range(HU):
            chain_arrival(way, 2, c).wait_recv()

    def chain_drain(way):
        for c in range(HU):
            chain_copy(way, 0, c).wait_send()

            @pl.when(has_next(way))
            def _():
                chain_copy(way, 1, c).wait_send()

            chain_copy(way, 2, c).wait_send()

    chain_begin(0)
    lax.fori_loop(0, HU, local_part(par), 0, unroll=3)

    @pl.when(sq + 1 < n)
    def _():
        for which in range(2):
            halo_copy(which, sq + 1).start()

    for r in range(R):
        same = use_mask[r] == seg[r : r + 1, :].astype(F32)
        pad_j = pad[r : r + 1, :]
        open_key = same & (((j_pos < i_pos) & (pad_j == 1)) | (i_pos == j_pos))
        far_mask[r] = open_key.astype(F32)
        near_mask[r] = (open_key & (i_pos - j_pos <= BAND)).astype(F32)
    project(6, w_query, q_s)
    loads[7].wait()
    loads[8].wait()
    for a in range(2):
        for hp in range(PAIRS):
            sides = [
                jnp.broadcast_to(blend[a : a + 1, 2 * hp + side : 2 * hp + side + 1], (1, T))
                for side in range(2)
            ]
            weight_s[a * PAIRS + hp : a * PAIRS + hp + 1, :] = jnp.where(lane_low(1), *sides)
    ones_pair = two_blocks(jnp.ones((T, T), BF))

    def far_local(u, _):
        r = unit_row(u)
        queries = q_s[u].astype(F32)
        values = two_blocks(v_s[u])
        mask = far_mask[r]
        mask = jnp.concatenate([mask, mask], 1)
        for a, (feature, _slope) in enumerate(FEATURES):
            fq = feature(queries).astype(BF)
            fq_s[a, u] = fq
            kernel = (nt(fq, two_blocks(fk_s[a, u])) * mask).astype(BF)
            kk_s[a, u] = kernel
            far_s[a, u] = nn(kernel, values)
            den_s[a, u] = nn(kernel, ones_pair)
        return 0

    lax.fori_loop(0, U, far_local, 0, unroll=4)

    for slot, step in enumerate((1, 2, -1)):
        came = (sq - step >= 0) & (sq - step < n)

        @pl.when(came)
        def _():
            info_copy(slot, sq).wait_recv()

    @pl.when(sq > 0)
    def _():
        for which in range(2):
            halo_copy(which, sq).wait_recv()

    i_low = lax.broadcasted_iota(jnp.int32, (HALO, T), 0)
    j_low = lax.broadcasted_iota(jnp.int32, (HALO, T), 1)
    for r in range(R):
        seg_i = use_mask[r]
        marks_before = info_in[0, 1, r : r + 1, :]
        reach = j_low >= T - BAND + i_low
        halo_mask[r] = (reach & (seg_i[:HALO] + 1.0 == marks_before)).astype(F32)
        use_mask[r] = (seg_i == info_in[0, 0, r : r + 1, :]).astype(F32)

    chain_pair(0)

    def near_local(u, _):
        r = unit_row(u)
        queries = q_s[u]
        scores = nt(queries, two_blocks(k_s[u])) * SCALE
        scores_halo = nt(queries[:HALO], two_blocks(hk_s[u])) * SCALE
        open_near = near_mask[r] > 0
        open_halo = halo_mask[r] > 0
        for side in range(2):
            lanes = slice(side * T, (side + 1) * T)
            s = jnp.where(open_near, scores[:, lanes], NEGATIVE)
            sh = jnp.where(open_halo, scores_halo[:, lanes], NEGATIVE)
            peak = jnp.max(s, -1, keepdims=True)
            peak_halo = jnp.maximum(peak[:HALO], jnp.max(sh, -1, keepdims=True))
            peak = jnp.concatenate([peak_halo, peak[HALO:]], 0)
            e = jnp.exp(s - peak)
            eh = jnp.exp(sh - peak_halo)
            norm = jnp.sum(e, -1, keepdims=True)
            norm_halo = norm[:HALO] + jnp.sum(eh, -1, keepdims=True)
            inverse = 1.0 / jnp.concatenate([norm_halo, norm[HALO:]], 0)
            p_s[u, :, lanes] = e * inverse
            ph_s[u, :, lanes] = eh * inverse[:HALO]
        near_s[u] = nn(p_s[u].astype(BF), two_blocks(v_s[u]))
        near_s[u, :HALO, :] += nn(ph_s[u].astype(BF), two_blocks(hv_s[u]))
        return 0

    entry = z * PARTS // nz
    for part in range(PARTS):

        @pl.when(entry == part)
        def _():
            chain_pass(0)

        lax.fori_loop(part * U // PARTS, (part + 1) * U // PARTS, near_local, 0, unroll=3)
    chain_finish(0)

    def blend_lanes(a, u):
        return weight_s[pl.ds(a * PAIRS + unit_pair(u), 1), :]

    def far_finish(u, _):
        r = unit_row(u)
        hp = unit_pair(u)
        use = use_mask[r]
        blended = near_s[u]
        for a in range(2):
            fq = fq_s[a, u]
            state = two_blocks(in_s[0, u, a * E : (a + 1) * E, :])
            norm = in_s[0, u, 2 * E + 8 * a : 2 * E + 8 * a + 1, :].astype(F32)
            numer = far_s[a, u] + use * nn(fq, state)
            weighted = (fq.astype(F32) * norm).astype(BF)
            denom = den_s[a, u] + use * nn(weighted, ones_block)
            far = numer / denom
            far_s[a, u] = far
            den_s[a, u] = denom
            blended = blended + blend_lanes(a, u) * far
        rows = pl.ds(pl.multiple_of(r * T, T), T)
        lanes = pl.ds(pl.multiple_of(hp * T, T), T)
        mixed[rows, lanes] = blended.astype(BF)
        return 0

    lax.fori_loop(0, U, far_finish, 0, unroll=4)

    loads[9].wait()
    middle[...] = tok[...].astype(F32) + nn(mixed[...], w_out[...])
    for r in range(R):
        rows = pl.ds(r * T, T)
        mid = middle[rows, :]
        inverse = lax.rsqrt(jnp.mean(mid * mid, -1, keepdims=True) + EPSILON)
        normed_two[rows, :] = (mid * inverse * gain_two[...]).astype(BF)
    total[...] = jnp.zeros_like(total)
    back_two[...] = jnp.zeros_like(back_two)
    for i in (10, 11, 12):
        loads[i].wait()

    def feed(t, _):
        at = pl.multiple_of(t * D, D)
        cols = pl.ds(at, D)
        up = nn(normed_two[...], w_up[:, cols])
        square = up * up
        tangent = jnp.tanh(GELU_A * (up + GELU_B * square * up))
        act = (0.5 * up * (1.0 + tangent)).astype(BF)
        slope = 0.5 * (1.0 + tangent) + 0.5 * up * (1.0 - tangent * tangent) * GELU_A * (
            1.0 + 3.0 * GELU_B * square
        )
        total[...] += nn(act, w_down[cols, :])
        keep(pl.multiple_of(row_down(t), D), tn(act, cot[...]))
        d_up = (nt(cot[...], w_down[cols, :]) * slope).astype(BF)
        keep(pl.multiple_of(row_up(t), D), tn(normed_two[...], d_up))
        back_two[...] += nt(d_up, w_up[:, cols])
        return 0

    lax.fori_loop(0, TILES // 2, feed, 0, unroll=2)
    sums(ORDER["down"])
    lax.fori_loop(TILES // 2, TILES, feed, 0, unroll=2)
    sums(ORDER["up"])
    out[...] = (middle[...] + total[...]).astype(BF)

    gain_grad_two = jnp.zeros((1, D), F32)
    for r in range(R):
        rows = pl.ds(r * T, T)
        mid = middle[rows, :]
        inverse = lax.rsqrt(jnp.mean(mid * mid, -1, keepdims=True) + EPSILON)
        d_n = back_two[rows, :]
        gain_grad_two += jnp.sum(d_n * mid * inverse, 0, keepdims=True)
        scaled = d_n * gain_two[...]
        d_mid = (
            cot[rows, :].astype(F32)
            + inverse * scaled
            - mid * (inverse * inverse * inverse) * jnp.mean(mid * scaled, -1, keepdims=True)
        )
        total[rows, :] = d_mid
        normed_two[rows, :] = d_mid.astype(BF)
    d_branch = normed_two[...]
    keep(ROW_OUT, tn(mixed[...], d_branch))
    d_blended = nt(d_branch, w_out[...]).astype(BF)
    for r in range(R):
        for hp in range(PAIRS):
            db_s[unit_of(r, hp)] = d_blended[r * T : (r + 1) * T, hp * T : (hp + 1) * T]
    sums(ORDER["branch"])

    gb_s[...] = jnp.zeros_like(gb_s)

    def far_prepare(u, _):
        r = unit_row(u)
        hp = unit_pair(u)
        use = use_mask[r]
        use_low = use.astype(BF)
        d_out = db_s[u].astype(F32)
        norms = []
        for a in range(2):
            far = far_s[a, u]
            inverse = 1.0 / den_s[a, u]
            product = d_out * far
            row = a * PAIRS + hp
            gb_s[pl.ds(row, 1), :] += jnp.sum(product, 0, keepdims=True)
            weight = blend_lanes(a, u)
            product = product * weight
            high = product.astype(BF)
            rest = (product - high.astype(F32)).astype(BF)
            dden = -(nn(high, ones_block) + nn(rest, ones_block)) * inverse
            dden_s[a, u] = dden
            dnum = (weight * d_out * inverse).astype(BF)
            low_s[a, u] = dnum
            used = fq_s[a, u] * use_low
            pay_s[1, u, a * E : (a + 1) * E, :] = pick(tn(used, dnum)).astype(BF)
            norm = jnp.sum(used.astype(F32) * dden, 0, keepdims=True)
            norms.append(jnp.broadcast_to(norm, (8, T)))
        pay_s[1, u, 2 * E : PAY, :] = jnp.concatenate(norms, 0).astype(BF)
        return 0

    def prepare_part(which):
        return lambda i, _: far_prepare(which * HU + i, 0)

    lax.fori_loop(0, HU, prepare_part(1 - par), 0, unroll=3)
    chain_begin(1)
    lax.fori_loop(0, HU, prepare_part(par), 0, unroll=3)

    def near_back(u, _):
        keys = two_blocks(k_s[u])
        halo_keys = two_blocks(hk_s[u])
        queries = q_s[u]
        d_out = db_s[u]
        dp = nt(d_out, two_blocks(v_s[u]))
        dp_halo = nt(d_out[:HALO], two_blocks(hv_s[u]))
        p = p_s[u]
        p_halo = ph_s[u]
        ds = []
        ds_halo = []
        for side in range(2):
            lanes = slice(side * T, (side + 1) * T)
            ps, phs = p[:, lanes], p_halo[:, lanes]
            delta = jnp.sum(ps * dp[:, lanes], -1, keepdims=True)
            delta_halo = delta[:HALO] + jnp.sum(phs * dp_halo[:, lanes], -1, keepdims=True)
            delta = jnp.concatenate([delta_halo, delta[HALO:]], 0)
            ds.append(ps * (dp[:, lanes] - delta))
            ds_halo.append(phs * (dp_halo[:, lanes] - delta_halo))
        ds = jnp.concatenate(ds, 1).astype(BF)
        ds_halo = jnp.concatenate(ds_halo, 1).astype(BF)
        near_s[u] = nn(ds, keys) * SCALE
        near_s[u, :HALO, :] += nn(ds_halo, halo_keys) * SCALE
        dk_s[u] = pick(tn(ds, queries)) * SCALE
        dv_s[u] = pick(tn(p.astype(BF), d_out))
        hdk_s[u] = (pick(tn(ds_halo, queries[:HALO])) * SCALE)[T - HALO :].astype(BF)
        hdv_s[u] = pick(tn(p_halo.astype(BF), d_out[:HALO]))[T - HALO :].astype(BF)
        return 0

    sums(ORDER["prepare"])
    lax.fori_loop(0, HU, near_back, 0, unroll=3)
    sums(ORDER["near_a"])
    lax.fori_loop(HU, U, near_back, 0, unroll=3)
    sums(ORDER["near_b"])

    def halo_back(which, to):
        src, dst = ((hdk_s, hdk_r), (hdv_s, hdv_r))[which]
        return send(src, dst, halo_send.at[2 + which], halo_recv.at[2 + which], to)

    @pl.when(sq > 0)
    def _():
        for which in range(2):
            halo_back(which, sq - 1).start()

    chain_pair(1)
    sums(ORDER["pair"])

    def far_back(u, _):
        r = unit_row(u)
        values = two_blocks(v_s[u])
        mask = far_mask[r]
        mask = jnp.concatenate([mask, mask], 1)
        use = use_mask[r]
        queries = q_s[u].astype(F32)
        keys = k_s[u].astype(F32)
        dq = near_s[u]
        dk = dk_s[u]
        dv = dv_s[u]
        for a, (_feature, slope) in enumerate(FEATURES):
            dnum = low_s[a, u]
            dden = dden_s[a, u]
            fq = fq_s[a, u]
            fk = two_blocks(fk_s[a, u])
            added = jnp.concatenate(
                [
                    jnp.broadcast_to(dden[:, 0:1], (T, T)),
                    jnp.broadcast_to(dden[:, E : E + 1], (T, T)),
                ],
                1,
            )
            d_kernel = ((nt(dnum, values) + added) * mask).astype(BF)
            dv += pick(tn(kk_s[a, u], dnum))
            state = two_blocks(in_s[0, u, a * E : (a + 1) * E, :])
            norm = in_s[0, u, 2 * E + 8 * a : 2 * E + 8 * a + 1, :].astype(F32)
            dfq = nn(d_kernel, fk) + use * (nt(dnum, state) + dden * norm)
            dq += dfq * slope(queries)
            dk += pick(tn(d_kernel, fq)) * slope(keys)
        near_s[u] = dq
        dk_s[u] = dk
        dv_s[u] = dv
        return 0

    turn = (nz - 1 - z) * PARTS // nz
    for part in range(PARTS):

        @pl.when(turn == part)
        def _():
            chain_pass(1)

        lax.fori_loop(part * U // PARTS, (part + 1) * U // PARTS, far_back, 0, unroll=3)
        sums(ORDER["far_%d" % part])

    for u in range(U):
        r, hp = (u % (2 * R)) // 2, (u // (2 * R)) * 2 + u % 2
        wide_s[0, r * T : (r + 1) * T, hp * T : (hp + 1) * T] = near_s[u].astype(BF)
    keep(ROW_Q, tn(normed[...], wide_s[0]))
    sums(ORDER["query"])
    back_two[...] = nt(wide_s[0], w_query[...])

    @pl.when(sq + 1 < n)
    def _():
        for which in range(2):
            halo_back(which, sq).wait_recv()

    chain_finish(1)
    sums(ORDER["state"])

    def far_close(u, _):
        r = unit_row(u)
        hp = unit_pair(u)
        tail = tail_mask[r]
        keys = k_s[u].astype(F32)
        values = v_s[u]
        dk = dk_s[u]
        dv = dv_s[u]
        for a, (_feature, slope) in enumerate(FEATURES):
            state = two_blocks(in_s[1, u, a * E : (a + 1) * E, :])
            norm = in_s[1, u, 2 * E + 8 * a : 2 * E + 8 * a + 1, :].astype(F32)
            dk += tail * (nt(values, state) + norm) * slope(keys)
            dv += tail * nn(fk_s[a, u], state)
        zero = jnp.zeros((T - HALO, T), F32)
        dk += jnp.concatenate([zero, hdk_r[u].astype(F32)], 0)
        dv += jnp.concatenate([zero, hdv_r[u].astype(F32)], 0)
        rows = pl.ds(pl.multiple_of(r * T, T), T)
        lanes = pl.ds(pl.multiple_of(hp * T, T), T)
        wide_s[1, rows, lanes] = dk.astype(BF)
        wide_s[2, rows, lanes] = dv.astype(BF)
        return 0

    lax.fori_loop(0, U, far_close, 0, unroll=4)
    sums(ORDER["close"])
    first = 2 - lax.rem(rw, 2)
    keep(pl.multiple_of(ROW_Q + first * D, D), tn(normed[...], wide_s[first]))
    sums(((3, 0, 0), (3, 1, 0)))
    rest = 3 - first
    keep(pl.multiple_of(ROW_Q + rest * D, D), tn(normed[...], wide_s[rest]))
    sums(ORDER["key"][:8])
    for i, weight in ((1, w_key), (2, w_value)):
        back_two[...] += nt(wide_s[i], weight[...])
    gain_grad_one = jnp.zeros((1, D), F32)
    for r in range(R):
        rows = pl.ds(r * T, T)
        x = tok[rows, :].astype(F32)
        inverse = lax.rsqrt(jnp.mean(x * x, -1, keepdims=True) + EPSILON)
        d_n = back_two[rows, :]
        gain_grad_one += jnp.sum(d_n * x * inverse, 0, keepdims=True)
        scaled = d_n * gain_one[...]
        d_x = (
            total[rows, :]
            + inverse * scaled
            - x * (inverse * inverse * inverse) * jnp.mean(x * scaled, -1, keepdims=True)
        )
        grad_tok[rows, :] = d_x.astype(BF)
    blends = [
        jnp.concatenate([gb_s[a * PAIRS + hp : a * PAIRS + hp + 1, :] for hp in range(PAIRS)], 1)
        for a in range(2)
    ]
    small_s[...] = jnp.concatenate(
        [gain_grad_one, gain_grad_two] + blends + [jnp.zeros((SMALL - 4, D), F32)], 0
    )
    small_step(0)
    sums(ORDER["key"][8:])
    sums(ORDER["back"])
    for i, step in enumerate(ORDER["tail"]):
        sums((step,))
        if i % 2 and i // 2 < len(partners):
            small_step(i // 2 + 1)
    for b in range(len(ORDER["tail"]) // 2, len(partners)):
        small_step(b + 1)
    sums_rest()
    small_out[...] = small_s[...]

    for slot, step in enumerate((1, 2, -1)):

        @pl.when((sq + step >= 0) & (sq + step < n))
        def _():
            info_copy(slot, sq + step).wait_send()

    @pl.when(sq + 1 < n)
    def _():
        for which in range(2):
            halo_copy(which, sq + 1).wait_send()

    @pl.when(sq > 0)
    def _():
        for which in range(2):
            halo_back(which, sq - 1).wait_send()

    chain_drain(0)
    chain_drain(1)
    for c in range(len(CHUNKS)):
        sum_drain(c)
        for color in range(2):
            full_copy(c, color).wait()


def widen_kernel(
    grads,
    small_in,
    out_in,
    back_in,
    g_one,
    g_two,
    g_blend,
    g_query,
    g_key,
    g_value,
    g_out,
    g_up,
    g_down,
    out,
    back,
    small,
    gains,
    blends,
    token,
    held,
    wide,
    small_sem,
    token_sem,
    in_sem,
    out_sem,
):
    blocks = ROWS_ALL // D
    targets = []
    for t in (0, 2):
        targets += [g_down.at[pl.ds((t + i) * D, D)] for i in range(2)]
        targets += [g_up.at[:, pl.ds((t + i) * D, D)] for i in range(2)]
    targets += [g_out, g_query, g_key, g_value]
    small_read = pltpu.make_async_copy(small_in, small, small_sem.at[0])
    reads = [
        pltpu.make_async_copy(grads.at[:, pl.ds(i * D, D)], held.at[i], in_sem.at[i])
        for i in range(blocks)
    ]
    token_reads = [
        pltpu.make_async_copy(src, token.at[i], token_sem.at[i])
        for i, src in enumerate((out_in, back_in))
    ]
    for read in [small_read] + reads + token_reads:
        read.start()
    writes = [
        pltpu.make_async_copy(wide.at[i], targets[i], out_sem.at[i]) for i in range(blocks)
    ]
    small_writes = [
        pltpu.make_async_copy(src, dst, small_sem.at[i + 1])
        for i, (src, dst) in enumerate(
            ((gains.at[0], g_one), (gains.at[1], g_two), (blends, g_blend))
        )
    ]
    token_writes = [
        pltpu.make_async_copy(token.at[i], dst, token_sem.at[i + 2])
        for i, dst in enumerate((out, back))
    ]
    for i in range(blocks):
        reads[i].wait()
        wide[i, :, :LANES] = held[i, 0].astype(F32)
        wide[i, :, LANES:] = held[i, 1].astype(F32)
        writes[i].start()
    for read, write in zip(token_reads, token_writes):
        read.wait()
        write.start()
    small_read.wait()
    gains[...] = small[:2, :]
    lane = lax.broadcasted_iota(jnp.int32, (H, D), 1) // E
    head = lax.broadcasted_iota(jnp.int32, (H, D), 0)
    for a in range(2):
        row = small[2 + a : 3 + a, :]
        per_head = jnp.sum(jnp.where(lane == head, row, 0.0), -1, keepdims=True)
        blends[a : a + 1, :] = jnp.broadcast_to(per_head, (H, H)).T[:1]
    for write in small_writes:
        write.start()
    for write in small_writes + writes + token_writes:
        write.wait()


def solution(mesh):
    n = mesh.shape["seq"]
    n_rows = mesh.shape["rows"]

    def shards(
        tokens,
        segment_ids,
        padding,
        gain_one,
        w_query,
        w_key,
        w_value,
        blend,
        w_out,
        gain_two,
        w_up,
        w_down,
        cotangent,
    ):
        R, tok_count, _ = tokens.shape
        M = R * tok_count
        U = R * PAIRS
        HU = U // 2
        vmem = pl.BlockSpec(memory_space=pltpu.VMEM)
        anyspace = pl.BlockSpec(memory_space=pl.ANY)
        V = pltpu.VMEM
        unit_f = V((U, T, T), F32)
        unit_b = V((U, T, T), BF)
        two_f = V((2, U, T, T), F32)
        two_b = V((2, U, T, T), BF)
        wide_f = V((M, D), F32)
        wide_b = V((M, D), BF)
        halo_b = V((U, HALO, T), BF)
        dma = pltpu.SemaphoreType.DMA
        plans, landed_rows = sum_plans(n_rows, n)
        stages = 2 * max(len(plan) for both in plans for plan in both)
        count = bits(n) + bits(n_rows)
        scratch = [
            V((2, ROWS_ALL, LANES), BF),
            V((2, ROWS_ALL, LANES), BF),
            V((2, landed_rows, LANES), BF),
            V((SMALL, D), F32),
            V((count, SMALL, D), F32),
            wide_b,
            V((R, T), jnp.int32),
            V((R, T), jnp.int32),
            V((1, D), F32),
            V((1, D), F32),
            V((2, H), F32),
            V((D, D), BF),
            V((D, D), BF),
            V((D, D), BF),
            V((D, D), BF),
            V((D, FF), BF),
            V((FF, D), BF),
            wide_b,
            V((2 * PAIRS, T), F32),
            wide_b,
            wide_b,
            wide_b,
            wide_f,
            wide_f,
            wide_f,
            unit_b,
            unit_b,
            unit_b,
            unit_b,
            unit_b,
            two_b,
            two_b,
            V((2, U, T, 2 * T), BF),
            V((U, T, 2 * T), F32),
            V((U, HALO, 2 * T), F32),
            unit_f,
            two_f,
            two_f,
            unit_b,
            two_b,
            two_f,
            unit_f,
            unit_f,
            halo_b,
            halo_b,
            halo_b,
            halo_b,
            V((3, M, D), BF),
            V((R, T, T), F32),
            V((R, T, T), F32),
            V((R, T, T), F32),
            V((R, T, T), F32),
            V((R, HALO, T), F32),
            V((2, 8, T), F32),
            V((3, 2, 8, T), F32),
            V((2 * PAIRS, T), F32),
            V((2, U, PAY, T), BF),
            V((2, HU, PAY, T), BF),
            V((HU, PAY, T), F32),
            V((2, HU, PAY, T), BF),
            V((2, HU, PAY, T), BF),
            V((2, U, PAY, T), BF),
            V((2, HU, PAY, T), BF),
            dma((13,)),
            dma((3,)),
            dma((3,)),
            dma((4,)),
            dma((4,)),
            dma((2, 3, HU)),
            dma((2, 3, HU)),
            dma((len(CHUNKS), 2, stages, 3)),
            dma((len(CHUNKS), 2, stages, 3)),
            dma((count,)),
            dma((count,)),
            dma((len(CHUNKS), 2)),
        ]
        out, grad_tok, small, grads = pl.pallas_call(
            functools.partial(layer_kernel, n, n_rows, R),
            out_shape=(
                jax.ShapeDtypeStruct((M, D), BF),
                jax.ShapeDtypeStruct((M, D), BF),
                jax.ShapeDtypeStruct((SMALL, D), F32),
                jax.ShapeDtypeStruct((2, ROWS_ALL, LANES), BF),
            ),
            in_specs=[pl.BlockSpec(memory_space=pltpu.HBM)] * 13,
            out_specs=(vmem, vmem, vmem, anyspace),
            scratch_shapes=scratch,
            compiler_params=pltpu.CompilerParams(
                collective_id=0, has_side_effects=True, vmem_limit_bytes=LAYER_VMEM
            ),
            name="layer",
        )(
            tokens.reshape(M, D),
            segment_ids,
            padding,
            gain_one.reshape(1, D),
            gain_two.reshape(1, D),
            blend,
            w_query,
            w_key,
            w_value,
            w_out,
            w_up,
            w_down,
            cotangent.reshape(M, D),
        )
        square = jax.ShapeDtypeStruct((D, D), F32)
        token = jax.ShapeDtypeStruct((M, D), BF)
        blocks = ROWS_ALL // D
        g_one, g_two, g_blend, g_query, g_key, g_value, g_out, g_up, g_down, out, grad_tok = (
          pl.pallas_call(
            widen_kernel,
            out_shape=(
                jax.ShapeDtypeStruct((D,), F32),
                jax.ShapeDtypeStruct((D,), F32),
                jax.ShapeDtypeStruct((2, H), F32),
                square,
                square,
                square,
                square,
                jax.ShapeDtypeStruct((D, FF), F32),
                jax.ShapeDtypeStruct((FF, D), F32),
                token,
                token,
            ),
            in_specs=[anyspace] * 4,
            out_specs=(anyspace,) * 11,
            scratch_shapes=[
                V((SMALL, D), F32),
                V((2, D), F32),
                V((2, H), F32),
                V((2, M, D), BF),
                V((blocks, 2, D, LANES), BF),
                V((blocks, D, D), F32),
                dma((4,)),
                dma((4,)),
                dma((blocks,)),
                dma((blocks,)),
            ],
            compiler_params=pltpu.CompilerParams(vmem_limit_bytes=WIDEN_VMEM),
            name="widen",
        )(grads, small, out, grad_tok))
        return (
            out.reshape(R, tok_count, D),
            grad_tok.reshape(R, tok_count, D),
            g_one,
            g_query,
            g_key,
            g_value,
            g_blend,
            g_out,
            g_two,
            g_up,
            g_down,
        )

    row, whole = P("rows", "seq", None), P()
    return jax.shard_map(
        shards,
        mesh=mesh,
        in_specs=(row, P("rows", "seq"), P("rows", "seq")) + (whole,) * 9 + (row,),
        out_specs=(row, row) + (whole,) * 9,
        check_vma=False,
    )
```
